32 devices in a mesh: dp: 16 (over z, y, x), ctx: 2 (over core).
Axes of the slice: x: 2, y: 2, z: 4, core: 2. Of those that a mesh axis runs over, the one named last changes fastest.
Arguments:
- layer_in: bfloat16 [16, 256, 4096], P('dp', 'ctx'), may hold values from -6 to 6
- inner_act: bfloat16 [16, 256, 2176], P('dp', 'ctx'), may hold values from -6 to 6
- readout: bfloat16 [16, 256, 64], P('dp', 'ctx'), may hold values from -0.75 to 0.75
- w_in: bfloat16 [4096, 132], P('dp'), may hold values from -0.09375 to 0.09375
- a_log: float32 [68], replicated, may hold values from -3.9 to -1.6
- dt_bias: float32 [68], replicated, may hold values from -4 to -1
- d_skip: float32 [68], replicated, may hold values from 0.5 to 1.5
- grad_out: bfloat16 [16, 256, 2176], P('dp', 'ctx'), may hold values from -6 to 6
Outputs:
- grad_x: bfloat16 [16, 256, 2176], P('dp', 'ctx')
- grad_c: bfloat16 [16, 256, 64], P('dp', 'ctx')
- grad_proj: bfloat16 [16, 256, 132], P('dp', 'ctx')
- grad_w: float32 [4096, 132], P('dp', 'ctx')
The draws below stay inside these ranges and needn't reach their ends.
All inputs are finite; a program needn't handle non-finite values.
Results may differ from the reference program's by a relative error of at most 0.015.
Values may be sent and summed in bfloat16 or wider, within the bound.
A program may use at most 64 MiB of HBM per device.

```python
import jax
import jax.numpy as jnp
from jax import lax

D = 4096
HEADS = 68
HEADDIM = 32
STATE = 64
BLOCK = 128
SEQS = 16
LEN = 256
COLS = 132


def raised(values, stream_key, source, target, parts, factor):
    def block_of(dim):
        return (jnp.arange(values.shape[dim]) // (values.shape[dim] // parts)).reshape((-1,) + (1,) * (values.ndim - 1 - dim))

    first = jax.random.permutation(stream_key, parts)[block_of(target)]
    other_side = (block_of(target) + parts // 2) % parts
    return jnp.where((block_of(source) == first) | (block_of(source) == other_side), factor * values, values)


def block_levels(own_key, shape, shards, smallest, largest):
    level, own = 1.0, jax.random.fold_in(own_key, 6)
    for dim, blocks in shards:
        heights = jnp.exp(jax.random.uniform(jax.random.fold_in(own, dim), (blocks,), jnp.float32, smallest / len(shards), largest / len(shards)))
        level = level * jnp.repeat(heights, shape[dim] // blocks).reshape([-1 if axis == dim else 1 for axis in range(len(shape))])
    return level


def normal_values(stream_key, shape, scale, limit, shards=(), held_as=jnp.bfloat16):
    values = jax.random.normal(stream_key, shape, jnp.float32) * scale
    if len(shards) > 0:
        values = block_levels(stream_key, shape, shards, -0.22, 0.18) * values
    return jnp.clip(values, min=-limit, max=limit).astype(held_as)


def noise_with(key, shape, scale, limit, shards, heavy, dtype=jnp.bfloat16):
    array = scale * jax.random.normal(key, shape, jnp.float32)
    if shards:
        array = array * block_levels(key, shape, shards, -0.22, 0.18)
    return jnp.clip(raised(array, jax.random.fold_in(key, 3), *heavy), -limit, limit).astype(dtype)


def setup_inputs(seed: int = 0) -> dict:
    key_list = jax.random.split(jax.random.key(seed), 9)
    return {
        "layer_in": noise_with(key_list[0], (SEQS, LEN, D), 1.0, 6.0, ((0, 16), (1, 2)), (0, 2, 16, 2.0)),
        "inner_act": normal_values(key_list[1], (SEQS, LEN, HEADS * HEADDIM), 1.0, 6.0, ((0, 16), (1, 2))),
        "readout": normal_values(key_list[2], (SEQS, LEN, STATE), (STATE ** -0.5), 0.75, ((0, 16), (1, 2))),
        "w_in": normal_values(key_list[3], (D, COLS), D ** -0.5, 0.09375, ((0, 16),)),
        "a_log": jnp.clip(jax.random.uniform(key_list[4], (HEADS,), jnp.float32, -3.9, -1.6), -3.9, -1.6),
        "dt_bias": jnp.clip(jax.random.uniform(key_list[5], (HEADS,), jnp.float32, -4.0, -1.0), -4.0, -1.0),
        "d_skip": jnp.clip(jax.random.uniform(key_list[6], (HEADS,), jnp.float32, 0.5, 1.5), 0.5, 1.5),
        "grad_out": normal_values(key_list[7], (SEQS, LEN, HEADS * HEADDIM), 1.0, 6.0, ((0, 16), (1, 2))),
    }


def prepare(projected, a_log, dt_bias):
    b_rows = projected[:, :STATE].astype(jnp.bfloat16)
    step_size = jax.nn.softplus(projected[:, STATE:] + dt_bias)
    decay_rate = -jnp.exp(a_log) * step_size
    return (b_rows, step_size, decay_rate)

def blocked(values, width):
    return values.reshape(values.shape[0] // BLOCK, BLOCK, width)

def block_forward(projected, inner_rows, c_rows, a_log, dt_bias, d_skip, entry_state):
    row_count = projected.shape[0]
    head_count = a_log.shape[0]
    head_width = inner_rows.shape[1] // head_count
    block_count = row_count // BLOCK
    b_rows, step_size, decay_rate = prepare(projected, a_log, dt_bias)
    inner_blocks = inner_rows.reshape(block_count, BLOCK, head_count, head_width)
    b_blocks = blocked(b_rows, STATE)
    c_blocks = blocked(c_rows, STATE)
    step_blocks = jnp.swapaxes(blocked(step_size, head_count), 1, 2)
    cum_blocks = jnp.cumsum(jnp.swapaxes(blocked(decay_rate, head_count), 1, 2), axis=2)
    position = jnp.arange(BLOCK)
    causal = position[:, None] >= position[None, :]

    def advance(carried, pieces):
        inner_c, b_c, c_c, step_c, cum_c = pieces
        scores = jnp.dot(c_c, b_c.T, preferred_element_type=jnp.float32)
        spread = cum_c[:, :, None] - cum_c[:, None, :]
        factor = jnp.where(causal, jnp.exp(jnp.where(causal, spread, 0.0)), 0.0)
        mixing = (scores[None] * factor * step_c[:, None, :]).astype(jnp.bfloat16)
        within = jnp.einsum('hts,shp->thp', mixing.astype(jnp.float32), inner_c.astype(jnp.float32))
        to_end = jnp.exp(cum_c[:, -1:] - cum_c) * step_c
        weighted = (b_c.astype(jnp.float32)[None] * to_end[:, :, None]).astype(jnp.bfloat16)
        added = jnp.einsum('shp,hsn->hpn', inner_c.astype(jnp.float32), weighted.astype(jnp.float32))
        carried_in = jnp.einsum('tn,hpn->thp', c_c.astype(jnp.float32), carried, precision=lax.Precision.HIGHEST)
        carried_in = carried_in * jnp.exp(cum_c).T[:, :, None]
        result = (within + carried_in + d_skip[None, :, None] * inner_c.astype(jnp.float32)).astype(jnp.bfloat16)
        carried = jnp.exp(cum_c[:, -1])[:, None, None] * carried + added
        return (carried, result)
    final_state, outputs = lax.scan(advance, entry_state, (inner_blocks, b_blocks, c_blocks, step_blocks, cum_blocks))
    return (outputs.reshape(row_count, head_count * head_width), final_state)

def reference(layer_in, inner_act, readout, w_in, a_log, dt_bias, d_skip, grad_out):
    zero_state = jnp.zeros((HEADS, HEADDIM, STATE), jnp.float32)

    def per_sequence(grad_sum, pieces):
        tokens, inner_rows, c_rows, grad_rows = pieces
        projected = jnp.dot(tokens, w_in, preferred_element_type=jnp.float32)

        def forward_only(proj_val, inner_val, c_val):
            layer_out, final_state = block_forward(proj_val, inner_val, c_val, a_log, dt_bias, d_skip, zero_state)
            return layer_out
        primal, pullback = jax.vjp(forward_only, projected, inner_rows, c_rows)
        grad_p, grad_v, grad_r = pullback(grad_rows)
        proj_grad = grad_p.astype(jnp.bfloat16)
        term = lax.dot_general(tokens, proj_grad, (((0,), (0,)), ((), ())), preferred_element_type=jnp.float32)
        return (grad_sum + term, (grad_v, grad_r, proj_grad))
    start_sum = jnp.zeros((D, STATE + HEADS), jnp.float32)
    grad_sum, (grad_x, grad_c, grad_proj) = lax.scan(per_sequence, start_sum, (layer_in, inner_act, readout, grad_out))
    return (grad_x, grad_c, grad_proj, grad_sum / SEQS)
```

```python
import functools

import jax
import jax.numpy as jnp
from jax import lax
from jax.experimental import pallas as pl
from jax.experimental.pallas import tpu as pltpu
from jax.sharding import PartitionSpec as P

STATE = 64
LANES = 128
MESH = pl.DeviceIdType.MESH
VMEM_MAIN = 62 * 1024 * 1024
VMEM_STORE = 4 * 1024 * 1024
F32 = jnp.float32
BF16 = jnp.bfloat16


def inner_group(n):
    b = 1
    while b * b < n and n % (2 * b) == 0:
        b *= 2
    return b


def up(n, m):
    return -(-n // m) * m


def dot(a, b):
    return jnp.dot(a, b, preferred_element_type=F32)


def dot_nt(a, b):
    return lax.dot_general(a, b, (((1,), (1,)), ((), ())), preferred_element_type=F32)


def split(v):
    hi = v.astype(BF16)
    return hi, (v - hi.astype(F32)).astype(BF16)


def dot_split(v, b):
    hi, lo = split(v)
    return dot(hi, b) + dot(lo, b)


def dot_exact(sel, v):
    hi, rest = v.astype(BF16), None
    rest = v - hi.astype(F32)
    mid, low = split(rest)
    return dot(sel, hi) + dot(sel, mid) + dot(sel, low)


def iota(shape, dim):
    return lax.broadcasted_iota(jnp.int32, shape, dim)


def kernel(cfg, tok_h, x_h, g_h, c, w, vec, dexp, gx, gc, gp, gw, tok, x, g, wall, trecv, gall, sloc, crecv,
           dall, spread_m, gather_m, xw, gwt, dx, proj, cum_r, dt_r, cumt, rowt, qacc, ds, part, pst, precv,
           decs, decr, wzs, wzr, wfs, wfr, as_, ar, gzs, gzr, gfs, gfr, cs, cr, ps, pr, es, er, ms, mr, ls):
    n_dp, n_ctx, t, rows, heads, width, cols = cfg
    wide = rows % LANES == 0
    halved = wide and rows % (n_ctx * LANES) == 0 and n_ctx == 2
    half = rows // n_ctx
    n_b = inner_group(n_dp)
    n_a = n_dp // n_b
    my_a, my_b = lax.div(lax.axis_index("dp"), n_b), lax.rem(lax.axis_index("dp"), n_b)
    loads = [pltpu.make_async_copy(src, dst, ls.at[i]) for i, (src, dst) in enumerate(((x_h, x), (g_h, g), (tok_h, tok)))]
    for load in loads:
        load.start()
    groups = x.shape[1] // LANES
    gh = LANES // width
    cb = cols // n_ctx
    cbp = up(cb, 8)
    me = lax.axis_index("dp")
    my = lax.axis_index("ctx")

    def peer(k):
        return lax.rem(me + k, n_dp)

    def mate(k):
        return lax.rem(my + k, n_ctx)

    def col(ref, i):
        return ref.at[:, pl.ds(pl.multiple_of(i * rows, LANES), rows)] if wide else ref.at[i]

    def blk(i):
        return pl.ds(pl.multiple_of(i * t, LANES), t)

    def lanes(q):
        return pl.ds(pl.multiple_of(q * LANES, LANES), LANES)

    barrier = pltpu.get_barrier_semaphore()

    def greet(k, carry):
        pl.semaphore_signal(barrier, inc=1, device_id=(peer(k), my), device_id_type=MESH)
        return carry

    def greet_mate(k, carry):
        pl.semaphore_signal(barrier, inc=1, device_id=(me, mate(k)), device_id_type=MESH)
        return carry

    lax.fori_loop(1, n_dp, greet, 0)
    lax.fori_loop(1, n_ctx, greet_mate, 0)
    pl.semaphore_wait(barrier, n_dp + n_ctx - 2)

    def origin(ka, kb):
        return lax.rem(my_a + n_a - ka, n_a) * n_b + lax.rem(my_b + n_b - kb, n_b)

    def w_slot(i):
        if halved:
            return wall.at[my, :, pl.ds(pl.multiple_of(i * half, LANES), half)]
        return col(wall, i)

    def g_slot(i):
        return gall.at[:, blk(i)]

    def far(slot, send, recv, ka):
        return pltpu.make_async_remote_copy(
            src_ref=slot(me), dst_ref=slot(me), send_sem=send.at[ka], recv_sem=recv.at[ka],
            device_id=(lax.rem(my_a + ka, n_a) * n_b + my_b, my), device_id_type=MESH)

    def near(slot, send, recv, ka, kb):
        i = origin(ka, 0)
        return pltpu.make_async_remote_copy(
            src_ref=slot(i), dst_ref=slot(i), send_sem=send.at[ka * n_b + kb], recv_sem=recv.at[ka * n_b + kb],
            device_id=(my_a * n_b + lax.rem(my_b + kb, n_b), my), device_id_type=MESH)

    def across(ka):
        i = lax.rem(my_a + n_a - ka, n_a) * n_b
        block = wall.at[my, :, pl.ds(pl.multiple_of(i * half, LANES), n_b * half)]
        return pltpu.make_async_remote_copy(
            src_ref=block, dst_ref=block, send_sem=ms.at[ka], recv_sem=mr.at[ka],
            device_id=(me, 1 - my), device_id_type=MESH)

    def a_copy(k):
        return pltpu.make_async_remote_copy(
            src_ref=col(tok, peer(k)), dst_ref=trecv.at[blk(me), :], send_sem=as_.at[k],
            recv_sem=ar.at[k], device_id=(peer(k), my), device_id_type=MESH)

    def c_copy(k):
        other = mate(k)
        which = jnp.where(other > my, 0, 1)
        return pltpu.make_async_remote_copy(
            src_ref=sloc.at[which], dst_ref=crecv.at[my], send_sem=cs.at[k], recv_sem=cr.at[k],
            device_id=(me, other), device_id_type=MESH)

    def d_copy(k):
        return pltpu.make_async_remote_copy(
            src_ref=decs, dst_ref=decr.at[my], send_sem=es.at[k], recv_sem=er.at[k],
            device_id=(me, mate(k)), device_id_type=MESH)

    def p_copy(k):
        return pltpu.make_async_remote_copy(
            src_ref=pst.at[mate(k)], dst_ref=precv.at[my], send_sem=ps.at[k], recv_sem=pr.at[k],
            device_id=(me, mate(k)), device_id_type=MESH)

    def each(n, act):
        def step(k, carry):
            act(k)
            return carry

        lax.fori_loop(1, n, step, 0)

    def spread_near(slot, send, recv, ka):
        each(n_b, lambda kb: near(slot, send, recv, ka, kb).start())

    def first(slot, send, recv, fsend, frecv):
        each(n_a, lambda ka: far(slot, send, recv, ka).start())
        spread_near(slot, fsend, frecv, 0)

    def pass_on(slot, send, recv, fsend, frecv):
        def one(ka):
            far(slot, send, recv, ka).wait_recv()
            spread_near(slot, fsend, frecv, ka)

        each(n_a, one)

    def arrive(slot, fsend, frecv, ka):
        each(n_b, lambda kb: near(slot, fsend, frecv, ka, kb).wait_recv())

    def settle(slot, send, recv, fsend, frecv):
        each(n_a, lambda ka: far(slot, send, recv, ka).wait_send())

        def one(ka, carry):
            each(n_b, lambda kb: near(slot, fsend, frecv, ka, kb).wait_send())
            return carry

        lax.fori_loop(0, n_a, one, 0)

    inner = x.shape[1]
    wcols = w.shape[0]
    if halved:
        wall[my, :, pl.ds(pl.multiple_of(me * half, LANES), half)] = w[:, pl.ds(pl.multiple_of(my * half, LANES), half)]
    elif wide:
        wall[:, pl.ds(pl.multiple_of(me * rows, LANES), rows)] = w[...]
    else:
        wall[me] = w[...]
    first(w_slot, wzs, wzr, wfs, wfr)
    loads[0].wait()
    loads[1].wait()
    loads[2].wait()
    pass_on(w_slot, wzs, wzr, wfs, wfr)
    each(n_dp, lambda k: a_copy(k).start())
    if wide:
        trecv[blk(me), :] = tok[:, pl.ds(pl.multiple_of(me * rows, LANES), rows)]
    else:
        trecv[blk(me), :] = tok[me]
    proj[...] = jnp.zeros_like(proj)
    qacc[...] = jnp.zeros_like(qacc)
    ds[...] = jnp.zeros_like(ds)
    rowt[...] = jnp.zeros_like(rowt)
    spread_m[...] = jnp.where(iota((LANES, inner), 0) == iota((LANES, inner), 1) // width, 1.0, 0.0).astype(BF16)
    gather_m[...] = jnp.where(iota((inner, LANES), 1) == iota((inner, LANES), 0) // width, 1.0, 0.0).astype(BF16)
    head = iota((t, LANES), 1) // width

    def outer(q, carry):
        x4 = x[:, lanes(q)]
        zero = jnp.zeros_like(x4)
        xm = jnp.concatenate([jnp.where(head == j, x4, zero) for j in range(gh)], axis=0)
        dall[q] = dot_nt(xm, g[:, lanes(q)])
        return carry

    lax.fori_loop(0, groups, outer, 0)

    def land(ka, carry):
        arrive(w_slot, wfs, wfr, ka)
        if halved:
            across(ka).start()
        return carry

    lax.fori_loop(0, n_a, land, 0)
    if halved:
        lax.fori_loop(0, n_a, lambda ka, carry: (across(ka).wait_recv(), carry)[1], 0)
        total = None
        for k in range(n_ctx):
            picked = jnp.concatenate(
                [tok[:, i * rows + k * half:i * rows + (k + 1) * half] for i in range(n_dp)], axis=1)
            term = dot_nt(picked, wall[k])
            total = term if total is None else total + term
        proj[:, :wcols] = total
    elif wide:
        proj[:, :wcols] = dot_nt(tok[...], wall[...])
    else:
        def shard(i, carry):
            proj[:, :wcols] += dot_nt(tok[i], wall[i])
            return carry

        lax.fori_loop(0, n_dp, shard, 0)
    rate_scale = -jnp.exp(vec[0:1, :])
    b = proj[:, :STATE].astype(BF16)
    z = proj[:, STATE:STATE + LANES] + vec[1:2, :]
    dt = jnp.maximum(z, 0.0) + jnp.log1p(jnp.exp(-jnp.abs(z)))
    row_i, col_i = iota((t, t), 0), iota((t, t), 1)
    lower = jnp.where(row_i >= col_i, 1.0, 0.0).astype(BF16)
    upper = jnp.where(col_i >= row_i, 1.0, 0.0).astype(BF16)
    cum = dot_exact(lower, rate_scale * dt)
    cum_r[...] = cum
    dt_r[...] = dt
    cumt[...] = cum.T
    last = cum_r[t - 1:t, :]
    to_end = jnp.exp(last - cum)
    wgt = to_end * dt
    grow = jnp.exp(cum)
    w_bf = wgt.astype(BF16)
    e_bf = grow.astype(BF16)
    cv = c[...]
    bt = b.astype(F32).T.astype(BF16)
    ct = cv.astype(F32).T.astype(BF16)

    span = [slice(q * LANES, (q + 1) * LANES) for q in range(groups)]
    for at in span:
        xw[:, at] = (dot(w_bf, spread_m[:, at]) * x[:, at].astype(F32)).astype(BF16)
        gwt[:, at] = (dot(e_bf, spread_m[:, at]) * g[:, at].astype(F32)).astype(BF16)
    sloc[0] = dot(bt, xw[...]).astype(BF16)
    sloc[1] = dot(ct, gwt[...]).astype(BF16)
    each(n_ctx, lambda k: c_copy(k).start())
    if n_ctx > 2:
        decs[...] = jnp.broadcast_to(jnp.exp(last), decs.shape)
        crecv[my] = jnp.zeros(crecv.shape[1:], BF16)
        decr[my] = jnp.zeros(decr.shape[1:], F32)
        each(n_ctx, lambda k: d_copy(k).start())

    scores = dot_nt(b, cv)
    causal = col_i >= row_i

    def mix(q, carry):
        g4 = g[:, lanes(q)]
        shift = lax.rem(LANES - gh * q, LANES)
        cum_s = pltpu.roll(cum_r[...], shift, 1)
        dt_s = pltpu.roll(dt_r[...], shift, 1)
        total = ds[...]
        quot = qacc[...]
        mixed = []
        for j in range(gh):
            h = gh * q + j
            spread = cumt[pl.ds(h, 1), :] - cum_s[:, j:j + 1]
            factor = jnp.exp(jnp.where(causal, spread, -1e30))
            step = dt_s[:, j:j + 1]
            d = dall[q, j * t:(j + 1) * t]
            fs = factor * scores
            mixed.append((fs * step).astype(BF16))
            u = d * fs
            quot = jnp.where(col_i == h, jnp.sum(u, axis=1, keepdims=True), quot)
            rowt[pl.ds(h, 1), :] = jnp.sum(u * step, axis=0, keepdims=True)
            total = total + d * (factor * step)
        ds[...] = total
        qacc[...] = quot
        out = dot(jnp.concatenate(mixed, axis=0), g4)
        acc = dexp[:, lanes(q)] * g4.astype(F32)
        for j in range(gh):
            acc = acc + jnp.where(head == j, out[j * t:(j + 1) * t], 0.0)
        dx[:, lanes(q)] = acc
        return carry

    lax.fori_loop(0, groups, mix, 0)
    each(n_ctx, lambda k: c_copy(k).wait_recv())
    if n_ctx > 2:
        each(n_ctx, lambda k: d_copy(k).wait_recv())

    sv = sg = jnp.zeros((t, LANES), F32)
    db2 = dc2 = jnp.zeros((t, STATE), F32)
    gs = jnp.zeros((8, LANES), F32)
    for at in span:
        e, et = spread_m[:, at], gather_m[at, :]
        if n_ctx == 2:
            got = crecv[1 - my, :, at]
            none = jnp.zeros_like(got)
            s4 = jnp.where(my > 0, got, none)
            g4s = jnp.where(my < 1, got, none)
        else:
            s = jnp.zeros((STATE, LANES), F32)
            k = s
            for i in range(n_ctx):
                dec = dot_split(decr[i], e)[0:1]
                s = jnp.where(i < my, dec * s + crecv[i, :, at].astype(F32), s)
            for i in reversed(range(n_ctx)):
                dec = dot_split(decr[i], e)[0:1]
                k = jnp.where(i > my, dec * k + crecv[i, :, at].astype(F32), k)
            s4, g4s = s.astype(BF16), k.astype(BF16)
            both = jnp.sum(s * k, axis=0, keepdims=True)
            gs = gs + dot_split(jnp.broadcast_to(both, (8, LANES)), et)
        us = dot(cv, s4)
        ug = dot(b, g4s)
        sv = sv + dot_split(x[:, at].astype(F32) * ug, et)
        sg = sg + dot_split(g[:, at].astype(F32) * us, et)
        db2 = db2 + dot_nt(xw[:, at], g4s)
        dc2 = dc2 + dot_nt(gwt[:, at], s4)
        gx[:, at] = (dx[:, at] + dot(w_bf, e) * ug).astype(BF16)
    dsv = ds[...]
    db = dot_split(dsv, cv) + db2
    dc = dot_split(dsv.T, b) + dc2
    gc[...] = dc.astype(BF16)
    quot = qacc[...]
    v = sv
    vw = v * wgt
    dcum = rowt[...].T + grow * sg - dt * quot - vw
    tail = jnp.sum(vw, axis=0, keepdims=True)
    if n_ctx > 2:
        tail = tail + jnp.exp(last) * gs[0:1, :]
    dcum = dcum + jnp.where(row_i == t - 1, tail, 0.0)
    drate = dot_exact(upper, dcum)
    ddt = quot + v * to_end + rate_scale * drate
    dz = ddt / (1.0 + jnp.exp(-z))
    proj[...] = jnp.zeros_like(proj)
    proj[:, :STATE] = db.astype(BF16).astype(F32)
    proj[:, STATE:cols] = dz[:, :heads]
    whole = proj[...]
    gall[:, blk(me)] = whole.T[:wcols].astype(BF16)
    first(g_slot, gzs, gzr, gfs, gfr)
    gp[...] = whole[:, :cols].astype(BF16)
    pass_on(g_slot, gzs, gzr, gfs, gfr)
    each(n_dp, lambda k: a_copy(k).wait_recv())
    lax.fori_loop(0, n_a, lambda ka, carry: (arrive(g_slot, gfs, gfr, ka), carry)[1], 0)
    part[...] = dot(gall[...], trecv[...])
    for o in range(n_ctx):
        pst[o] = part[o * cb:o * cb + cbp, :]
    each(n_ctx, lambda k: p_copy(k).start())
    each(n_ctx, lambda k: p_copy(k).wait_recv())

    def add(k, acc):
        return acc + precv[mate(k)]

    total = lax.fori_loop(1, n_ctx, add, pst[my])
    gw[...] = (total * (1.0 / n_dp)).T[:, :cb]
    settle(w_slot, wzs, wzr, wfs, wfr)
    if halved:
        lax.fori_loop(0, n_a, lambda ka, carry: (across(ka).wait_send(), carry)[1], 0)
    each(n_dp, lambda k: a_copy(k).wait_send())
    settle(g_slot, gzs, gzr, gfs, gfr)
    each(n_ctx, lambda k: c_copy(k).wait_send())
    each(n_ctx, lambda k: p_copy(k).wait_send())
    if n_ctx > 2:
        each(n_ctx, lambda k: d_copy(k).wait_send())


def store(*refs):
    sems = refs[-1]
    copies = [pltpu.make_async_copy(refs[i], refs[4 + i], sems.at[i]) for i in range(4)]
    for copy in copies:
        copy.start()
    for copy in copies:
        copy.wait()


def per_device(layer_in, inner_act, readout, w_in, a_log, dt_bias, d_skip, grad_out):
    n_dp, n_ctx = lax.axis_size("dp"), lax.axis_size("ctx")
    tokens, x, c, g = layer_in[0], inner_act[0], readout[0], grad_out[0]
    t, inner = x.shape
    rows, cols = w_in.shape
    heads = a_log.shape[0]
    width = inner // heads
    wcols = up(cols, 16)
    wide = rows % LANES == 0
    wt = jnp.pad(w_in.T, ((0, wcols - cols), (0, 0)))
    if not wide:
        tokens = jnp.swapaxes(tokens.reshape(t, n_dp, rows), 0, 1)
    vec = jnp.pad(jnp.stack([a_log, dt_bias]), ((0, 6), (0, LANES - heads)))
    dexp = jnp.repeat(d_skip, width)[None]
    cb = cols // n_ctx
    cbp = up(cb, 8)
    vm = pltpu.VMEM
    n_a = n_dp // inner_group(n_dp)
    if not wide:
        wall = (n_dp, wcols, rows)
    elif rows % (n_ctx * LANES) == 0 and n_ctx == 2:
        wall = (n_ctx, wcols, n_dp * rows // n_ctx)
    else:
        wall = (wcols, n_dp * rows)
    scratch = [
        vm(tokens.shape, BF16),
        vm((t, inner), BF16),
        vm((t, inner), BF16),
        vm(wall, BF16),
        vm((n_dp * t, rows), BF16),
        vm((wcols, n_dp * t), BF16),
        vm((2, STATE, inner), BF16),
        vm((n_ctx, STATE, inner), BF16),
        vm((inner // LANES, LANES // width * t, t), F32),
        vm((LANES, inner), BF16),
        vm((inner, LANES), BF16),
        vm((t, inner), BF16),
        vm((t, inner), BF16),
        vm((t, inner), F32),
        vm((t, 2 * LANES), F32),
        vm((t, LANES), F32),
        vm((t, LANES), F32),
        vm((LANES, t), F32),
        vm((LANES, t), F32),
        vm((t, LANES), F32),
        vm((t, t), F32),
        vm((wcols, rows), F32),
        vm((n_ctx, cbp, rows), F32),
        vm((n_ctx, cbp, rows), F32),
        vm((8, LANES), F32),
        vm((n_ctx, 8, LANES), F32),
    ]
    dma = pltpu.SemaphoreType.DMA
    scratch += [dma((n_a,))] * 2 + [dma((n_dp,))] * 4 + [dma((n_a,))] * 2 + [dma((n_dp,))] * 2
    scratch += [dma((n_ctx,))] * 6 + [dma((n_a,))] * 2 + [dma((3,))]
    hbm = pl.BlockSpec(memory_space=pltpu.HBM)
    spec = pl.BlockSpec(memory_space=pltpu.VMEM)
    cfg = (n_dp, n_ctx, t, rows, heads, width, cols)
    results = pl.pallas_call(
        functools.partial(kernel, cfg),
        out_shape=(
            jax.ShapeDtypeStruct((t, inner), BF16),
            jax.ShapeDtypeStruct((t, STATE), BF16),
            jax.ShapeDtypeStruct((t, cols), BF16),
            jax.ShapeDtypeStruct((rows, cb), F32),
        ),
        in_specs=[hbm] * 3 + [spec] * 4,
        out_specs=(spec,) * 4,
        scratch_shapes=scratch,
        compiler_params=pltpu.CompilerParams(
            collective_id=0, has_side_effects=True, vmem_limit_bytes=48 * 1024 * 1024),
        name="ssm_backward",
    )(tokens, x, g, c, wt, vec, dexp)
    gx, gc, gp, gw = pl.pallas_call(
        store,
        out_shape=tuple(jax.ShapeDtypeStruct(r.shape, r.dtype) for r in results),
        in_specs=[spec] * 4,
        out_specs=(hbm,) * 4,
        scratch_shapes=[dma((4,))],
        name="store_results",
    )(*results)
    return (gx[None], gc[None], gp[None], gw)


LOG2E = 1.4426950408889634
HROWS = 80
WROWS = 144


def exact_right(v, sel):
    hi = v.astype(BF16)
    mid, low = split(v - hi.astype(F32))
    return dot(hi, sel) + dot(mid, sel) + dot(low, sel)


def flip(i, k):
    if k == 0:
        return i
    if k == 1:
        return i + 1 - 2 * lax.rem(i, 2)
    if k == 2:
        return i + 2 - 4 * lax.div(i, 2)
    return 3 - i


def pair_kernel(cfg, tok_h, x_h, g_h, ct_h, w_h, alog_h, bias_h, skip_h, gx, gct, gpt, gwt,
                tok, x, g, a, ct, wv, alog, bias, skip, wall, spread, dall, gm, dg, mall, ascale, spu, ssend, srecv,
                xy, au, proj, ds, rowt, cst, csr, gph, gpr, pown, psend, precv, qsend, qrecv,
                wzs, wzr, wps, wpr, xs, xr, ks, kr, rs, rr, zs, zr, ls):
    t, rows, heads, width, cols = cfg
    half = rows // 2
    inner = x.shape[1]
    groups = inner // LANES
    gh = LANES // width
    cb = cols // 2
    me, my = lax.axis_index("dp"), lax.axis_index("ctx")
    za, pb = lax.div(me, 4), lax.rem(me, 4)
    mate = (me, 1 - my)

    def lanes(q, n=LANES):
        return pl.ds(pl.multiple_of(q * n, LANES), n)

    def local(src, dst, i):
        return pltpu.make_async_copy(src, dst, ls.at[i])

    smalls = [local(w_h, wv, 0), local(alog_h, alog, 1), local(bias_h, bias, 2), local(skip_h, skip, 3), local(ct_h, ct, 4)]
    tok_in = local(tok_h, tok.at[pl.ds(0, t)], 5)
    x_in, g_in = local(x_h, x, 6), local(g_h, g, 7)
    for load in smalls:
        load.start()
    tok_in.start()
    x_in.start()
    g_in.start()

    @pl.when(my == 0)
    def _():
        local(x_h, a, 8).start()

    @pl.when(my == 1)
    def _():
        local(g_h, a, 8).start()

    def remote(src, dst, send, recv, to):
        return pltpu.make_async_remote_copy(
            src_ref=src, dst_ref=dst, send_sem=send, recv_sem=recv, device_id=to, device_id_type=MESH)

    def z_peer(k):
        return (flip(za, k) * 4 + pb, my)

    def p_peer(k):
        return (za * 4 + flip(pb, k), my)

    barrier = pltpu.get_barrier_semaphore()
    for to in [z_peer(k) for k in (3, 2, 1)] + [p_peer(k) for k in (3, 2, 1)] + [mate]:
        pl.semaphore_signal(barrier, inc=1, device_id=to, device_id_type=MESH)

    smalls[0].wait()
    wfull = jnp.concatenate([wv[...], jnp.zeros((WROWS - cols, rows), BF16)], axis=0)
    wall[my, me] = jnp.where(my == 0, wfull[:, :half], wfull[:, half:])

    pl.semaphore_wait(barrier, 7)

    def w_z(k):
        return remote(wall.at[my, me], wall.at[my, me], wzs.at[k], wzr.at[k], z_peer(k))

    def w_p(kz, kp):
        slot = wall.at[my, flip(za, kz) * 4 + pb]
        return remote(slot, slot, wps.at[kz * 4 + kp], wpr.at[kz * 4 + kp], p_peer(kp))

    def w_x(kz):
        block = wall.at[my, pl.ds(flip(za, kz) * 4, 4)]
        return remote(block, block, xs.at[kz], xr.at[kz], mate)

    def mate_copy(src, dst, i):
        return remote(src, dst, ks.at[i], kr.at[i], mate)

    for k in (3, 2, 1):
        w_z(k).start()
    for k in (3, 1, 2):
        w_p(0, k).start()
    tok_in.wait()
    tok_x = mate_copy(tok.at[pl.ds(0, t)], tok.at[pl.ds(t, t)], 0)
    tok_x.start()

    for load in smalls[1:]:
        load.wait()
    spread[...] = jnp.where(iota((LANES, inner), 0) == iota((LANES, inner), 1) // width, 1.0, 0.0).astype(BF16)

    def row(ref):
        return jnp.concatenate([ref[...], jnp.zeros((1, LANES - heads), F32)], axis=1)

    rate_t = -jnp.exp(jnp.broadcast_to(row(alog), (LANES, LANES)).T[:HROWS])
    bias_t = jnp.broadcast_to(row(bias), (LANES, LANES)).T[:HROWS]
    skip_hi, skip_lo = split(jnp.broadcast_to(row(skip), (16, LANES)))
    x_in.wait()
    g_in.wait()
    head = iota((t, LANES), 1) // width

    def outer(q, carry):
        x4, g4 = x[:, lanes(q)], g[:, lanes(q)]
        zero = jnp.zeros_like(x4)
        dall[q] = dot_nt(jnp.concatenate([jnp.where(head == j, x4, zero) for j in range(gh)], axis=0), g4)
        gm[q] = jnp.concatenate([jnp.where(head == j, g4, zero) for j in range(gh)], axis=0)
        e = spread[:, lanes(q)]
        skip4 = (dot(skip_hi, e) + dot(skip_lo, e))[0:1]
        dg[:, lanes(q)] = skip4 * g4.astype(F32)
        return carry

    lax.fori_loop(0, groups, outer, 0)
    ds[...] = jnp.zeros_like(ds)
    rowt[...] = jnp.zeros_like(rowt)
    csr[...] = jnp.zeros_like(csr)
    ctv = ct[...]
    row_i, col_i = iota((t, t), 0), iota((t, t), 1)
    later = jnp.where(col_i >= row_i, 1.0, 0.0).astype(BF16)
    sooner = jnp.where(row_i >= col_i, 1.0, 0.0).astype(BF16)
    first = my == 0

    @pl.when(first)
    def _():
        local(x_h, a, 8).wait()

    @pl.when(my == 1)
    def _():
        local(g_h, a, 8).wait()

    def take(kz, acc):
        w_x(kz).wait_recv()
        base = flip(za, kz) * 4
        for j in range(4):
            block = jnp.concatenate([wall[0, base + j], wall[1, base + j]], axis=1)
            term = dot_nt(block, tok[0:t, lanes(base + j, rows)])
            acc = term if acc is None else acc + term
        return acc

    def landed(kz):
        for kp in (1, 2, 3):
            w_p(kz, kp).wait_recv()
        w_x(kz).start()

    for kz in (1, 2, 3):
        w_z(kz).wait_recv()
        for kp in (3, 1, 2):
            w_p(kz, kp).start()
    acc = None
    for kz in range(4):
        landed(kz)
        if kz > 0:
            acc = take(kz - 1, acc)
    acc = take(3, acc)

    z = acc[STATE:] + bias_t
    bt = acc[:STATE].astype(BF16)
    dt = jnp.maximum(z, 0.0) + jnp.log1p(jnp.exp(-jnp.abs(z)))
    cum = exact_right(rate_t * dt, later)
    csr[0:HROWS] = cum * LOG2E - jnp.log(jnp.maximum(dt, 1e-37)) * LOG2E
    cst[...] = cum * LOG2E
    wgt = jnp.exp(cum[:, t - 1:t] - cum) * dt
    scale_t = jnp.where(first, wgt, jnp.exp(cum))
    scale = jnp.concatenate([scale_t, jnp.zeros((LANES - HROWS, t), F32)], axis=0).T.astype(BF16)
    csr[...] = csr[...].T
    pad = jnp.zeros((LANES - STATE, t), F32)
    b = jnp.concatenate([bt.astype(F32), pad], axis=0).T[:, :STATE].astype(BF16)
    lt = jnp.where(first, bt, ctv)
    left = jnp.concatenate([lt.astype(F32), pad], axis=0).T[:, :STATE].astype(BF16)
    for q in range(groups):
        at = slice(q * LANES, (q + 1) * LANES)
        s4 = dot(scale, spread[:, at])
        spu[:, at] = jnp.where(first, s4, 0.0)
        ascale[:, at] = (s4 * a[:, at].astype(F32)).astype(BF16)
    ssend[...] = dot(lt, ascale[...]).astype(BF16)
    state_x = mate_copy(ssend, srecv, 1)
    state_x.start()

    scores = jnp.where(col_i >= row_i, dot(b, ctv), 0.0)
    dscore_rows = 32

    def mix(q, carry):
        shift = lax.rem(LANES - gh * q, LANES)
        cs = pltpu.roll(csr[...], shift, 1)
        tops = [cst[pl.ds(gh * q + j, 1), :] for j in range(gh)]
        sums = [jnp.zeros((8, t), F32) for _ in range(gh)]
        for r in range(t // dscore_rows):
            at = slice(r * dscore_rows, (r + 1) * dscore_rows)
            total = ds[at]
            for j in range(gh):
                e = jnp.exp2(jnp.minimum(tops[j] - cs[at, j:j + 1], 100.0))
                m = e * scores[at]
                d = dall[q, j * t + r * dscore_rows:j * t + (r + 1) * dscore_rows]
                mall[q, at, j * LANES:(j + 1) * LANES] = m.astype(BF16)
                total = total + d * e
                u = d * m
                for i in range(dscore_rows // 8):
                    sums[j] = sums[j] + u[8 * i:8 * i + 8]
            ds[at] = total
        for j in range(gh):
            rowt[pl.ds(gh * q + j, 1), :] = jnp.sum(sums[j], axis=0, keepdims=True)
        return carry

    lax.fori_loop(0, groups, mix, 0)
    state_x.wait_recv()
    for q in range(groups):
        at = slice(q * LANES, (q + 1) * LANES)
        u = dot(left, srecv[:, at])
        y = dot(mall[q], gm[q]) + spu[:, at] * u
        au[:, at] = (ascale[:, at].astype(F32) * u).astype(BF16)
        xy[:, at] = (x[:, at].astype(F32) * y).astype(BF16)
        gx[:, at] = (y + dg[:, at]).astype(BF16)
    sel = spread[:HROWS]
    qt = dot_nt(sel, xy[...])
    zt = dot_nt(sel, au[...])
    d2 = dot_nt(srecv[...], ascale[...])
    dscore = jnp.where(col_i >= row_i, ds[...], 0.0).astype(BF16)
    dbt = dot_nt(ctv, dscore) + jnp.where(first, d2, 0.0)
    dct = dot(bt, dscore) + jnp.where(first, 0.0, d2)
    gct[...] = dct.astype(BF16)
    tail = jnp.sum(zt, axis=1, keepdims=True)
    dcum = rowt[...] - qt + jnp.where(first, jnp.where(iota((HROWS, t), 1) == t - 1, tail, 0.0), zt)
    hi, lo = split(dcum)
    drate = dot(hi, sooner) + dot(lo, sooner)
    sig = 1.0 / (1.0 + jnp.exp(-z))
    ratio = jnp.where(dt > 1e-30, sig / jnp.maximum(dt, 1e-30), 1.0)
    dzt = qt * ratio + rate_t * drate * sig
    proj[0:STATE] = dbt
    proj[STATE:] = dzt
    gph[0] = proj[0:HROWS].astype(BF16)
    gph[1] = jnp.concatenate([proj[cb:cols], jnp.zeros((HROWS - cb, t), F32)], axis=0).astype(BF16)
    gp_x = mate_copy(gph.at[1 - my], gpr, 2)
    gp_x.start()
    gpt[...] = proj[0:cols].astype(BF16)

    tok_x.wait_recv()
    gp_x.wait_recv()
    lhs = jnp.concatenate([gph[my], gpr[...]], axis=1)

    def r_p(kz, kp):
        return remote(psend.at[kz, kp], precv.at[kz, kp], rs.at[kz * 4 + kp], rr.at[kz * 4 + kp], p_peer(kp))

    def r_z(kz):
        return remote(qsend.at[kz], qrecv.at[kz], zs.at[kz], zr.at[kz], z_peer(kz))

    order = (3, 2, 1, 0)
    for kz in order:
        for kp in (3, 1, 2, 0):
            i = flip(za, kz) * 4 + flip(pb, kp)
            part = dot(lhs, tok[:, lanes(i, rows)])
            if kp == 0:
                pown[kz] = part
            else:
                psend[kz, kp] = part.astype(BF16)
                r_p(kz, kp).start()
    for kz in order:
        total = pown[kz]
        for kp in (1, 2, 3):
            r_p(kz, kp).wait_recv()
            total = total + precv[kz, kp].astype(F32)
        if kz == 0:
            for k in (1, 2, 3):
                r_z(k).wait_recv()
                total = total + qrecv[k].astype(F32)
            gwt[...] = (total * (1.0 / 16))[:cb]
        else:
            qsend[kz] = total.astype(BF16)
            r_z(kz).start()

    for k in (1, 2, 3):
        w_z(k).wait_send()
        r_z(k).wait_send()
        for kz in range(4):
            w_p(kz, k).wait_send()
            r_p(kz, k).wait_send()
    for kz in range(4):
        w_x(kz).wait_send()
    tok_x.wait_send()
    state_x.wait_send()
    gp_x.wait_send()


def pair_device(layer_in, inner_act, readout, w_in, a_log, dt_bias, d_skip, grad_out):
    tokens, x, ct, g = layer_in[0], inner_act[0], readout[0].T, grad_out[0]
    t, inner = x.shape
    rows, cols = w_in.shape
    heads = a_log.shape[0]
    width = inner // heads
    groups, gh = inner // LANES, LANES // width
    cb = cols // 2
    vm = pltpu.VMEM
    scratch = [
        vm((2 * t, tokens.shape[1]), BF16),
        vm((t, inner), BF16),
        vm((t, inner), BF16),
        vm((t, inner), BF16),
        vm((STATE, t), BF16),
        vm((cols, rows), BF16),
        vm((1, heads), F32),
        vm((1, heads), F32),
        vm((1, heads), F32),
        vm((2, 16, WROWS, rows // 2), BF16),
        vm((LANES, inner), BF16),
        vm((groups, gh * t, t), F32),
        vm((groups, gh * t, LANES), BF16),
        vm((t, inner), F32),
        vm((groups, t, gh * t), BF16),
        vm((t, inner), BF16),
        vm((t, inner), F32),
        vm((STATE, inner), BF16),
        vm((STATE, inner), BF16),
        vm((t, inner), BF16),
        vm((t, inner), BF16),
        vm((WROWS, t), F32),
        vm((t, t), F32),
        vm((HROWS, t), F32),
        vm((HROWS, t), F32),
        vm((LANES, LANES), F32),
        vm((2, HROWS, t), BF16),
        vm((HROWS, t), BF16),
        vm((4, HROWS, rows), F32),
        vm((4, 4, HROWS, rows), BF16),
        vm((4, 4, HROWS, rows), BF16),
        vm((4, HROWS, rows), BF16),
        vm((4, HROWS, rows), BF16),
    ]
    dma = pltpu.SemaphoreType.DMA
    scratch += [dma((4,))] * 2 + [dma((16,))] * 2 + [dma((4,))] * 4 + [dma((16,))] * 2 + [dma((4,))] * 2 + [dma((9,))]
    hbm = pl.BlockSpec(memory_space=pltpu.HBM)
    spec = pl.BlockSpec(memory_space=pltpu.VMEM)
    results = pl.pallas_call(
        functools.partial(pair_kernel, (t, rows, heads, width, cols)),
        out_shape=(
            jax.ShapeDtypeStruct((t, inner), BF16),
            jax.ShapeDtypeStruct((STATE, t), BF16),
            jax.ShapeDtypeStruct((cols, t), BF16),
            jax.ShapeDtypeStruct((cb, rows), F32),
        ),
        in_specs=[hbm] * 8,
        out_specs=(spec,) * 4,
        scratch_shapes=scratch,
        compiler_params=pltpu.CompilerParams(
            collective_id=0, has_side_effects=True, vmem_limit_bytes=VMEM_MAIN),
        name="ssm_backward",
    )(tokens, x, g, ct, w_in.T, a_log[None], dt_bias[None], d_skip[None])
    gx, gct, gpt, gwt = pl.pallas_call(
        store,
        out_shape=tuple(jax.ShapeDtypeStruct(r.shape, r.dtype) for r in results),
        in_specs=[spec] * 4,
        out_specs=(hbm,) * 4,
        scratch_shapes=[dma((4,))],
        compiler_params=pltpu.CompilerParams(vmem_limit_bytes=VMEM_STORE),
        name="store_results",
    )(*results)
    return (gx[None], gct.T[None], gpt.T[None], gwt.T)


def solution(mesh):
    in_specs = (
        P("dp", "ctx", None),
        P("dp", "ctx", None),
        P("dp", "ctx", None),
        P("dp", None),
        P(),
        P(),
        P(),
        P("dp", "ctx", None),
    )
    out_specs = (P("dp", "ctx", None), P("dp", "ctx", None), P("dp", "ctx", None), P("dp", "ctx"))
    pairs = mesh.shape["dp"] == 16 and mesh.shape["ctx"] == 2
    return jax.shard_map(
        pair_device if pairs else per_device, mesh=mesh, in_specs=in_specs, out_specs=out_specs, check_vma=False
    )
```

```python
import functools

import jax
import jax.numpy as jnp
from jax import lax
from jax.experimental import pallas as pl
from jax.experimental.pallas import tpu as pltpu
from jax.sharding import PartitionSpec as P

STATE = 64
LANES = 128
MESH = pl.DeviceIdType.MESH
VMEM_MAIN = 62 * 1024 * 1024
VMEM_STORE = 62 * 1024 * 1024
F32 = jnp.float32
BF16 = jnp.bfloat16


def inner_group(n):
    b = 1
    while b * b < n and n % (2 * b) == 0:
        b *= 2
    return b


def up(n, m):
    return -(-n // m) * m


def dot(a, b):
    return jnp.dot(a, b, preferred_element_type=F32)


def dot_nt(a, b):
    return lax.dot_general(a, b, (((1,), (1,)), ((), ())), preferred_element_type=F32)


def split(v):
    hi = v.astype(BF16)
    return hi, (v - hi.astype(F32)).astype(BF16)


def dot_split(v, b):
    hi, lo = split(v)
    return dot(hi, b) + dot(lo, b)


def dot_exact(sel, v):
    hi, rest = v.astype(BF16), None
    rest = v - hi.astype(F32)
    mid, low = split(rest)
    return dot(sel, hi) + dot(sel, mid) + dot(sel, low)


def iota(shape, dim):
    return lax.broadcasted_iota(jnp.int32, shape, dim)


def kernel(cfg, tok_h, x_h, g_h, c, w, vec, dexp, gx, gc, gp, gw, tok, x, g, wall, trecv, gall, sloc, crecv,
           dall, spread_m, gather_m, xw, gwt, dx, proj, cum_r, dt_r, cumt, rowt, qacc, ds, part, pst, precv,
           decs, decr, wzs, wzr, wfs, wfr, as_, ar, gzs, gzr, gfs, gfr, cs, cr, ps, pr, es, er, ms, mr, ls):
    n_dp, n_ctx, t, rows, heads, width, cols = cfg
    wide = rows % LANES == 0
    halved = wide and rows % (n_ctx * LANES) == 0 and n_ctx == 2
    half = rows // n_ctx
    n_b = inner_group(n_dp)
    n_a = n_dp // n_b
    my_a, my_b = lax.div(lax.axis_index("dp"), n_b), lax.rem(lax.axis_index("dp"), n_b)
    loads = [pltpu.make_async_copy(src, dst, ls.at[i]) for i, (src, dst) in enumerate(((x_h, x), (g_h, g), (tok_h, tok)))]
    for load in loads:
        load.start()
    groups = x.shape[1] // LANES
    gh = LANES // width
    cb = cols // n_ctx
    cbp = up(cb, 8)
    me = lax.axis_index("dp")
    my = lax.axis_index("ctx")

    def peer(k):
        return lax.rem(me + k, n_dp)

    def mate(k):
        return lax.rem(my + k, n_ctx)

    def col(ref, i):
        return ref.at[:, pl.ds(pl.multiple_of(i * rows, LANES), rows)] if wide else ref.at[i]

    def blk(i):
        return pl.ds(pl.multiple_of(i * t, LANES), t)

    def lanes(q):
        return pl.ds(pl.multiple_of(q * LANES, LANES), LANES)

    barrier = pltpu.get_barrier_semaphore()

    def greet(k, carry):
        pl.semaphore_signal(barrier, inc=1, device_id=(peer(k), my), device_id_type=MESH)
        return carry

    def greet_mate(k, carry):
        pl.semaphore_signal(barrier, inc=1, device_id=(me, mate(k)), device_id_type=MESH)
        return carry

    lax.fori_loop(1, n_dp, greet, 0)
    lax.fori_loop(1, n_ctx, greet_mate, 0)
    pl.semaphore_wait(barrier, n_dp + n_ctx - 2)

    def origin(ka, kb):
        return lax.rem(my_a + n_a - ka, n_a) * n_b + lax.rem(my_b + n_b - kb, n_b)

    def w_slot(i):
        if halved:
            return wall.at[my, :, pl.ds(pl.multiple_of(i * half, LANES), half)]
        return col(wall, i)

    def g_slot(i):
        return gall.at[:, blk(i)]

    def far(slot, send, recv, ka):
        return pltpu.make_async_remote_copy(
            src_ref=slot(me), dst_ref=slot(me), send_sem=send.at[ka], recv_sem=recv.at[ka],
            device_id=(lax.rem(my_a + ka, n_a) * n_b + my_b, my), device_id_type=MESH)

    def near(slot, send, recv, ka, kb):
        i = origin(ka, 0)
        return pltpu.make_async_remote_copy(
            src_ref=slot(i), dst_ref=slot(i), send_sem=send.at[ka * n_b + kb], recv_sem=recv.at[ka * n_b + kb],
            device_id=(my_a * n_b + lax.rem(my_b + kb, n_b), my), device_id_type=MESH)

    def across(ka):
        i = lax.rem(my_a + n_a - ka, n_a) * n_b
        block = wall.at[my, :, pl.ds(pl.multiple_of(i * half, LANES), n_b * half)]
        return pltpu.make_async_remote_copy(
            src_ref=block, dst_ref=block, send_sem=ms.at[ka], recv_sem=mr.at[ka],
            device_id=(me, 1 - my), device_id_type=MESH)

    def a_copy(k):
        return pltpu.make_async_remote_copy(
            src_ref=col(tok, peer(k)), dst_ref=trecv.at[blk(me), :], send_sem=as_.at[k],
            recv_sem=ar.at[k], device_id=(peer(k), my), device_id_type=MESH)

    def c_copy(k):
        other = mate(k)
        which = jnp.where(other > my, 0, 1)
        return pltpu.make_async_remote_copy(
            src_ref=sloc.at[which], dst_ref=crecv.at[my], send_sem=cs.at[k], recv_sem=cr.at[k],
            device_id=(me, other), device_id_type=MESH)

    def d_copy(k):
        return pltpu.make_async_remote_copy(
            src_ref=decs, dst_ref=decr.at[my], send_sem=es.at[k], recv_sem=er.at[k],
            device_id=(me, mate(k)), device_id_type=MESH)

    def p_copy(k):
        return pltpu.make_async_remote_copy(
            src_ref=pst.at[mate(k)], dst_ref=precv.at[my], send_sem=ps.at[k], recv_sem=pr.at[k],
            device_id=(me, mate(k)), device_id_type=MESH)

    def each(n, act):
        def step(k, carry):
            act(k)
            return carry

        lax.fori_loop(1, n, step, 0)

    def spread_near(slot, send, recv, ka):
        each(n_b, lambda kb: near(slot, send, recv, ka, kb).start())

    def first(slot, send, recv, fsend, frecv):
        each(n_a, lambda ka: far(slot, send, recv, ka).start())
        spread_near(slot, fsend, frecv, 0)

    def pass_on(slot, send, recv, fsend, frecv):
        def one(ka):
            far(slot, send, recv, ka).wait_recv()
            spread_near(slot, fsend, frecv, ka)

        each(n_a, one)

    def arrive(slot, fsend, frecv, ka):
        each(n_b, lambda kb: near(slot, fsend, frecv, ka, kb).wait_recv())

    def settle(slot, send, recv, fsend, frecv):
        each(n_a, lambda ka: far(slot, send, recv, ka).wait_send())

        def one(ka, carry):
            each(n_b, lambda kb: near(slot, fsend, frecv, ka, kb).wait_send())
            return carry

        lax.fori_loop(0, n_a, one, 0)

    inner = x.shape[1]
    wcols = w.shape[0]
    if halved:
        wall[my, :, pl.ds(pl.multiple_of(me * half, LANES), half)] = w[:, pl.ds(pl.multiple_of(my * half, LANES), half)]
    elif wide:
        wall[:, pl.ds(pl.multiple_of(me * rows, LANES), rows)] = w[...]
    else:
        wall[me] = w[...]
    first(w_slot, wzs, wzr, wfs, wfr)
    loads[0].wait()
    loads[1].wait()
    loads[2].wait()
    pass_on(w_slot, wzs, wzr, wfs, wfr)
    each(n_dp, lambda k: a_copy(k).start())
    if wide:
        trecv[blk(me), :] = tok[:, pl.ds(pl.multiple_of(me * rows, LANES), rows)]
    else:
        trecv[blk(me), :] = tok[me]
    proj[...] = jnp.zeros_like(proj)
    qacc[...] = jnp.zeros_like(qacc)
    ds[...] = jnp.zeros_like(ds)
    rowt[...] = jnp.zeros_like(rowt)
    spread_m[...] = jnp.where(iota((LANES, inner), 0) == iota((LANES, inner), 1) // width, 1.0, 0.0).astype(BF16)
    gather_m[...] = jnp.where(iota((inner, LANES), 1) == iota((inner, LANES), 0) // width, 1.0, 0.0).astype(BF16)
    head = iota((t, LANES), 1) // width

    def outer(q, carry):
        x4 = x[:, lanes(q)]
        zero = jnp.zeros_like(x4)
        xm = jnp.concatenate([jnp.where(head == j, x4, zero) for j in range(gh)], axis=0)
        dall[q] = dot_nt(xm, g[:, lanes(q)])
        return carry

    lax.fori_loop(0, groups, outer, 0)

    def land(ka, carry):
        arrive(w_slot, wfs, wfr, ka)
        if halved:
            across(ka).start()
        return carry

    lax.fori_loop(0, n_a, land, 0)
    if halved:
        lax.fori_loop(0, n_a, lambda ka, carry: (across(ka).wait_recv(), carry)[1], 0)
        total = None
        for k in range(n_ctx):
            picked = jnp.concatenate(
                [tok[:, i * rows + k * half:i * rows + (k + 1) * half] for i in range(n_dp)], axis=1)
            term = dot_nt(picked, wall[k])
            total = term if total is None else total + term
        proj[:, :wcols] = total
    elif wide:
        proj[:, :wcols] = dot_nt(tok[...], wall[...])
    else:
        def shard(i, carry):
            proj[:, :wcols] += dot_nt(tok[i], wall[i])
            return carry

        lax.fori_loop(0, n_dp, shard, 0)
    rate_scale = -jnp.exp(vec[0:1, :])
    b = proj[:, :STATE].astype(BF16)
    z = proj[:, STATE:STATE + LANES] + vec[1:2, :]
    dt = jnp.maximum(z, 0.0) + jnp.log1p(jnp.exp(-jnp.abs(z)))
    row_i, col_i = iota((t, t), 0), iota((t, t), 1)
    lower = jnp.where(row_i >= col_i, 1.0, 0.0).astype(BF16)
    upper = jnp.where(col_i >= row_i, 1.0, 0.0).astype(BF16)
    cum = dot_exact(lower, rate_scale * dt)
    cum_r[...] = cum
    dt_r[...] = dt
    cumt[...] = cum.T
    last = cum_r[t - 1:t, :]
    to_end = jnp.exp(last - cum)
    wgt = to_end * dt
    grow = jnp.exp(cum)
    w_bf = wgt.astype(BF16)
    e_bf = grow.astype(BF16)
    cv = c[...]
    bt = b.astype(F32).T.astype(BF16)
    ct = cv.astype(F32).T.astype(BF16)

    span = [slice(q * LANES, (q + 1) * LANES) for q in range(groups)]
    for at in span:
        xw[:, at] = (dot(w_bf, spread_m[:, at]) * x[:, at].astype(F32)).astype(BF16)
        gwt[:, at] = (dot(e_bf, spread_m[:, at]) * g[:, at].astype(F32)).astype(BF16)
    sloc[0] = dot(bt, xw[...]).astype(BF16)
    sloc[1] = dot(ct, gwt[...]).astype(BF16)
    each(n_ctx, lambda k: c_copy(k).start())
    if n_ctx > 2:
        decs[...] = jnp.broadcast_to(jnp.exp(last), decs.shape)
        crecv[my] = jnp.zeros(crecv.shape[1:], BF16)
        decr[my] = jnp.zeros(decr.shape[1:], F32)
        each(n_ctx, lambda k: d_copy(k).start())

    scores = dot_nt(b, cv)
    causal = col_i >= row_i

    def mix(q, carry):
        g4 = g[:, lanes(q)]
        shift = lax.rem(LANES - gh * q, LANES)
        cum_s = pltpu.roll(cum_r[...], shift, 1)
        dt_s = pltpu.roll(dt_r[...], shift, 1)
        total = ds[...]
        quot = qacc[...]
        mixed = []
        for j in range(gh):
            h = gh * q + j
            spread = cumt[pl.ds(h, 1), :] - cum_s[:, j:j + 1]
            factor = jnp.exp(jnp.where(causal, spread, -1e30))
            step = dt_s[:, j:j + 1]
            d = dall[q, j * t:(j + 1) * t]
            fs = factor * scores
            mixed.append((fs * step).astype(BF16))
            u = d * fs
            quot = jnp.where(col_i == h, jnp.sum(u, axis=1, keepdims=True), quot)
            rowt[pl.ds(h, 1), :] = jnp.sum(u * step, axis=0, keepdims=True)
            total = total + d * (factor * step)
        ds[...] = total
        qacc[...] = quot
        out = dot(jnp.concatenate(mixed, axis=0), g4)
        acc = dexp[:, lanes(q)] * g4.astype(F32)
        for j in range(gh):
            acc = acc + jnp.where(head == j, out[j * t:(j + 1) * t], 0.0)
        dx[:, lanes(q)] = acc
        return carry

    lax.fori_loop(0, groups, mix, 0)
    each(n_ctx, lambda k: c_copy(k).wait_recv())
    if n_ctx > 2:
        each(n_ctx, lambda k: d_copy(k).wait_recv())

    sv = sg = jnp.zeros((t, LANES), F32)
    db2 = dc2 = jnp.zeros((t, STATE), F32)
    gs = jnp.zeros((8, LANES), F32)
    for at in span:
        e, et = spread_m[:, at], gather_m[at, :]
        if n_ctx == 2:
            got = crecv[1 - my, :, at]
            none = jnp.zeros_like(got)
            s4 = jnp.where(my > 0, got, none)
            g4s = jnp.where(my < 1, got, none)
        else:
            s = jnp.zeros((STATE, LANES), F32)
            k = s
            for i in range(n_ctx):
                dec = dot_split(decr[i], e)[0:1]
                s = jnp.where(i < my, dec * s + crecv[i, :, at].astype(F32), s)
            for i in reversed(range(n_ctx)):
                dec = dot_split(decr[i], e)[0:1]
                k = jnp.where(i > my, dec * k + crecv[i, :, at].astype(F32), k)
            s4, g4s = s.astype(BF16), k.astype(BF16)
            both = jnp.sum(s * k, axis=0, keepdims=True)
            gs = gs + dot_split(jnp.broadcast_to(both, (8, LANES)), et)
        us = dot(cv, s4)
        ug = dot(b, g4s)
        sv = sv + dot_split(x[:, at].astype(F32) * ug, et)
        sg = sg + dot_split(g[:, at].astype(F32) * us, et)
        db2 = db2 + dot_nt(xw[:, at], g4s)
        dc2 = dc2 + dot_nt(gwt[:, at], s4)
        gx[:, at] = (dx[:, at] + dot(w_bf, e) * ug).astype(BF16)
    dsv = ds[...]
    db = dot_split(dsv, cv) + db2
    dc = dot_split(dsv.T, b) + dc2
    gc[...] = dc.astype(BF16)
    quot = qacc[...]
    v = sv
    vw = v * wgt
    dcum = rowt[...].T + grow * sg - dt * quot - vw
    tail = jnp.sum(vw, axis=0, keepdims=True)
    if n_ctx > 2:
        tail = tail + jnp.exp(last) * gs[0:1, :]
    dcum = dcum + jnp.where(row_i == t - 1, tail, 0.0)
    drate = dot_exact(upper, dcum)
    ddt = quot + v * to_end + rate_scale * drate
    dz = ddt / (1.0 + jnp.exp(-z))
    proj[...] = jnp.zeros_like(proj)
    proj[:, :STATE] = db.astype(BF16).astype(F32)
    proj[:, STATE:cols] = dz[:, :heads]
    whole = proj[...]
    gall[:, blk(me)] = whole.T[:wcols].astype(BF16)
    first(g_slot, gzs, gzr, gfs, gfr)
    gp[...] = whole[:, :cols].astype(BF16)
    pass_on(g_slot, gzs, gzr, gfs, gfr)
    each(n_dp, lambda k: a_copy(k).wait_recv())
    lax.fori_loop(0, n_a, lambda ka, carry: (arrive(g_slot, gfs, gfr, ka), carry)[1], 0)
    part[...] = dot(gall[...], trecv[...])
    for o in range(n_ctx):
        pst[o] = part[o * cb:o * cb + cbp, :]
    each(n_ctx, lambda k: p_copy(k).start())
    each(n_ctx, lambda k: p_copy(k).wait_recv())

    def add(k, acc):
        return acc + precv[mate(k)]

    total = lax.fori_loop(1, n_ctx, add, pst[my])
    gw[...] = (total * (1.0 / n_dp)).T[:, :cb]
    settle(w_slot, wzs, wzr, wfs, wfr)
    if halved:
        lax.fori_loop(0, n_a, lambda ka, carry: (across(ka).wait_send(), carry)[1], 0)
    each(n_dp, lambda k: a_copy(k).wait_send())
    settle(g_slot, gzs, gzr, gfs, gfr)
    each(n_ctx, lambda k: c_copy(k).wait_send())
    each(n_ctx, lambda k: p_copy(k).wait_send())
    if n_ctx > 2:
        each(n_ctx, lambda k: d_copy(k).wait_send())


def store(*refs):
    sems = refs[-1]
    copies = [pltpu.make_async_copy(refs[i], refs[4 + i], sems.at[i]) for i in range(4)]
    for copy in copies:
        copy.start()
    for copy in copies:
        copy.wait()


def per_device(layer_in, inner_act, readout, w_in, a_log, dt_bias, d_skip, grad_out):
    n_dp, n_ctx = lax.axis_size("dp"), lax.axis_size("ctx")
    tokens, x, c, g = layer_in[0], inner_act[0], readout[0], grad_out[0]
    t, inner = x.shape
    rows, cols = w_in.shape
    heads = a_log.shape[0]
    width = inner // heads
    wcols = up(cols, 16)
    wide = rows % LANES == 0
    wt = jnp.pad(w_in.T, ((0, wcols - cols), (0, 0)))
    if not wide:
        tokens = jnp.swapaxes(tokens.reshape(t, n_dp, rows), 0, 1)
    vec = jnp.pad(jnp.stack([a_log, dt_bias]), ((0, 6), (0, LANES - heads)))
    dexp = jnp.repeat(d_skip, width)[None]
    cb = cols // n_ctx
    cbp = up(cb, 8)
    vm = pltpu.VMEM
    n_a = n_dp // inner_group(n_dp)
    if not wide:
        wall = (n_dp, wcols, rows)
    elif rows % (n_ctx * LANES) == 0 and n_ctx == 2:
        wall = (n_ctx, wcols, n_dp * rows // n_ctx)
    else:
        wall = (wcols, n_dp * rows)
    scratch = [
        vm(tokens.shape, BF16),
        vm((t, inner), BF16),
        vm((t, inner), BF16),
        vm(wall, BF16),
        vm((n_dp * t, rows), BF16),
        vm((wcols, n_dp * t), BF16),
        vm((2, STATE, inner), BF16),
        vm((n_ctx, STATE, inner), BF16),
        vm((inner // LANES, LANES // width * t, t), F32),
        vm((LANES, inner), BF16),
        vm((inner, LANES), BF16),
        vm((t, inner), BF16),
        vm((t, inner), BF16),
        vm((t, inner), F32),
        vm((t, 2 * LANES), F32),
        vm((t, LANES), F32),
        vm((t, LANES), F32),
        vm((LANES, t), F32),
        vm((LANES, t), F32),
        vm((t, LANES), F32),
        vm((t, t), F32),
        vm((wcols, rows), F32),
        vm((n_ctx, cbp, rows), F32),
        vm((n_ctx, cbp, rows), F32),
        vm((8, LANES), F32),
        vm((n_ctx, 8, LANES), F32),
    ]
    dma = pltpu.SemaphoreType.DMA
    scratch += [dma((n_a,))] * 2 + [dma((n_dp,))] * 4 + [dma((n_a,))] * 2 + [dma((n_dp,))] * 2
    scratch += [dma((n_ctx,))] * 6 + [dma((n_a,))] * 2 + [dma((3,))]
    hbm = pl.BlockSpec(memory_space=pltpu.HBM)
    spec = pl.BlockSpec(memory_space=pltpu.VMEM)
    cfg = (n_dp, n_ctx, t, rows, heads, width, cols)
    results = pl.pallas_call(
        functools.partial(kernel, cfg),
        out_shape=(
            jax.ShapeDtypeStruct((t, inner), BF16),
            jax.ShapeDtypeStruct((t, STATE), BF16),
            jax.ShapeDtypeStruct((t, cols), BF16),
            jax.ShapeDtypeStruct((rows, cb), F32),
        ),
        in_specs=[hbm] * 3 + [spec] * 4,
        out_specs=(spec,) * 4,
        scratch_shapes=scratch,
        compiler_params=pltpu.CompilerParams(
            collective_id=0, has_side_effects=True, vmem_limit_bytes=48 * 1024 * 1024),
        name="ssm_backward",
    )(tokens, x, g, c, wt, vec, dexp)
    gx, gc, gp, gw = pl.pallas_call(
        store,
        out_shape=tuple(jax.ShapeDtypeStruct(r.shape, r.dtype) for r in results),
        in_specs=[spec] * 4,
        out_specs=(hbm,) * 4,
        scratch_shapes=[dma((4,))],
        name="store_results",
    )(*results)
    return (gx[None], gc[None], gp[None], gw)


LOG2E = 1.4426950408889634
HROWS = 80
WROWS = 144


def exact_right(v, sel):
    hi = v.astype(BF16)
    mid, low = split(v - hi.astype(F32))
    return dot(hi, sel) + dot(mid, sel) + dot(low, sel)


def flip(i, k):
    if k == 0:
        return i
    if k == 1:
        return i + 1 - 2 * lax.rem(i, 2)
    if k == 2:
        return i + 2 - 4 * lax.div(i, 2)
    return 3 - i


def pair_kernel(cfg, tok_h, x_h, g_h, ct_h, w_h, alog_h, bias_h, skip_h, gx_h, gct_h, gpt_h, gwt_h,
                tok, x, g, a, ct, wv, alog, bias, skip, wall, spread, dall, gm, dg, mall, ascale, spu, ssend, srecv,
                xy, au, proj, ds, rowt, cst, csr, gph, gpr, pown, psend, precv, qsend, qrecv,
                gx, gct, gpt, gwt,
                wzs, wzr, wps, wpr, xs, xr, ks, kr, rs, rr, zs, zr, ls):
    t, rows, heads, width, cols = cfg
    half = rows // 2
    inner = x.shape[1]
    groups = inner // LANES
    gh = LANES // width
    cb = cols // 2
    me, my = lax.axis_index("dp"), lax.axis_index("ctx")
    za, pb = lax.div(me, 4), lax.rem(me, 4)
    mate = (me, 1 - my)

    def lanes(q, n=LANES):
        return pl.ds(pl.multiple_of(q * n, LANES), n)

    def local(src, dst, i):
        return pltpu.make_async_copy(src, dst, ls.at[i])

    smalls = [local(w_h, wv, 0), local(alog_h, alog, 1), local(bias_h, bias, 2), local(skip_h, skip, 3), local(ct_h, ct, 4)]
    tok_in = local(tok_h, tok.at[pl.ds(0, t)], 5)
    x_in, g_in = local(x_h, x, 6), local(g_h, g, 7)
    for load in smalls:
        load.start()
    tok_in.start()
    x_in.start()
    g_in.start()

    @pl.when(my == 0)
    def _():
        local(x_h, a, 8).start()

    @pl.when(my == 1)
    def _():
        local(g_h, a, 8).start()

    def remote(src, dst, send, recv, to):
        return pltpu.make_async_remote_copy(
            src_ref=src, dst_ref=dst, send_sem=send, recv_sem=recv, device_id=to, device_id_type=MESH)

    def z_peer(k):
        return (flip(za, k) * 4 + pb, my)

    def p_peer(k):
        return (za * 4 + flip(pb, k), my)

    def n_peer(k):
        return (flip(za, 1) * 4 + flip(pb, k), my)

    barrier = pltpu.get_barrier_semaphore()
    for to in [z_peer(k) for k in (3, 2, 1)] + [n_peer(k) for k in (3, 2, 1)] + [p_peer(k) for k in (3, 2, 1)] + [mate]:
        pl.semaphore_signal(barrier, inc=1, device_id=to, device_id_type=MESH)

    smalls[0].wait()
    wfull = jnp.concatenate([wv[...], jnp.zeros((WROWS - cols, rows), BF16)], axis=0)
    wall[my, me] = jnp.where(my == 0, wfull[:, :half], wfull[:, half:])

    pl.semaphore_wait(barrier, 10)

    def w_z(k):
        return remote(wall.at[my, me], wall.at[my, me], wzs.at[k], wzr.at[k], z_peer(k))

    def w_p(kz, kp):
        if kz == 1:
            return remote(wall.at[my, me], wall.at[my, me], wps.at[4 + kp], wpr.at[4 + kp], n_peer(kp))
        slot = wall.at[my, flip(za, kz) * 4 + pb]
        return remote(slot, slot, wps.at[kz * 4 + kp], wpr.at[kz * 4 + kp], p_peer(kp))

    def w_x(kz):
        block = wall.at[my, pl.ds(flip(za, kz) * 4, 4)]
        return remote(block, block, xs.at[kz], xr.at[kz], mate)

    def mate_copy(src, dst, i):
        return remote(src, dst, ks.at[i], kr.at[i], mate)

    for k in (3, 2, 1):
        w_z(k).start()
    for kz in (0, 1):
        for k in (3, 1, 2):
            w_p(kz, k).start()
    tok_in.wait()
    tok_x = mate_copy(tok.at[pl.ds(0, t)], tok.at[pl.ds(t, t)], 0)
    tok_x.start()

    for load in smalls[1:]:
        load.wait()
    spread[...] = jnp.where(iota((LANES, inner), 0) == iota((LANES, inner), 1) // width, 1.0, 0.0).astype(BF16)

    def row(ref):
        return jnp.concatenate([ref[...], jnp.zeros((1, LANES - heads), F32)], axis=1)

    rate_t = -jnp.exp(jnp.broadcast_to(row(alog), (LANES, LANES)).T[:HROWS])
    bias_t = jnp.broadcast_to(row(bias), (LANES, LANES)).T[:HROWS]
    skip_hi, skip_lo = split(jnp.broadcast_to(row(skip), (16, LANES)))
    x_in.wait()
    g_in.wait()
    head = iota((t, LANES), 1) // width

    def outer(q, carry):
        x4, g4 = x[:, lanes(q)], g[:, lanes(q)]
        zero = jnp.zeros_like(x4)
        dall[q] = dot_nt(jnp.concatenate([jnp.where(head == j, x4, zero) for j in range(gh)], axis=0), g4)
        gm[q] = jnp.concatenate([jnp.where(head == j, g4, zero) for j in range(gh)], axis=0)
        e = spread[:, lanes(q)]
        skip4 = (dot(skip_hi, e) + dot(skip_lo, e))[0:1]
        dg[:, lanes(q)] = skip4 * g4.astype(F32)
        return carry

    lax.fori_loop(0, groups, outer, 0)
    ds[...] = jnp.zeros_like(ds)
    rowt[...] = jnp.zeros_like(rowt)
    csr[...] = jnp.zeros_like(csr)
    ctv = ct[...]
    row_i, col_i = iota((t, t), 0), iota((t, t), 1)
    later = jnp.where(col_i >= row_i, 1.0, 0.0).astype(BF16)
    sooner = jnp.where(row_i >= col_i, 1.0, 0.0).astype(BF16)
    first = my == 0

    @pl.when(first)
    def _():
        local(x_h, a, 8).wait()

    @pl.when(my == 1)
    def _():
        local(g_h, a, 8).wait()

    def take(kz, acc):
        w_x(kz).wait_recv()
        base = flip(za, kz) * 4
        for j in range(4):
            block = jnp.concatenate([wall[0, base + j], wall[1, base + j]], axis=1)
            term = dot_nt(block, tok[0:t, lanes(base + j, rows)])
            acc = term if acc is None else acc + term
        return acc

    def landed(kz):
        for kp in (1, 2, 3):
            w_p(kz, kp).wait_recv()
        w_x(kz).start()

    for kz in (1, 2, 3):
        w_z(kz).wait_recv()
        if kz > 1:
            for kp in (3, 1, 2):
                w_p(kz, kp).start()
    acc = None
    for kz in range(4):
        landed(kz)
        if kz > 0:
            acc = take(kz - 1, acc)
    acc = take(3, acc)

    z = acc[STATE:] + bias_t
    bt = acc[:STATE].astype(BF16)
    dt = jnp.maximum(z, 0.0) + jnp.log1p(jnp.exp(-jnp.abs(z)))
    cum = exact_right(rate_t * dt, later)
    csr[0:HROWS] = cum * LOG2E - jnp.log(jnp.maximum(dt, 1e-37)) * LOG2E
    cst[...] = cum * LOG2E
    wgt = jnp.exp(cum[:, t - 1:t] - cum) * dt
    scale_t = jnp.where(first, wgt, jnp.exp(cum))
    scale = jnp.concatenate([scale_t, jnp.zeros((LANES - HROWS, t), F32)], axis=0).T.astype(BF16)
    csr[...] = csr[...].T
    pad = jnp.zeros((LANES - STATE, t), F32)
    b = jnp.concatenate([bt.astype(F32), pad], axis=0).T[:, :STATE].astype(BF16)
    lt = jnp.where(first, bt, ctv)
    left = jnp.concatenate([lt.astype(F32), pad], axis=0).T[:, :STATE].astype(BF16)
    for q in range(groups):
        at = slice(q * LANES, (q + 1) * LANES)
        s4 = dot(scale, spread[:, at])
        spu[:, at] = jnp.where(first, s4, 0.0)
        ascale[:, at] = (s4 * a[:, at].astype(F32)).astype(BF16)
    ssend[...] = dot(lt, ascale[...]).astype(BF16)
    state_x = mate_copy(ssend, srecv, 1)
    state_x.start()

    scores = jnp.where(col_i >= row_i, dot(b, ctv), 0.0)
    dscore_rows = 32

    def mix(q, carry):
        shift = lax.rem(LANES - gh * q, LANES)
        cs = pltpu.roll(csr[...], shift, 1)
        tops = [cst[pl.ds(gh * q + j, 1), :] for j in range(gh)]
        sums = [jnp.zeros((8, t), F32) for _ in range(gh)]
        for r in range(t // dscore_rows):
            at = slice(r * dscore_rows, (r + 1) * dscore_rows)
            total = ds[at]
            for j in range(gh):
                e = jnp.exp2(jnp.minimum(tops[j] - cs[at, j:j + 1], 100.0))
                m = e * scores[at]
                d = dall[q, j * t + r * dscore_rows:j * t + (r + 1) * dscore_rows]
                mall[q, at, j * LANES:(j + 1) * LANES] = m.astype(BF16)
                total = total + d * e
                u = d * m
                for i in range(dscore_rows // 8):
                    sums[j] = sums[j] + u[8 * i:8 * i + 8]
            ds[at] = total
        for j in range(gh):
            rowt[pl.ds(gh * q + j, 1), :] = jnp.sum(sums[j], axis=0, keepdims=True)
        return carry

    lax.fori_loop(0, groups, mix, 0)
    state_x.wait_recv()
    for q in range(groups):
        at = slice(q * LANES, (q + 1) * LANES)
        u = dot(left, srecv[:, at])
        y = dot(mall[q], gm[q]) + spu[:, at] * u
        au[:, at] = (ascale[:, at].astype(F32) * u).astype(BF16)
        xy[:, at] = (x[:, at].astype(F32) * y).astype(BF16)
        gx[:, at] = (y + dg[:, at]).astype(BF16)
    gx_out = local(gx, gx_h, 9)
    gx_out.start()
    sel = spread[:HROWS]
    qt = dot_nt(sel, xy[...])
    zt = dot_nt(sel, au[...])
    d2 = dot_nt(srecv[...], ascale[...])
    dscore = jnp.where(col_i >= row_i, ds[...], 0.0).astype(BF16)
    dbt = dot_nt(ctv, dscore) + jnp.where(first, d2, 0.0)
    dct = dot(bt, dscore) + jnp.where(first, 0.0, d2)
    gct[...] = dct.astype(BF16)
    gct_out = local(gct, gct_h, 10)
    gct_out.start()
    tail = jnp.sum(zt, axis=1, keepdims=True)
    dcum = rowt[...] - qt + jnp.where(first, jnp.where(iota((HROWS, t), 1) == t - 1, tail, 0.0), zt)
    hi, lo = split(dcum)
    drate = dot(hi, sooner) + dot(lo, sooner)
    sig = 1.0 / (1.0 + jnp.exp(-z))
    ratio = jnp.where(dt > 1e-30, sig / jnp.maximum(dt, 1e-30), 1.0)
    dzt = qt * ratio + rate_t * drate * sig
    proj[0:STATE] = dbt
    proj[STATE:] = dzt
    gph[0] = proj[0:HROWS].astype(BF16)
    gph[1] = jnp.concatenate([proj[cb:cols], jnp.zeros((HROWS - cb, t), F32)], axis=0).astype(BF16)
    gp_x = mate_copy(gph.at[1 - my], gpr, 2)
    gp_x.start()
    gpt[...] = proj[0:cols].astype(BF16)
    gpt_out = local(gpt, gpt_h, 11)
    gpt_out.start()

    tok_x.wait_recv()
    gp_x.wait_recv()
    lhs = jnp.concatenate([gph[my], gpr[...]], axis=1)

    def r_p(kz, kp):
        to = p_peer(kp)
        return remote(psend.at[kz, kp], precv.at[kz, kp], rs.at[kz * 4 + kp], rr.at[kz * 4 + kp], to)

    def r_z(kz):
        return remote(qsend.at[kz], qrecv.at[kz], zs.at[kz], zr.at[kz], z_peer(kz))

    def packed(part):
        sides = (part[:, :half], part[:, half:])
        return jnp.concatenate([side[:STATE] for side in sides] + [side[STATE:STATE + 8] for side in sides], axis=0)

    order = (3, 2, 1, 0)
    for kz in order:
        for kp in (3, 1, 2, 0):
            i = flip(za, kz) * 4 + flip(pb, kp)
            part = packed(dot(lhs, tok[:, lanes(i, rows)]))
            if kp == 0:
                pown[kz] = part
            else:
                psend[kz, kp] = part.astype(BF16)
                r_p(kz, kp).start()
    for kz in (3, 2, 1):
        total = pown[kz]
        for kp in (1, 2, 3):
            r_p(kz, kp).wait_recv()
            total = total + precv[kz, kp].astype(F32)
        qsend[kz] = total.astype(BF16)
        r_z(kz).start()
    total = pown[0]
    for kz, kp in [(0, k) for k in (1, 2, 3)]:
        r_p(kz, kp).wait_recv()
        total = total + precv[kz, kp].astype(F32)
    for kz in (3, 2, 1):
        r_z(kz).wait_recv()
        total = total + qrecv[kz].astype(F32)
    total = total * (1.0 / 16)
    at = 2 * STATE
    gwt[0:STATE] = jnp.concatenate([total[:STATE], total[STATE:at]], axis=1)
    gwt[STATE:cb] = jnp.concatenate([total[at:at + 8], total[at + 8:]], axis=1)[:cb - STATE]
    gwt_out = local(gwt, gwt_h, 12)
    gwt_out.start()

    for k in (1, 2, 3):
        w_z(k).wait_send()
        for kz in range(4):
            w_p(kz, k).wait_send()
            r_p(kz, k).wait_send()
    for kz in (3, 2, 1):
        r_z(kz).wait_send()
    for kz in range(4):
        w_x(kz).wait_send()
    tok_x.wait_send()
    state_x.wait_send()
    gp_x.wait_send()
    for out in (gx_out, gct_out, gpt_out, gwt_out):
        out.wait()


def store_pair(*refs):
    srcs, dsts, held, ins, outs = refs[:4], refs[4:8], refs[8:12], refs[12], refs[13]
    loads = [pltpu.make_async_copy(srcs[i], held[i], ins.at[i]) for i in range(4)]
    stores = [pltpu.make_async_copy(held[i], dsts[i], outs.at[i]) for i in range(4)]
    for i in (3, 0, 2, 1):
        loads[i].start()
    for i in (3, 0, 2, 1):
        loads[i].wait()
        stores[i].start()
    for store in stores:
        store.wait()


def pair_device(layer_in, inner_act, readout, w_in, a_log, dt_bias, d_skip, grad_out):
    tokens, x, ct, g = layer_in[0], inner_act[0], readout[0].T, grad_out[0]
    t, inner = x.shape
    rows, cols = w_in.shape
    heads = a_log.shape[0]
    width = inner // heads
    groups, gh = inner // LANES, LANES // width
    cb = cols // 2
    vm = pltpu.VMEM
    scratch = [
        vm((2 * t, tokens.shape[1]), BF16),
        vm((t, inner), BF16),
        vm((t, inner), BF16),
        vm((t, inner), BF16),
        vm((STATE, t), BF16),
        vm((cols, rows), BF16),
        vm((1, heads), F32),
        vm((1, heads), F32),
        vm((1, heads), F32),
        vm((2, 16, WROWS, rows // 2), BF16),
        vm((LANES, inner), BF16),
        vm((groups, gh * t, t), F32),
        vm((groups, gh * t, LANES), BF16),
        vm((t, inner), F32),
        vm((groups, t, gh * t), BF16),
        vm((t, inner), BF16),
        vm((t, inner), F32),
        vm((STATE, inner), BF16),
        vm((STATE, inner), BF16),
        vm((t, inner), BF16),
        vm((t, inner), BF16),
        vm((WROWS, t), F32),
        vm((t, t), F32),
        vm((HROWS, t), F32),
        vm((HROWS, t), F32),
        vm((LANES, LANES), F32),
        vm((2, HROWS, t), BF16),
        vm((HROWS, t), BF16),
        vm((4, WROWS, rows // 2), F32),
        vm((4, 4, WROWS, rows // 2), BF16),
        vm((4, 4, WROWS, rows // 2), BF16),
        vm((4, WROWS, rows // 2), BF16),
        vm((4, WROWS, rows // 2), BF16),
        vm((t, inner), BF16),
        vm((STATE, t), BF16),
        vm((cols, t), BF16),
        vm((cb, rows), F32),
    ]
    dma = pltpu.SemaphoreType.DMA
    scratch += [dma((4,))] * 2 + [dma((16,))] * 2 + [dma((4,))] * 4 + [dma((16,))] * 2 + [dma((4,))] * 2 + [dma((13,))]
    hbm = pl.BlockSpec(memory_space=pltpu.HBM)
    results = pl.pallas_call(
        functools.partial(pair_kernel, (t, rows, heads, width, cols)),
        out_shape=(
            jax.ShapeDtypeStruct((t, inner), BF16),
            jax.ShapeDtypeStruct((STATE, t), BF16),
            jax.ShapeDtypeStruct((cols, t), BF16),
            jax.ShapeDtypeStruct((cb, rows), F32),
        ),
        in_specs=[hbm] * 8,
        out_specs=(hbm,) * 4,
        scratch_shapes=scratch,
        compiler_params=pltpu.CompilerParams(
            collective_id=0, has_side_effects=True, vmem_limit_bytes=VMEM_MAIN),
        name="ssm_backward",
    )(tokens, x, g, ct, w_in.T, a_log[None], dt_bias[None], d_skip[None])
    gx, gct, gpt, gwt = pl.pallas_call(
        store_pair,
        out_shape=tuple(jax.ShapeDtypeStruct(r.shape, r.dtype) for r in results),
        in_specs=[hbm] * 4,
        out_specs=(hbm,) * 4,
        scratch_shapes=[vm(r.shape, r.dtype) for r in results] + [dma((4,))] * 2,
        compiler_params=pltpu.CompilerParams(vmem_limit_bytes=VMEM_STORE),
        name="store_results",
    )(*results)
    return (gx[None], gct.T[None], gpt.T[None], gwt.T)


def solution(mesh):
    in_specs = (
        P("dp", "ctx", None),
        P("dp", "ctx", None),
        P("dp", "ctx", None),
        P("dp", None),
        P(),
        P(),
        P(),
        P("dp", "ctx", None),
    )
    out_specs = (P("dp", "ctx", None), P("dp", "ctx", None), P("dp", "ctx", None), P("dp", "ctx"))
    pairs = mesh.shape["dp"] == 16 and mesh.shape["ctx"] == 2
    return jax.shard_map(
        pair_device if pairs else per_device, mesh=mesh, in_specs=in_specs, out_specs=out_specs, check_vma=False
    )
```

```python
import functools

import jax
import jax.numpy as jnp
from jax import lax
from jax.experimental import pallas as pl
from jax.experimental.pallas import tpu as pltpu
from jax.sharding import PartitionSpec as P

STATE = 64
LANES = 128
MESH = pl.DeviceIdType.MESH
VMEM_MAIN = 62 * 1024 * 1024
VMEM_STORE = 62 * 1024 * 1024
F32 = jnp.float32
BF16 = jnp.bfloat16


def inner_group(n):
    b = 1
    while b * b < n and n % (2 * b) == 0:
        b *= 2
    return b


def up(n, m):
    return -(-n // m) * m


def dot(a, b):
    return jnp.dot(a, b, preferred_element_type=F32)


def dot_nt(a, b):
    return lax.dot_general(a, b, (((1,), (1,)), ((), ())), preferred_element_type=F32)


def split(v):
    hi = v.astype(BF16)
    return hi, (v - hi.astype(F32)).astype(BF16)


def dot_split(v, b):
    hi, lo = split(v)
    return dot(hi, b) + dot(lo, b)


def dot_exact(sel, v):
    hi, rest = v.astype(BF16), None
    rest = v - hi.astype(F32)
    mid, low = split(rest)
    return dot(sel, hi) + dot(sel, mid) + dot(sel, low)


def iota(shape, dim):
    return lax.broadcasted_iota(jnp.int32, shape, dim)


def kernel(cfg, tok_h, x_h, g_h, c, w, vec, dexp, gx, gc, gp, gw, tok, x, g, wall, trecv, gall, sloc, crecv,
           dall, spread_m, gather_m, xw, gwt, dx, proj, cum_r, dt_r, cumt, rowt, qacc, ds, part, pst, precv,
           decs, decr, wzs, wzr, wfs, wfr, as_, ar, gzs, gzr, gfs, gfr, cs, cr, ps, pr, es, er, ms, mr, ls):
    n_dp, n_ctx, t, rows, heads, width, cols = cfg
    wide = rows % LANES == 0
    halved = wide and rows % (n_ctx * LANES) == 0 and n_ctx == 2
    half = rows // n_ctx
    n_b = inner_group(n_dp)
    n_a = n_dp // n_b
    my_a, my_b = lax.div(lax.axis_index("dp"), n_b), lax.rem(lax.axis_index("dp"), n_b)
    loads = [pltpu.make_async_copy(src, dst, ls.at[i]) for i, (src, dst) in enumerate(((x_h, x), (g_h, g), (tok_h, tok)))]
    for load in loads:
        load.start()
    groups = x.shape[1] // LANES
    gh = LANES // width
    cb = cols // n_ctx
    cbp = up(cb, 8)
    me = lax.axis_index("dp")
    my = lax.axis_index("ctx")

    def peer(k):
        return lax.rem(me + k, n_dp)

    def mate(k):
        return lax.rem(my + k, n_ctx)

    def col(ref, i):
        return ref.at[:, pl.ds(pl.multiple_of(i * rows, LANES), rows)] if wide else ref.at[i]

    def blk(i):
        return pl.ds(pl.multiple_of(i * t, LANES), t)

    def lanes(q):
        return pl.ds(pl.multiple_of(q * LANES, LANES), LANES)

    barrier = pltpu.get_barrier_semaphore()

    def greet(k, carry):
        pl.semaphore_signal(barrier, inc=1, device_id=(peer(k), my), device_id_type=MESH)
        return carry

    def greet_mate(k, carry):
        pl.semaphore_signal(barrier, inc=1, device_id=(me, mate(k)), device_id_type=MESH)
        return carry

    lax.fori_loop(1, n_dp, greet, 0)
    lax.fori_loop(1, n_ctx, greet_mate, 0)
    pl.semaphore_wait(barrier, n_dp + n_ctx - 2)

    def origin(ka, kb):
        return lax.rem(my_a + n_a - ka, n_a) * n_b + lax.rem(my_b + n_b - kb, n_b)

    def w_slot(i):
        if halved:
            return wall.at[my, :, pl.ds(pl.multiple_of(i * half, LANES), half)]
        return col(wall, i)

    def g_slot(i):
        return gall.at[:, blk(i)]

    def far(slot, send, recv, ka):
        return pltpu.make_async_remote_copy(
            src_ref=slot(me), dst_ref=slot(me), send_sem=send.at[ka], recv_sem=recv.at[ka],
            device_id=(lax.rem(my_a + ka, n_a) * n_b + my_b, my), device_id_type=MESH)

    def near(slot, send, recv, ka, kb):
        i = origin(ka, 0)
        return pltpu.make_async_remote_copy(
            src_ref=slot(i), dst_ref=slot(i), send_sem=send.at[ka * n_b + kb], recv_sem=recv.at[ka * n_b + kb],
            device_id=(my_a * n_b + lax.rem(my_b + kb, n_b), my), device_id_type=MESH)

    def across(ka):
        i = lax.rem(my_a + n_a - ka, n_a) * n_b
        block = wall.at[my, :, pl.ds(pl.multiple_of(i * half, LANES), n_b * half)]
        return pltpu.make_async_remote_copy(
            src_ref=block, dst_ref=block, send_sem=ms.at[ka], recv_sem=mr.at[ka],
            device_id=(me, 1 - my), device_id_type=MESH)

    def a_copy(k):
        return pltpu.make_async_remote_copy(
            src_ref=col(tok, peer(k)), dst_ref=trecv.at[blk(me), :], send_sem=as_.at[k],
            recv_sem=ar.at[k], device_id=(peer(k), my), device_id_type=MESH)

    def c_copy(k):
        other = mate(k)
        which = jnp.where(other > my, 0, 1)
        return pltpu.make_async_remote_copy(
            src_ref=sloc.at[which], dst_ref=crecv.at[my], send_sem=cs.at[k], recv_sem=cr.at[k],
            device_id=(me, other), device_id_type=MESH)

    def d_copy(k):
        return pltpu.make_async_remote_copy(
            src_ref=decs, dst_ref=decr.at[my], send_sem=es.at[k], recv_sem=er.at[k],
            device_id=(me, mate(k)), device_id_type=MESH)

    def p_copy(k):
        return pltpu.make_async_remote_copy(
            src_ref=pst.at[mate(k)], dst_ref=precv.at[my], send_sem=ps.at[k], recv_sem=pr.at[k],
            device_id=(me, mate(k)), device_id_type=MESH)

    def each(n, act):
        def step(k, carry):
            act(k)
            return carry

        lax.fori_loop(1, n, step, 0)

    def spread_near(slot, send, recv, ka):
        each(n_b, lambda kb: near(slot, send, recv, ka, kb).start())

    def first(slot, send, recv, fsend, frecv):
        each(n_a, lambda ka: far(slot, send, recv, ka).start())
        spread_near(slot, fsend, frecv, 0)

    def pass_on(slot, send, recv, fsend, frecv):
        def one(ka):
            far(slot, send, recv, ka).wait_recv()
            spread_near(slot, fsend, frecv, ka)

        each(n_a, one)

    def arrive(slot, fsend, frecv, ka):
        each(n_b, lambda kb: near(slot, fsend, frecv, ka, kb).wait_recv())

    def settle(slot, send, recv, fsend, frecv):
        each(n_a, lambda ka: far(slot, send, recv, ka).wait_send())

        def one(ka, carry):
            each(n_b, lambda kb: near(slot, fsend, frecv, ka, kb).wait_send())
            return carry

        lax.fori_loop(0, n_a, one, 0)

    inner = x.shape[1]
    wcols = w.shape[0]
    if halved:
        wall[my, :, pl.ds(pl.multiple_of(me * half, LANES), half)] = w[:, pl.ds(pl.multiple_of(my * half, LANES), half)]
    elif wide:
        wall[:, pl.ds(pl.multiple_of(me * rows, LANES), rows)] = w[...]
    else:
        wall[me] = w[...]
    first(w_slot, wzs, wzr, wfs, wfr)
    loads[0].wait()
    loads[1].wait()
    loads[2].wait()
    pass_on(w_slot, wzs, wzr, wfs, wfr)
    each(n_dp, lambda k: a_copy(k).start())
    if wide:
        trecv[blk(me), :] = tok[:, pl.ds(pl.multiple_of(me * rows, LANES), rows)]
    else:
        trecv[blk(me), :] = tok[me]
    proj[...] = jnp.zeros_like(proj)
    qacc[...] = jnp.zeros_like(qacc)
    ds[...] = jnp.zeros_like(ds)
    rowt[...] = jnp.zeros_like(rowt)
    spread_m[...] = jnp.where(iota((LANES, inner), 0) == iota((LANES, inner), 1) // width, 1.0, 0.0).astype(BF16)
    gather_m[...] = jnp.where(iota((inner, LANES), 1) == iota((inner, LANES), 0) // width, 1.0, 0.0).astype(BF16)
    head = iota((t, LANES), 1) // width

    def outer(q, carry):
        x4 = x[:, lanes(q)]
        zero = jnp.zeros_like(x4)
        xm = jnp.concatenate([jnp.where(head == j, x4, zero) for j in range(gh)], axis=0)
        dall[q] = dot_nt(xm, g[:, lanes(q)])
        return carry

    lax.fori_loop(0, groups, outer, 0)

    def land(ka, carry):
        arrive(w_slot, wfs, wfr, ka)
        if halved:
            across(ka).start()
        return carry

    lax.fori_loop(0, n_a, land, 0)
    if halved:
        lax.fori_loop(0, n_a, lambda ka, carry: (across(ka).wait_recv(), carry)[1], 0)
        total = None
        for k in range(n_ctx):
            picked = jnp.concatenate(
                [tok[:, i * rows + k * half:i * rows + (k + 1) * half] for i in range(n_dp)], axis=1)
            term = dot_nt(picked, wall[k])
            total = term if total is None else total + term
        proj[:, :wcols] = total
    elif wide:
        proj[:, :wcols] = dot_nt(tok[...], wall[...])
    else:
        def shard(i, carry):
            proj[:, :wcols] += dot_nt(tok[i], wall[i])
            return carry

        lax.fori_loop(0, n_dp, shard, 0)
    rate_scale = -jnp.exp(vec[0:1, :])
    b = proj[:, :STATE].astype(BF16)
    z = proj[:, STATE:STATE + LANES] + vec[1:2, :]
    dt = jnp.maximum(z, 0.0) + jnp.log1p(jnp.exp(-jnp.abs(z)))
    row_i, col_i = iota((t, t), 0), iota((t, t), 1)
    lower = jnp.where(row_i >= col_i, 1.0, 0.0).astype(BF16)
    upper = jnp.where(col_i >= row_i, 1.0, 0.0).astype(BF16)
    cum = dot_exact(lower, rate_scale * dt)
    cum_r[...] = cum
    dt_r[...] = dt
    cumt[...] = cum.T
    last = cum_r[t - 1:t, :]
    to_end = jnp.exp(last - cum)
    wgt = to_end * dt
    grow = jnp.exp(cum)
    w_bf = wgt.astype(BF16)
    e_bf = grow.astype(BF16)
    cv = c[...]
    bt = b.astype(F32).T.astype(BF16)
    ct = cv.astype(F32).T.astype(BF16)

    span = [slice(q * LANES, (q + 1) * LANES) for q in range(groups)]
    for at in span:
        xw[:, at] = (dot(w_bf, spread_m[:, at]) * x[:, at].astype(F32)).astype(BF16)
        gwt[:, at] = (dot(e_bf, spread_m[:, at]) * g[:, at].astype(F32)).astype(BF16)
    sloc[0] = dot(bt, xw[...]).astype(BF16)
    sloc[1] = dot(ct, gwt[...]).astype(BF16)
    each(n_ctx, lambda k: c_copy(k).start())
    if n_ctx > 2:
        decs[...] = jnp.broadcast_to(jnp.exp(last), decs.shape)
        crecv[my] = jnp.zeros(crecv.shape[1:], BF16)
        decr[my] = jnp.zeros(decr.shape[1:], F32)
        each(n_ctx, lambda k: d_copy(k).start())

    scores = dot_nt(b, cv)
    causal = col_i >= row_i

    def mix(q, carry):
        g4 = g[:, lanes(q)]
        shift = lax.rem(LANES - gh * q, LANES)
        cum_s = pltpu.roll(cum_r[...], shift, 1)
        dt_s = pltpu.roll(dt_r[...], shift, 1)
        total = ds[...]
        quot = qacc[...]
        mixed = []
        for j in range(gh):
            h = gh * q + j
            spread = cumt[pl.ds(h, 1), :] - cum_s[:, j:j + 1]
            factor = jnp.exp(jnp.where(causal, spread, -1e30))
            step = dt_s[:, j:j + 1]
            d = dall[q, j * t:(j + 1) * t]
            fs = factor * scores
            mixed.append((fs * step).astype(BF16))
            u = d * fs
            quot = jnp.where(col_i == h, jnp.sum(u, axis=1, keepdims=True), quot)
            rowt[pl.ds(h, 1), :] = jnp.sum(u * step, axis=0, keepdims=True)
            total = total + d * (factor * step)
        ds[...] = total
        qacc[...] = quot
        out = dot(jnp.concatenate(mixed, axis=0), g4)
        acc = dexp[:, lanes(q)] * g4.astype(F32)
        for j in range(gh):
            acc = acc + jnp.where(head == j, out[j * t:(j + 1) * t], 0.0)
        dx[:, lanes(q)] = acc
        return carry

    lax.fori_loop(0, groups, mix, 0)
    each(n_ctx, lambda k: c_copy(k).wait_recv())
    if n_ctx > 2:
        each(n_ctx, lambda k: d_copy(k).wait_recv())

    sv = sg = jnp.zeros((t, LANES), F32)
    db2 = dc2 = jnp.zeros((t, STATE), F32)
    gs = jnp.zeros((8, LANES), F32)
    for at in span:
        e, et = spread_m[:, at], gather_m[at, :]
        if n_ctx == 2:
            got = crecv[1 - my, :, at]
            none = jnp.zeros_like(got)
            s4 = jnp.where(my > 0, got, none)
            g4s = jnp.where(my < 1, got, none)
        else:
            s = jnp.zeros((STATE, LANES), F32)
            k = s
            for i in range(n_ctx):
                dec = dot_split(decr[i], e)[0:1]
                s = jnp.where(i < my, dec * s + crecv[i, :, at].astype(F32), s)
            for i in reversed(range(n_ctx)):
                dec = dot_split(decr[i], e)[0:1]
                k = jnp.where(i > my, dec * k + crecv[i, :, at].astype(F32), k)
            s4, g4s = s.astype(BF16), k.astype(BF16)
            both = jnp.sum(s * k, axis=0, keepdims=True)
            gs = gs + dot_split(jnp.broadcast_to(both, (8, LANES)), et)
        us = dot(cv, s4)
        ug = dot(b, g4s)
        sv = sv + dot_split(x[:, at].astype(F32) * ug, et)
        sg = sg + dot_split(g[:, at].astype(F32) * us, et)
        db2 = db2 + dot_nt(xw[:, at], g4s)
        dc2 = dc2 + dot_nt(gwt[:, at], s4)
        gx[:, at] = (dx[:, at] + dot(w_bf, e) * ug).astype(BF16)
    dsv = ds[...]
    db = dot_split(dsv, cv) + db2
    dc = dot_split(dsv.T, b) + dc2
    gc[...] = dc.astype(BF16)
    quot = qacc[...]
    v = sv
    vw = v * wgt
    dcum = rowt[...].T + grow * sg - dt * quot - vw
    tail = jnp.sum(vw, axis=0, keepdims=True)
    if n_ctx > 2:
        tail = tail + jnp.exp(last) * gs[0:1, :]
    dcum = dcum + jnp.where(row_i == t - 1, tail, 0.0)
    drate = dot_exact(upper, dcum)
    ddt = quot + v * to_end + rate_scale * drate
    dz = ddt / (1.0 + jnp.exp(-z))
    proj[...] = jnp.zeros_like(proj)
    proj[:, :STATE] = db.astype(BF16).astype(F32)
    proj[:, STATE:cols] = dz[:, :heads]
    whole = proj[...]
    gall[:, blk(me)] = whole.T[:wcols].astype(BF16)
    first(g_slot, gzs, gzr, gfs, gfr)
    gp[...] = whole[:, :cols].astype(BF16)
    pass_on(g_slot, gzs, gzr, gfs, gfr)
    each(n_dp, lambda k: a_copy(k).wait_recv())
    lax.fori_loop(0, n_a, lambda ka, carry: (arrive(g_slot, gfs, gfr, ka), carry)[1], 0)
    part[...] = dot(gall[...], trecv[...])
    for o in range(n_ctx):
        pst[o] = part[o * cb:o * cb + cbp, :]
    each(n_ctx, lambda k: p_copy(k).start())
    each(n_ctx, lambda k: p_copy(k).wait_recv())

    def add(k, acc):
        return acc + precv[mate(k)]

    total = lax.fori_loop(1, n_ctx, add, pst[my])
    gw[...] = (total * (1.0 / n_dp)).T[:, :cb]
    settle(w_slot, wzs, wzr, wfs, wfr)
    if halved:
        lax.fori_loop(0, n_a, lambda ka, carry: (across(ka).wait_send(), carry)[1], 0)
    each(n_dp, lambda k: a_copy(k).wait_send())
    settle(g_slot, gzs, gzr, gfs, gfr)
    each(n_ctx, lambda k: c_copy(k).wait_send())
    each(n_ctx, lambda k: p_copy(k).wait_send())
    if n_ctx > 2:
        each(n_ctx, lambda k: d_copy(k).wait_send())


def store(*refs):
    sems = refs[-1]
    copies = [pltpu.make_async_copy(refs[i], refs[4 + i], sems.at[i]) for i in range(4)]
    for copy in copies:
        copy.start()
    for copy in copies:
        copy.wait()


def per_device(layer_in, inner_act, readout, w_in, a_log, dt_bias, d_skip, grad_out):
    n_dp, n_ctx = lax.axis_size("dp"), lax.axis_size("ctx")
    tokens, x, c, g = layer_in[0], inner_act[0], readout[0], grad_out[0]
    t, inner = x.shape
    rows, cols = w_in.shape
    heads = a_log.shape[0]
    width = inner // heads
    wcols = up(cols, 16)
    wide = rows % LANES == 0
    wt = jnp.pad(w_in.T, ((0, wcols - cols), (0, 0)))
    if not wide:
        tokens = jnp.swapaxes(tokens.reshape(t, n_dp, rows), 0, 1)
    vec = jnp.pad(jnp.stack([a_log, dt_bias]), ((0, 6), (0, LANES - heads)))
    dexp = jnp.repeat(d_skip, width)[None]
    cb = cols // n_ctx
    cbp = up(cb, 8)
    vm = pltpu.VMEM
    n_a = n_dp // inner_group(n_dp)
    if not wide:
        wall = (n_dp, wcols, rows)
    elif rows % (n_ctx * LANES) == 0 and n_ctx == 2:
        wall = (n_ctx, wcols, n_dp * rows // n_ctx)
    else:
        wall = (wcols, n_dp * rows)
    scratch = [
        vm(tokens.shape, BF16),
        vm((t, inner), BF16),
        vm((t, inner), BF16),
        vm(wall, BF16),
        vm((n_dp * t, rows), BF16),
        vm((wcols, n_dp * t), BF16),
        vm((2, STATE, inner), BF16),
        vm((n_ctx, STATE, inner), BF16),
        vm((inner // LANES, LANES // width * t, t), F32),
        vm((LANES, inner), BF16),
        vm((inner, LANES), BF16),
        vm((t, inner), BF16),
        vm((t, inner), BF16),
        vm((t, inner), F32),
        vm((t, 2 * LANES), F32),
        vm((t, LANES), F32),
        vm((t, LANES), F32),
        vm((LANES, t), F32),
        vm((LANES, t), F32),
        vm((t, LANES), F32),
        vm((t, t), F32),
        vm((wcols, rows), F32),
        vm((n_ctx, cbp, rows), F32),
        vm((n_ctx, cbp, rows), F32),
        vm((8, LANES), F32),
        vm((n_ctx, 8, LANES), F32),
    ]
    dma = pltpu.SemaphoreType.DMA
    scratch += [dma((n_a,))] * 2 + [dma((n_dp,))] * 4 + [dma((n_a,))] * 2 + [dma((n_dp,))] * 2
    scratch += [dma((n_ctx,))] * 6 + [dma((n_a,))] * 2 + [dma((3,))]
    hbm = pl.BlockSpec(memory_space=pltpu.HBM)
    spec = pl.BlockSpec(memory_space=pltpu.VMEM)
    cfg = (n_dp, n_ctx, t, rows, heads, width, cols)
    results = pl.pallas_call(
        functools.partial(kernel, cfg),
        out_shape=(
            jax.ShapeDtypeStruct((t, inner), BF16),
            jax.ShapeDtypeStruct((t, STATE), BF16),
            jax.ShapeDtypeStruct((t, cols), BF16),
            jax.ShapeDtypeStruct((rows, cb), F32),
        ),
        in_specs=[hbm] * 3 + [spec] * 4,
        out_specs=(spec,) * 4,
        scratch_shapes=scratch,
        compiler_params=pltpu.CompilerParams(
            collective_id=0, has_side_effects=True, vmem_limit_bytes=48 * 1024 * 1024),
        name="ssm_backward",
    )(tokens, x, g, c, wt, vec, dexp)
    gx, gc, gp, gw = pl.pallas_call(
        store,
        out_shape=tuple(jax.ShapeDtypeStruct(r.shape, r.dtype) for r in results),
        in_specs=[spec] * 4,
        out_specs=(hbm,) * 4,
        scratch_shapes=[dma((4,))],
        name="store_results",
    )(*results)
    return (gx[None], gc[None], gp[None], gw)


LOG2E = 1.4426950408889634
HROWS = 80
WROWS = 144


def exact_right(v, sel):
    hi = v.astype(BF16)
    mid, low = split(v - hi.astype(F32))
    return dot(hi, sel) + dot(mid, sel) + dot(low, sel)


def flip(i, k):
    if k == 0:
        return i
    if k == 1:
        return i + 1 - 2 * lax.rem(i, 2)
    if k == 2:
        return i + 2 - 4 * lax.div(i, 2)
    return 3 - i


def pair_kernel(cfg, tok_h, x_h, g_h, ct_h, w_h, alog_h, bias_h, skip_h, gx_h, gct_h, gpt_h, gwt_h,
                tok, x, g, a, ct, wv, alog, bias, skip, wall, spread, dall, gm, dg, mall, ascale, spu, ssend, srecv,
                xy, au, proj, ds, rowt, cst, csr, gph, gpr, pown, psend, precv, qsend, qrecv,
                gx, gct, gpt, gwt,
                wzs, wzr, wps, wpr, xs, xr, ks, kr, rs, rr, zs, zr, ls):
    t, rows, heads, width, cols = cfg
    half = rows // 2
    inner = x.shape[1]
    groups = inner // LANES
    gh = LANES // width
    cb = cols // 2
    me, my = lax.axis_index("dp"), lax.axis_index("ctx")
    za, pb = lax.div(me, 4), lax.rem(me, 4)
    mate = (me, 1 - my)

    def lanes(q, n=LANES):
        return pl.ds(pl.multiple_of(q * n, LANES), n)

    def local(src, dst, i):
        return pltpu.make_async_copy(src, dst, ls.at[i])

    smalls = [local(w_h, wv, 0), local(alog_h, alog, 1), local(bias_h, bias, 2), local(skip_h, skip, 3), local(ct_h, ct, 4)]
    tok_in = local(tok_h, tok.at[pl.ds(0, t)], 5)
    x_in, g_in = local(x_h, x, 6), local(g_h, g, 7)
    for load in smalls:
        load.start()
    tok_in.start()
    x_in.start()
    g_in.start()

    @pl.when(my == 0)
    def _():
        local(x_h, a, 8).start()

    @pl.when(my == 1)
    def _():
        local(g_h, a, 8).start()

    def remote(src, dst, send, recv, to):
        return pltpu.make_async_remote_copy(
            src_ref=src, dst_ref=dst, send_sem=send, recv_sem=recv, device_id=to, device_id_type=MESH)

    def z_peer(k):
        return (flip(za, k) * 4 + pb, my)

    def p_peer(k):
        return (za * 4 + flip(pb, k), my)

    def n_peer(k):
        return (flip(za, 1) * 4 + flip(pb, k), my)

    barrier = pltpu.get_barrier_semaphore()
    for to in [z_peer(k) for k in (3, 2, 1)] + [n_peer(k) for k in (3, 2, 1)] + [p_peer(k) for k in (3, 2, 1)] + [mate]:
        pl.semaphore_signal(barrier, inc=1, device_id=to, device_id_type=MESH)

    smalls[0].wait()
    wfull = jnp.concatenate([wv[...], jnp.zeros((WROWS - cols, rows), BF16)], axis=0)
    wall[my, me] = jnp.where(my == 0, wfull[:, :half], wfull[:, half:])

    pl.semaphore_wait(barrier, 10)

    def w_z(k):
        return remote(wall.at[my, me], wall.at[my, me], wzs.at[k], wzr.at[k], z_peer(k))

    def w_p(kz, kp):
        if kz == 1:
            return remote(wall.at[my, me], wall.at[my, me], wps.at[4 + kp], wpr.at[4 + kp], n_peer(kp))
        slot = wall.at[my, flip(za, kz) * 4 + pb]
        return remote(slot, slot, wps.at[kz * 4 + kp], wpr.at[kz * 4 + kp], p_peer(kp))

    def w_x(kz):
        block = wall.at[my, pl.ds(flip(za, kz) * 4, 4)]
        return remote(block, block, xs.at[kz], xr.at[kz], mate)

    def mate_copy(src, dst, i):
        return remote(src, dst, ks.at[i], kr.at[i], mate)

    for k in (3, 2, 1):
        w_z(k).start()
    for kz in (0, 1):
        for k in (3, 1, 2):
            w_p(kz, k).start()
    tok_in.wait()
    tok_x = mate_copy(tok.at[pl.ds(0, t)], tok.at[pl.ds(t, t)], 0)
    tok_x.start()

    for load in smalls[1:]:
        load.wait()
    spread[...] = jnp.where(iota((LANES, inner), 0) == iota((LANES, inner), 1) // width, 1.0, 0.0).astype(BF16)

    def row(ref):
        return jnp.concatenate([ref[...], jnp.zeros((1, LANES - heads), F32)], axis=1)

    rate_t = -jnp.exp(jnp.broadcast_to(row(alog), (LANES, LANES)).T[:HROWS])
    bias_t = jnp.broadcast_to(row(bias), (LANES, LANES)).T[:HROWS]
    skip_hi, skip_lo = split(jnp.broadcast_to(row(skip), (16, LANES)))
    x_in.wait()
    g_in.wait()
    head = iota((t, LANES), 1) // width

    def outer(q, carry):
        x4, g4 = x[:, lanes(q)], g[:, lanes(q)]
        zero = jnp.zeros_like(x4)
        dall[q] = dot_nt(jnp.concatenate([jnp.where(head == j, x4, zero) for j in range(gh)], axis=0), g4)
        gm[q] = jnp.concatenate([jnp.where(head == j, g4, zero) for j in range(gh)], axis=0)
        e = spread[:, lanes(q)]
        skip4 = (dot(skip_hi, e) + dot(skip_lo, e))[0:1]
        dg[:, lanes(q)] = skip4 * g4.astype(F32)
        return carry

    lax.fori_loop(0, groups, outer, 0)
    ds[...] = jnp.zeros_like(ds)
    rowt[...] = jnp.zeros_like(rowt)
    csr[...] = jnp.zeros_like(csr)
    ctv = ct[...]
    row_i, col_i = iota((t, t), 0), iota((t, t), 1)
    later = jnp.where(col_i >= row_i, 1.0, 0.0).astype(BF16)
    sooner = jnp.where(row_i >= col_i, 1.0, 0.0).astype(BF16)
    first = my == 0

    @pl.when(first)
    def _():
        local(x_h, a, 8).wait()

    @pl.when(my == 1)
    def _():
        local(g_h, a, 8).wait()

    def take(kz, acc):
        w_x(kz).wait_recv()
        base = flip(za, kz) * 4
        for j in range(4):
            block = jnp.concatenate([wall[0, base + j], wall[1, base + j]], axis=1)
            term = dot_nt(block, tok[0:t, lanes(base + j, rows)])
            acc = term if acc is None else acc + term
        return acc

    def landed(kz):
        for kp in (1, 2, 3):
            w_p(kz, kp).wait_recv()
        w_x(kz).start()

    for kz in (1, 2, 3):
        w_z(kz).wait_recv()
        if kz > 1:
            for kp in (3, 1, 2):
                w_p(kz, kp).start()
    acc = None
    for kz in range(4):
        landed(kz)
        if kz > 0:
            acc = take(kz - 1, acc)
    acc = take(3, acc)

    z = acc[STATE:] + bias_t
    bt = acc[:STATE].astype(BF16)
    dt = jnp.maximum(z, 0.0) + jnp.log1p(jnp.exp(-jnp.abs(z)))
    cum = exact_right(rate_t * dt, later)
    csr[0:HROWS] = cum * LOG2E - jnp.log(jnp.maximum(dt, 1e-37)) * LOG2E
    cst[...] = cum * LOG2E
    wgt = jnp.exp(cum[:, t - 1:t] - cum) * dt
    scale_t = jnp.where(first, wgt, jnp.exp(cum))
    scale = jnp.concatenate([scale_t, jnp.zeros((LANES - HROWS, t), F32)], axis=0).T.astype(BF16)
    csr[...] = csr[...].T
    pad = jnp.zeros((LANES - STATE, t), F32)
    b = jnp.concatenate([bt.astype(F32), pad], axis=0).T[:, :STATE].astype(BF16)
    lt = jnp.where(first, bt, ctv)
    left = jnp.concatenate([lt.astype(F32), pad], axis=0).T[:, :STATE].astype(BF16)
    for q in range(groups):
        at = slice(q * LANES, (q + 1) * LANES)
        s4 = dot(scale, spread[:, at])
        spu[:, at] = jnp.where(first, s4, 0.0)
        ascale[:, at] = (s4 * a[:, at].astype(F32)).astype(BF16)
    ssend[...] = dot(lt, ascale[...]).astype(BF16)
    state_x = mate_copy(ssend, srecv, 1)
    state_x.start()

    scores = jnp.where(col_i >= row_i, dot(b, ctv), 0.0)
    dscore_rows = 32

    def mix(q, carry):
        cs = csr[:, gh * q:gh * q + gh]
        tops = [cst[pl.ds(gh * q + j, 1), :] for j in range(gh)]
        sums = [jnp.zeros((8, t), F32) for _ in range(gh)]
        for r in range(t // dscore_rows):
            at = slice(r * dscore_rows, (r + 1) * dscore_rows)
            total = ds[at]
            for j in range(gh):
                e = jnp.exp2(jnp.minimum(tops[j] - cs[at, j:j + 1], 100.0))
                m = e * scores[at]
                d = dall[q, j * t + r * dscore_rows:j * t + (r + 1) * dscore_rows]
                mall[q, at, j * LANES:(j + 1) * LANES] = m.astype(BF16)
                total = total + d * e
                u = d * m
                for i in range(dscore_rows // 8):
                    sums[j] = sums[j] + u[8 * i:8 * i + 8]
            ds[at] = total
        for j in range(gh):
            rowt[pl.ds(gh * q + j, 1), :] = jnp.sum(sums[j], axis=0, keepdims=True)
        return carry

    for q in range(groups):
        mix(q, 0)
    state_x.wait_recv()
    for q in range(groups):
        at = slice(q * LANES, (q + 1) * LANES)
        u = dot(left, srecv[:, at])
        y = dot(mall[q], gm[q]) + spu[:, at] * u
        au[:, at] = (ascale[:, at].astype(F32) * u).astype(BF16)
        xy[:, at] = (x[:, at].astype(F32) * y).astype(BF16)
        gx[:, at] = (y + dg[:, at]).astype(BF16)
    gx_out = local(gx, gx_h, 9)
    gx_out.start()
    sel = spread[:HROWS]
    qt = dot_nt(sel, xy[...])
    zt = dot_nt(sel, au[...])
    d2 = dot_nt(srecv[...], ascale[...])
    dscore = jnp.where(col_i >= row_i, ds[...], 0.0).astype(BF16)
    dbt = dot_nt(ctv, dscore) + jnp.where(first, d2, 0.0)
    dct = dot(bt, dscore) + jnp.where(first, 0.0, d2)
    gct[...] = dct.astype(BF16)
    gct_out = local(gct, gct_h, 10)
    gct_out.start()
    tail = jnp.sum(zt, axis=1, keepdims=True)
    dcum = rowt[...] - qt + jnp.where(first, jnp.where(iota((HROWS, t), 1) == t - 1, tail, 0.0), zt)
    hi, lo = split(dcum)
    drate = dot(hi, sooner) + dot(lo, sooner)
    sig = 1.0 / (1.0 + jnp.exp(-z))
    ratio = jnp.where(dt > 1e-30, sig / jnp.maximum(dt, 1e-30), 1.0)
    dzt = qt * ratio + rate_t * drate * sig
    proj[0:STATE] = dbt
    proj[STATE:] = dzt
    gph[0] = proj[0:HROWS].astype(BF16)
    gph[1] = jnp.concatenate([proj[cb:cols], jnp.zeros((HROWS - cb, t), F32)], axis=0).astype(BF16)
    gp_x = mate_copy(gph.at[1 - my], gpr, 2)
    gp_x.start()
    gpt[...] = proj[0:cols].astype(BF16)
    gpt_out = local(gpt, gpt_h, 11)
    gpt_out.start()

    tok_x.wait_recv()
    gp_x.wait_recv()
    lhs = jnp.concatenate([gph[my], gpr[...]], axis=1)

    def r_p(kz, kp):
        to = p_peer(kp)
        return remote(psend.at[kz, kp], precv.at[kz, kp], rs.at[kz * 4 + kp], rr.at[kz * 4 + kp], to)

    def r_z(kz):
        return remote(qsend.at[kz], qrecv.at[kz], zs.at[kz], zr.at[kz], z_peer(kz))

    def packed(part):
        sides = (part[:, :half], part[:, half:])
        return jnp.concatenate([side[:STATE] for side in sides] + [side[STATE:STATE + 8] for side in sides], axis=0)

    order = (3, 2, 1, 0)
    for kz in order:
        for kp in (3, 1, 2, 0):
            i = flip(za, kz) * 4 + flip(pb, kp)
            part = packed(dot(lhs, tok[:, lanes(i, rows)]))
            if kp == 0:
                pown[kz] = part
            else:
                psend[kz, kp] = part.astype(BF16)
                r_p(kz, kp).start()
    for kz in (3, 2, 1):
        total = pown[kz]
        for kp in (1, 2, 3):
            r_p(kz, kp).wait_recv()
            total = total + precv[kz, kp].astype(F32)
        qsend[kz] = total.astype(BF16)
        r_z(kz).start()
    total = pown[0]
    for kz, kp in [(0, k) for k in (1, 2, 3)]:
        r_p(kz, kp).wait_recv()
        total = total + precv[kz, kp].astype(F32)
    for kz in (3, 2, 1):
        r_z(kz).wait_recv()
        total = total + qrecv[kz].astype(F32)
    total = total * (1.0 / 16)
    at = 2 * STATE
    gwt[0:STATE] = jnp.concatenate([total[:STATE], total[STATE:at]], axis=1)
    gwt[STATE:cb] = jnp.concatenate([total[at:at + 8], total[at + 8:]], axis=1)[:cb - STATE]
    gwt_out = local(gwt, gwt_h, 12)
    gwt_out.start()

    for k in (1, 2, 3):
        w_z(k).wait_send()
        for kz in range(4):
            w_p(kz, k).wait_send()
            r_p(kz, k).wait_send()
    for kz in (3, 2, 1):
        r_z(kz).wait_send()
    for kz in range(4):
        w_x(kz).wait_send()
    tok_x.wait_send()
    state_x.wait_send()
    gp_x.wait_send()
    for out in (gx_out, gct_out, gpt_out, gwt_out):
        out.wait()


def store_pair(*refs):
    srcs, dsts, held, ins, outs = refs[:4], refs[4:8], refs[8:12], refs[12], refs[13]
    loads = [pltpu.make_async_copy(srcs[i], held[i], ins.at[i]) for i in range(4)]
    stores = [pltpu.make_async_copy(held[i], dsts[i], outs.at[i]) for i in range(4)]
    for i in (3, 0, 2, 1):
        loads[i].start()
    for i in (3, 0, 2, 1):
        loads[i].wait()
        stores[i].start()
    for store in stores:
        store.wait()


def pair_device(layer_in, inner_act, readout, w_in, a_log, dt_bias, d_skip, grad_out):
    tokens, x, ct, g = layer_in[0], inner_act[0], readout[0].T, grad_out[0]
    t, inner = x.shape
    rows, cols = w_in.shape
    heads = a_log.shape[0]
    width = inner // heads
    groups, gh = inner // LANES, LANES // width
    cb = cols // 2
    vm = pltpu.VMEM
    scratch = [
        vm((2 * t, tokens.shape[1]), BF16),
        vm((t, inner), BF16),
        vm((t, inner), BF16),
        vm((t, inner), BF16),
        vm((STATE, t), BF16),
        vm((cols, rows), BF16),
        vm((1, heads), F32),
        vm((1, heads), F32),
        vm((1, heads), F32),
        vm((2, 16, WROWS, rows // 2), BF16),
        vm((LANES, inner), BF16),
        vm((groups, gh * t, t), F32),
        vm((groups, gh * t, LANES), BF16),
        vm((t, inner), F32),
        vm((groups, t, gh * t), BF16),
        vm((t, inner), BF16),
        vm((t, inner), F32),
        vm((STATE, inner), BF16),
        vm((STATE, inner), BF16),
        vm((t, inner), BF16),
        vm((t, inner), BF16),
        vm((WROWS, t), F32),
        vm((t, t), F32),
        vm((HROWS, t), F32),
        vm((HROWS, t), F32),
        vm((LANES, LANES), F32),
        vm((2, HROWS, t), BF16),
        vm((HROWS, t), BF16),
        vm((4, WROWS, rows // 2), F32),
        vm((4, 4, WROWS, rows // 2), BF16),
        vm((4, 4, WROWS, rows // 2), BF16),
        vm((4, WROWS, rows // 2), BF16),
        vm((4, WROWS, rows // 2), BF16),
        vm((t, inner), BF16),
        vm((STATE, t), BF16),
        vm((cols, t), BF16),
        vm((cb, rows), F32),
    ]
    dma = pltpu.SemaphoreType.DMA
    scratch += [dma((4,))] * 2 + [dma((16,))] * 2 + [dma((4,))] * 4 + [dma((16,))] * 2 + [dma((4,))] * 2 + [dma((13,))]
    hbm = pl.BlockSpec(memory_space=pltpu.HBM)
    results = pl.pallas_call(
        functools.partial(pair_kernel, (t, rows, heads, width, cols)),
        out_shape=(
            jax.ShapeDtypeStruct((t, inner), BF16),
            jax.ShapeDtypeStruct((STATE, t), BF16),
            jax.ShapeDtypeStruct((cols, t), BF16),
            jax.ShapeDtypeStruct((cb, rows), F32),
        ),
        in_specs=[hbm] * 8,
        out_specs=(hbm,) * 4,
        scratch_shapes=scratch,
        compiler_params=pltpu.CompilerParams(
            collective_id=0, has_side_effects=True, vmem_limit_bytes=VMEM_MAIN),
        name="ssm_backward",
    )(tokens, x, g, ct, w_in.T, a_log[None], dt_bias[None], d_skip[None])
    gx, gct, gpt, gwt = pl.pallas_call(
        store_pair,
        out_shape=tuple(jax.ShapeDtypeStruct(r.shape, r.dtype) for r in results),
        in_specs=[hbm] * 4,
        out_specs=(hbm,) * 4,
        scratch_shapes=[vm(r.shape, r.dtype) for r in results] + [dma((4,))] * 2,
        compiler_params=pltpu.CompilerParams(vmem_limit_bytes=VMEM_STORE),
        name="store_results",
    )(*results)
    return (gx[None], gct.T[None], gpt.T[None], gwt.T)


def solution(mesh):
    in_specs = (
        P("dp", "ctx", None),
        P("dp", "ctx", None),
        P("dp", "ctx", None),
        P("dp", None),
        P(),
        P(),
        P(),
        P("dp", "ctx", None),
    )
    out_specs = (P("dp", "ctx", None), P("dp", "ctx", None), P("dp", "ctx", None), P("dp", "ctx"))
    pairs = mesh.shape["dp"] == 16 and mesh.shape["ctx"] == 2
    return jax.shard_map(
        pair_device if pairs else per_device, mesh=mesh, in_specs=in_specs, out_specs=out_specs, check_vma=False
    )
```

```python
import functools

import jax
import jax.numpy as jnp
from jax import lax
from jax.experimental import pallas as pl
from jax.experimental.pallas import tpu as pltpu
from jax.sharding import PartitionSpec as P

STATE = 64
MOVED = (3, 2)
LANES = 128
MESH = pl.DeviceIdType.MESH
VMEM_MAIN = 62 * 1024 * 1024
VMEM_STORE = 62 * 1024 * 1024
F32 = jnp.float32
BF16 = jnp.bfloat16


def inner_group(n):
    b = 1
    while b * b < n and n % (2 * b) == 0:
        b *= 2
    return b


def up(n, m):
    return -(-n // m) * m


def dot(a, b):
    return jnp.dot(a, b, preferred_element_type=F32)


def dot_nt(a, b):
    return lax.dot_general(a, b, (((1,), (1,)), ((), ())), preferred_element_type=F32)


def split(v):
    hi = v.astype(BF16)
    return hi, (v - hi.astype(F32)).astype(BF16)


def dot_split(v, b):
    hi, lo = split(v)
    return dot(hi, b) + dot(lo, b)


def dot_exact(sel, v):
    hi, rest = v.astype(BF16), None
    rest = v - hi.astype(F32)
    mid, low = split(rest)
    return dot(sel, hi) + dot(sel, mid) + dot(sel, low)


def iota(shape, dim):
    return lax.broadcasted_iota(jnp.int32, shape, dim)


def kernel(cfg, tok_h, x_h, g_h, c, w, vec, dexp, gx, gc, gp, gw, tok, x, g, wall, trecv, gall, sloc, crecv,
           dall, spread_m, gather_m, xw, gwt, dx, proj, cum_r, dt_r, cumt, rowt, qacc, ds, part, pst, precv,
           decs, decr, wzs, wzr, wfs, wfr, as_, ar, gzs, gzr, gfs, gfr, cs, cr, ps, pr, es, er, ms, mr, ls):
    n_dp, n_ctx, t, rows, heads, width, cols = cfg
    wide = rows % LANES == 0
    halved = wide and rows % (n_ctx * LANES) == 0 and n_ctx == 2
    half = rows // n_ctx
    n_b = inner_group(n_dp)
    n_a = n_dp // n_b
    my_a, my_b = lax.div(lax.axis_index("dp"), n_b), lax.rem(lax.axis_index("dp"), n_b)
    loads = [pltpu.make_async_copy(src, dst, ls.at[i]) for i, (src, dst) in enumerate(((x_h, x), (g_h, g), (tok_h, tok)))]
    for load in loads:
        load.start()
    groups = x.shape[1] // LANES
    gh = LANES // width
    cb = cols // n_ctx
    cbp = up(cb, 8)
    me = lax.axis_index("dp")
    my = lax.axis_index("ctx")

    def peer(k):
        return lax.rem(me + k, n_dp)

    def mate(k):
        return lax.rem(my + k, n_ctx)

    def col(ref, i):
        return ref.at[:, pl.ds(pl.multiple_of(i * rows, LANES), rows)] if wide else ref.at[i]

    def blk(i):
        return pl.ds(pl.multiple_of(i * t, LANES), t)

    def lanes(q):
        return pl.ds(pl.multiple_of(q * LANES, LANES), LANES)

    barrier = pltpu.get_barrier_semaphore()

    def greet(k, carry):
        pl.semaphore_signal(barrier, inc=1, device_id=(peer(k), my), device_id_type=MESH)
        return carry

    def greet_mate(k, carry):
        pl.semaphore_signal(barrier, inc=1, device_id=(me, mate(k)), device_id_type=MESH)
        return carry

    lax.fori_loop(1, n_dp, greet, 0)
    lax.fori_loop(1, n_ctx, greet_mate, 0)
    pl.semaphore_wait(barrier, n_dp + n_ctx - 2)

    def origin(ka, kb):
        return lax.rem(my_a + n_a - ka, n_a) * n_b + lax.rem(my_b + n_b - kb, n_b)

    def w_slot(i):
        if halved:
            return wall.at[my, :, pl.ds(pl.multiple_of(i * half, LANES), half)]
        return col(wall, i)

    def g_slot(i):
        return gall.at[:, blk(i)]

    def far(slot, send, recv, ka):
        return pltpu.make_async_remote_copy(
            src_ref=slot(me), dst_ref=slot(me), send_sem=send.at[ka], recv_sem=recv.at[ka],
            device_id=(lax.rem(my_a + ka, n_a) * n_b + my_b, my), device_id_type=MESH)

    def near(slot, send, recv, ka, kb):
        i = origin(ka, 0)
        return pltpu.make_async_remote_copy(
            src_ref=slot(i), dst_ref=slot(i), send_sem=send.at[ka * n_b + kb], recv_sem=recv.at[ka * n_b + kb],
            device_id=(my_a * n_b + lax.rem(my_b + kb, n_b), my), device_id_type=MESH)

    def across(ka):
        i = lax.rem(my_a + n_a - ka, n_a) * n_b
        block = wall.at[my, :, pl.ds(pl.multiple_of(i * half, LANES), n_b * half)]
        return pltpu.make_async_remote_copy(
            src_ref=block, dst_ref=block, send_sem=ms.at[ka], recv_sem=mr.at[ka],
            device_id=(me, 1 - my), device_id_type=MESH)

    def a_copy(k):
        return pltpu.make_async_remote_copy(
            src_ref=col(tok, peer(k)), dst_ref=trecv.at[blk(me), :], send_sem=as_.at[k],
            recv_sem=ar.at[k], device_id=(peer(k), my), device_id_type=MESH)

    def c_copy(k):
        other = mate(k)
        which = jnp.where(other > my, 0, 1)
        return pltpu.make_async_remote_copy(
            src_ref=sloc.at[which], dst_ref=crecv.at[my], send_sem=cs.at[k], recv_sem=cr.at[k],
            device_id=(me, other), device_id_type=MESH)

    def d_copy(k):
        return pltpu.make_async_remote_copy(
            src_ref=decs, dst_ref=decr.at[my], send_sem=es.at[k], recv_sem=er.at[k],
            device_id=(me, mate(k)), device_id_type=MESH)

    def p_copy(k):
        return pltpu.make_async_remote_copy(
            src_ref=pst.at[mate(k)], dst_ref=precv.at[my], send_sem=ps.at[k], recv_sem=pr.at[k],
            device_id=(me, mate(k)), device_id_type=MESH)

    def each(n, act):
        def step(k, carry):
            act(k)
            return carry

        lax.fori_loop(1, n, step, 0)

    def spread_near(slot, send, recv, ka):
        each(n_b, lambda kb: near(slot, send, recv, ka, kb).start())

    def first(slot, send, recv, fsend, frecv):
        each(n_a, lambda ka: far(slot, send, recv, ka).start())
        spread_near(slot, fsend, frecv, 0)

    def pass_on(slot, send, recv, fsend, frecv):
        def one(ka):
            far(slot, send, recv, ka).wait_recv()
            spread_near(slot, fsend, frecv, ka)

        each(n_a, one)

    def arrive(slot, fsend, frecv, ka):
        each(n_b, lambda kb: near(slot, fsend, frecv, ka, kb).wait_recv())

    def settle(slot, send, recv, fsend, frecv):
        each(n_a, lambda ka: far(slot, send, recv, ka).wait_send())

        def one(ka, carry):
            each(n_b, lambda kb: near(slot, fsend, frecv, ka, kb).wait_send())
            return carry

        lax.fori_loop(0, n_a, one, 0)

    inner = x.shape[1]
    wcols = w.shape[0]
    if halved:
        wall[my, :, pl.ds(pl.multiple_of(me * half, LANES), half)] = w[:, pl.ds(pl.multiple_of(my * half, LANES), half)]
    elif wide:
        wall[:, pl.ds(pl.multiple_of(me * rows, LANES), rows)] = w[...]
    else:
        wall[me] = w[...]
    first(w_slot, wzs, wzr, wfs, wfr)
    loads[0].wait()
    loads[1].wait()
    loads[2].wait()
    pass_on(w_slot, wzs, wzr, wfs, wfr)
    each(n_dp, lambda k: a_copy(k).start())
    if wide:
        trecv[blk(me), :] = tok[:, pl.ds(pl.multiple_of(me * rows, LANES), rows)]
    else:
        trecv[blk(me), :] = tok[me]
    proj[...] = jnp.zeros_like(proj)
    qacc[...] = jnp.zeros_like(qacc)
    ds[...] = jnp.zeros_like(ds)
    rowt[...] = jnp.zeros_like(rowt)
    spread_m[...] = jnp.where(iota((LANES, inner), 0) == iota((LANES, inner), 1) // width, 1.0, 0.0).astype(BF16)
    gather_m[...] = jnp.where(iota((inner, LANES), 1) == iota((inner, LANES), 0) // width, 1.0, 0.0).astype(BF16)
    head = iota((t, LANES), 1) // width

    def outer(q, carry):
        x4 = x[:, lanes(q)]
        zero = jnp.zeros_like(x4)
        xm = jnp.concatenate([jnp.where(head == j, x4, zero) for j in range(gh)], axis=0)
        dall[q] = dot_nt(xm, g[:, lanes(q)])
        return carry

    lax.fori_loop(0, groups, outer, 0)

    def land(ka, carry):
        arrive(w_slot, wfs, wfr, ka)
        if halved:
            across(ka).start()
        return carry

    lax.fori_loop(0, n_a, land, 0)
    if halved:
        lax.fori_loop(0, n_a, lambda ka, carry: (across(ka).wait_recv(), carry)[1], 0)
        total = None
        for k in range(n_ctx):
            picked = jnp.concatenate(
                [tok[:, i * rows + k * half:i * rows + (k + 1) * half] for i in range(n_dp)], axis=1)
            term = dot_nt(picked, wall[k])
            total = term if total is None else total + term
        proj[:, :wcols] = total
    elif wide:
        proj[:, :wcols] = dot_nt(tok[...], wall[...])
    else:
        def shard(i, carry):
            proj[:, :wcols] += dot_nt(tok[i], wall[i])
            return carry

        lax.fori_loop(0, n_dp, shard, 0)
    rate_scale = -jnp.exp(vec[0:1, :])
    b = proj[:, :STATE].astype(BF16)
    z = proj[:, STATE:STATE + LANES] + vec[1:2, :]
    dt = jnp.maximum(z, 0.0) + jnp.log1p(jnp.exp(-jnp.abs(z)))
    row_i, col_i = iota((t, t), 0), iota((t, t), 1)
    lower = jnp.where(row_i >= col_i, 1.0, 0.0).astype(BF16)
    upper = jnp.where(col_i >= row_i, 1.0, 0.0).astype(BF16)
    cum = dot_exact(lower, rate_scale * dt)
    cum_r[...] = cum
    dt_r[...] = dt
    cumt[...] = cum.T
    last = cum_r[t - 1:t, :]
    to_end = jnp.exp(last - cum)
    wgt = to_end * dt
    grow = jnp.exp(cum)
    w_bf = wgt.astype(BF16)
    e_bf = grow.astype(BF16)
    cv = c[...]
    bt = b.astype(F32).T.astype(BF16)
    ct = cv.astype(F32).T.astype(BF16)

    span = [slice(q * LANES, (q + 1) * LANES) for q in range(groups)]
    for at in span:
        xw[:, at] = (dot(w_bf, spread_m[:, at]) * x[:, at].astype(F32)).astype(BF16)
        gwt[:, at] = (dot(e_bf, spread_m[:, at]) * g[:, at].astype(F32)).astype(BF16)
    sloc[0] = dot(bt, xw[...]).astype(BF16)
    sloc[1] = dot(ct, gwt[...]).astype(BF16)
    each(n_ctx, lambda k: c_copy(k).start())
    if n_ctx > 2:
        decs[...] = jnp.broadcast_to(jnp.exp(last), decs.shape)
        crecv[my] = jnp.zeros(crecv.shape[1:], BF16)
        decr[my] = jnp.zeros(decr.shape[1:], F32)
        each(n_ctx, lambda k: d_copy(k).start())

    scores = dot_nt(b, cv)
    causal = col_i >= row_i

    def mix(q, carry):
        g4 = g[:, lanes(q)]
        shift = lax.rem(LANES - gh * q, LANES)
        cum_s = pltpu.roll(cum_r[...], shift, 1)
        dt_s = pltpu.roll(dt_r[...], shift, 1)
        total = ds[...]
        quot = qacc[...]
        mixed = []
        for j in range(gh):
            h = gh * q + j
            spread = cumt[pl.ds(h, 1), :] - cum_s[:, j:j + 1]
            factor = jnp.exp(jnp.where(causal, spread, -1e30))
            step = dt_s[:, j:j + 1]
            d = dall[q, j * t:(j + 1) * t]
            fs = factor * scores
            mixed.append((fs * step).astype(BF16))
            u = d * fs
            quot = jnp.where(col_i == h, jnp.sum(u, axis=1, keepdims=True), quot)
            rowt[pl.ds(h, 1), :] = jnp.sum(u * step, axis=0, keepdims=True)
            total = total + d * (factor * step)
        ds[...] = total
        qacc[...] = quot
        out = dot(jnp.concatenate(mixed, axis=0), g4)
        acc = dexp[:, lanes(q)] * g4.astype(F32)
        for j in range(gh):
            acc = acc + jnp.where(head == j, out[j * t:(j + 1) * t], 0.0)
        dx[:, lanes(q)] = acc
        return carry

    lax.fori_loop(0, groups, mix, 0)
    each(n_ctx, lambda k: c_copy(k).wait_recv())
    if n_ctx > 2:
        each(n_ctx, lambda k: d_copy(k).wait_recv())

    sv = sg = jnp.zeros((t, LANES), F32)
    db2 = dc2 = jnp.zeros((t, STATE), F32)
    gs = jnp.zeros((8, LANES), F32)
    for at in span:
        e, et = spread_m[:, at], gather_m[at, :]
        if n_ctx == 2:
            got = crecv[1 - my, :, at]
            none = jnp.zeros_like(got)
            s4 = jnp.where(my > 0, got, none)
            g4s = jnp.where(my < 1, got, none)
        else:
            s = jnp.zeros((STATE, LANES), F32)
            k = s
            for i in range(n_ctx):
                dec = dot_split(decr[i], e)[0:1]
                s = jnp.where(i < my, dec * s + crecv[i, :, at].astype(F32), s)
            for i in reversed(range(n_ctx)):
                dec = dot_split(decr[i], e)[0:1]
                k = jnp.where(i > my, dec * k + crecv[i, :, at].astype(F32), k)
            s4, g4s = s.astype(BF16), k.astype(BF16)
            both = jnp.sum(s * k, axis=0, keepdims=True)
            gs = gs + dot_split(jnp.broadcast_to(both, (8, LANES)), et)
        us = dot(cv, s4)
        ug = dot(b, g4s)
        sv = sv + dot_split(x[:, at].astype(F32) * ug, et)
        sg = sg + dot_split(g[:, at].astype(F32) * us, et)
        db2 = db2 + dot_nt(xw[:, at], g4s)
        dc2 = dc2 + dot_nt(gwt[:, at], s4)
        gx[:, at] = (dx[:, at] + dot(w_bf, e) * ug).astype(BF16)
    dsv = ds[...]
    db = dot_split(dsv, cv) + db2
    dc = dot_split(dsv.T, b) + dc2
    gc[...] = dc.astype(BF16)
    quot = qacc[...]
    v = sv
    vw = v * wgt
    dcum = rowt[...].T + grow * sg - dt * quot - vw
    tail = jnp.sum(vw, axis=0, keepdims=True)
    if n_ctx > 2:
        tail = tail + jnp.exp(last) * gs[0:1, :]
    dcum = dcum + jnp.where(row_i == t - 1, tail, 0.0)
    drate = dot_exact(upper, dcum)
    ddt = quot + v * to_end + rate_scale * drate
    dz = ddt / (1.0 + jnp.exp(-z))
    proj[...] = jnp.zeros_like(proj)
    proj[:, :STATE] = db.astype(BF16).astype(F32)
    proj[:, STATE:cols] = dz[:, :heads]
    whole = proj[...]
    gall[:, blk(me)] = whole.T[:wcols].astype(BF16)
    first(g_slot, gzs, gzr, gfs, gfr)
    gp[...] = whole[:, :cols].astype(BF16)
    pass_on(g_slot, gzs, gzr, gfs, gfr)
    each(n_dp, lambda k: a_copy(k).wait_recv())
    lax.fori_loop(0, n_a, lambda ka, carry: (arrive(g_slot, gfs, gfr, ka), carry)[1], 0)
    part[...] = dot(gall[...], trecv[...])
    for o in range(n_ctx):
        pst[o] = part[o * cb:o * cb + cbp, :]
    each(n_ctx, lambda k: p_copy(k).start())
    each(n_ctx, lambda k: p_copy(k).wait_recv())

    def add(k, acc):
        return acc + precv[mate(k)]

    total = lax.fori_loop(1, n_ctx, add, pst[my])
    gw[...] = (total * (1.0 / n_dp)).T[:, :cb]
    settle(w_slot, wzs, wzr, wfs, wfr)
    if halved:
        lax.fori_loop(0, n_a, lambda ka, carry: (across(ka).wait_send(), carry)[1], 0)
    each(n_dp, lambda k: a_copy(k).wait_send())
    settle(g_slot, gzs, gzr, gfs, gfr)
    each(n_ctx, lambda k: c_copy(k).wait_send())
    each(n_ctx, lambda k: p_copy(k).wait_send())
    if n_ctx > 2:
        each(n_ctx, lambda k: d_copy(k).wait_send())


def store(*refs):
    sems = refs[-1]
    copies = [pltpu.make_async_copy(refs[i], refs[4 + i], sems.at[i]) for i in range(4)]
    for copy in copies:
        copy.start()
    for copy in copies:
        copy.wait()


def per_device(layer_in, inner_act, readout, w_in, a_log, dt_bias, d_skip, grad_out):
    n_dp, n_ctx = lax.axis_size("dp"), lax.axis_size("ctx")
    tokens, x, c, g = layer_in[0], inner_act[0], readout[0], grad_out[0]
    t, inner = x.shape
    rows, cols = w_in.shape
    heads = a_log.shape[0]
    width = inner // heads
    wcols = up(cols, 16)
    wide = rows % LANES == 0
    wt = jnp.pad(w_in.T, ((0, wcols - cols), (0, 0)))
    if not wide:
        tokens = jnp.swapaxes(tokens.reshape(t, n_dp, rows), 0, 1)
    vec = jnp.pad(jnp.stack([a_log, dt_bias]), ((0, 6), (0, LANES - heads)))
    dexp = jnp.repeat(d_skip, width)[None]
    cb = cols // n_ctx
    cbp = up(cb, 8)
    vm = pltpu.VMEM
    n_a = n_dp // inner_group(n_dp)
    if not wide:
        wall = (n_dp, wcols, rows)
    elif rows % (n_ctx * LANES) == 0 and n_ctx == 2:
        wall = (n_ctx, wcols, n_dp * rows // n_ctx)
    else:
        wall = (wcols, n_dp * rows)
    scratch = [
        vm(tokens.shape, BF16),
        vm((t, inner), BF16),
        vm((t, inner), BF16),
        vm(wall, BF16),
        vm((n_dp * t, rows), BF16),
        vm((wcols, n_dp * t), BF16),
        vm((2, STATE, inner), BF16),
        vm((n_ctx, STATE, inner), BF16),
        vm((inner // LANES, LANES // width * t, t), F32),
        vm((LANES, inner), BF16),
        vm((inner, LANES), BF16),
        vm((t, inner), BF16),
        vm((t, inner), BF16),
        vm((t, inner), F32),
        vm((t, 2 * LANES), F32),
        vm((t, LANES), F32),
        vm((t, LANES), F32),
        vm((LANES, t), F32),
        vm((LANES, t), F32),
        vm((t, LANES), F32),
        vm((t, t), F32),
        vm((wcols, rows), F32),
        vm((n_ctx, cbp, rows), F32),
        vm((n_ctx, cbp, rows), F32),
        vm((8, LANES), F32),
        vm((n_ctx, 8, LANES), F32),
    ]
    dma = pltpu.SemaphoreType.DMA
    scratch += [dma((n_a,))] * 2 + [dma((n_dp,))] * 4 + [dma((n_a,))] * 2 + [dma((n_dp,))] * 2
    scratch += [dma((n_ctx,))] * 6 + [dma((n_a,))] * 2 + [dma((3,))]
    hbm = pl.BlockSpec(memory_space=pltpu.HBM)
    spec = pl.BlockSpec(memory_space=pltpu.VMEM)
    cfg = (n_dp, n_ctx, t, rows, heads, width, cols)
    results = pl.pallas_call(
        functools.partial(kernel, cfg),
        out_shape=(
            jax.ShapeDtypeStruct((t, inner), BF16),
            jax.ShapeDtypeStruct((t, STATE), BF16),
            jax.ShapeDtypeStruct((t, cols), BF16),
            jax.ShapeDtypeStruct((rows, cb), F32),
        ),
        in_specs=[hbm] * 3 + [spec] * 4,
        out_specs=(spec,) * 4,
        scratch_shapes=scratch,
        compiler_params=pltpu.CompilerParams(
            collective_id=0, has_side_effects=True, vmem_limit_bytes=48 * 1024 * 1024),
        name="ssm_backward",
    )(tokens, x, g, c, wt, vec, dexp)
    gx, gc, gp, gw = pl.pallas_call(
        store,
        out_shape=tuple(jax.ShapeDtypeStruct(r.shape, r.dtype) for r in results),
        in_specs=[spec] * 4,
        out_specs=(hbm,) * 4,
        scratch_shapes=[dma((4,))],
        name="store_results",
    )(*results)
    return (gx[None], gc[None], gp[None], gw)


LOG2E = 1.4426950408889634
HROWS = 80
WROWS = 144


def exact_right(v, sel):
    hi = v.astype(BF16)
    mid, low = split(v - hi.astype(F32))
    return dot(hi, sel) + dot(mid, sel) + dot(low, sel)


def flip(i, k):
    if k == 0:
        return i
    if k == 1:
        return i + 1 - 2 * lax.rem(i, 2)
    if k == 2:
        return i + 2 - 4 * lax.div(i, 2)
    return 3 - i


def pair_kernel(cfg, tok_h, x_h, g_h, ct_h, w_h, alog_h, bias_h, skip_h, gx_h, gct_h, gpt_h, own_h, qrecv,
                tok, x, g, a, ct, wv, alog, bias, skip, wall, spread, dall, gm, dg, mall, ascale, spu, ssend, srecv,
                xy, au, proj, ds, rowt, cst, csr, gph, gpall, tokp, pown, psend, precv, qsend,
                gx, gct, gpt, own,
                wzs, wzr, wps, wpr, xs, xr, ks, kr, rs, rr, zs, zr, ts, tr, fs, fr, gs, gr, ls):
    t, rows, heads, width, cols = cfg
    half = rows // 2
    inner = x.shape[1]
    groups = inner // LANES
    gh = LANES // width
    cb = cols // 2
    me, my = lax.axis_index("dp"), lax.axis_index("ctx")
    za, pb = lax.div(me, 4), lax.rem(me, 4)
    mate = (me, 1 - my)

    def lanes(q, n=LANES):
        return pl.ds(pl.multiple_of(q * n, LANES), n)

    def local(src, dst, i):
        return pltpu.make_async_copy(src, dst, ls.at[i])

    smalls = [local(w_h, wv, 0), local(alog_h, alog, 1), local(bias_h, bias, 2), local(skip_h, skip, 3), local(ct_h, ct, 4)]
    tok_in = local(tok_h, tok.at[pl.ds(0, t)], 5)
    x_in, g_in = local(x_h, x, 6), local(g_h, g, 7)
    for load in smalls:
        load.start()
    tok_in.start()
    x_in.start()
    g_in.start()

    @pl.when(my == 0)
    def _():
        local(x_h, a, 8).start()

    @pl.when(my == 1)
    def _():
        local(g_h, a, 8).start()

    def remote(src, dst, send, recv, to):
        return pltpu.make_async_remote_copy(
            src_ref=src, dst_ref=dst, send_sem=send, recv_sem=recv, device_id=to, device_id_type=MESH)

    def z_peer(k):
        return (flip(za, k) * 4 + pb, my)

    def p_peer(k):
        return (za * 4 + flip(pb, k), my)

    def c_peer(k):
        return (za * 4 + flip(pb, k), 1 - my)

    def n_peer(k):
        return (flip(za, 1) * 4 + flip(pb, k), my)

    barrier = pltpu.get_barrier_semaphore()
    for to in [z_peer(k) for k in (3, 2, 1)] + [n_peer(k) for k in (3, 2, 1)] + [p_peer(k) for k in (3, 2, 1)] + [c_peer(k) for k in (3, 2, 1)] + [mate]:
        pl.semaphore_signal(barrier, inc=1, device_id=to, device_id_type=MESH)

    smalls[0].wait()
    wfull = jnp.concatenate([wv[...], jnp.zeros((WROWS - cols, rows), BF16)], axis=0)
    wall[my, me] = jnp.where(my == 0, wfull[:, :half], wfull[:, half:])

    pl.semaphore_wait(barrier, 13)

    def w_z(k):
        return remote(wall.at[my, me], wall.at[my, me], wzs.at[k], wzr.at[k], z_peer(k))

    def w_p(kz, kp):
        if kz == 1:
            return remote(wall.at[my, me], wall.at[my, me], wps.at[4 + kp], wpr.at[4 + kp], n_peer(kp))
        slot = wall.at[my, flip(za, kz) * 4 + pb]
        return remote(slot, slot, wps.at[kz * 4 + kp], wpr.at[kz * 4 + kp], p_peer(kp))

    def w_x(kz):
        block = wall.at[my, pl.ds(flip(za, kz) * 4, 4)]
        return remote(block, block, xs.at[kz], xr.at[kz], mate)

    def t_copy(kz, kp):
        i = flip(za, kz) * 4 + flip(pb, kp)
        return remote(tok.at[pl.ds(0, t), lanes(i, rows)], tokp.at[kz - 1, kp, pl.ds(pl.multiple_of(my * t, t), t)],
                      ts.at[kz * 4 + kp], tr.at[kz * 4 + kp], p_peer(kp))

    def f_copy(kz, kp):
        block = tokp.at[kz - 1, kp, pl.ds(pl.multiple_of(my * t, t), t)]
        return remote(block, block, fs.at[kz * 4 + kp], fr.at[kz * 4 + kp], mate)

    def g_copy(k, other):
        to = (mate if k == 0 else c_peer(k)) if other else p_peer(k)
        return remote(gph.at[1 - my if other else my], gpall.at[k, my], gs.at[2 * k + other], gr.at[2 * k + other], to)

    def mate_copy(src, dst, i):
        return remote(src, dst, ks.at[i], kr.at[i], mate)

    for k in (3, 2, 1):
        w_z(k).start()
    for kz in (0, 1):
        for k in (3, 1, 2):
            w_p(kz, k).start()
    tok_in.wait()
    tok_x = mate_copy(tok.at[pl.ds(0, t)], tok.at[pl.ds(t, t)], 0)
    tok_x.start()

    for load in smalls[1:]:
        load.wait()
    spread[...] = jnp.where(iota((LANES, inner), 0) == iota((LANES, inner), 1) // width, 1.0, 0.0).astype(BF16)

    def row(ref):
        return jnp.concatenate([ref[...], jnp.zeros((1, LANES - heads), F32)], axis=1)

    rate_t = -jnp.exp(jnp.broadcast_to(row(alog), (LANES, LANES)).T[:HROWS])
    bias_t = jnp.broadcast_to(row(bias), (LANES, LANES)).T[:HROWS]
    skip_hi, skip_lo = split(jnp.broadcast_to(row(skip), (16, LANES)))
    x_in.wait()
    g_in.wait()
    head = iota((t, LANES), 1) // width

    def outer(q, carry):
        x4, g4 = x[:, lanes(q)], g[:, lanes(q)]
        zero = jnp.zeros_like(x4)
        dall[q] = dot_nt(jnp.concatenate([jnp.where(head == j, x4, zero) for j in range(gh)], axis=0), g4)
        gm[q] = jnp.concatenate([jnp.where(head == j, g4, zero) for j in range(gh)], axis=0)
        e = spread[:, lanes(q)]
        skip4 = (dot(skip_hi, e) + dot(skip_lo, e))[0:1]
        dg[:, lanes(q)] = skip4 * g4.astype(F32)
        return carry

    lax.fori_loop(0, groups, outer, 0)
    ds[...] = jnp.zeros_like(ds)
    rowt[...] = jnp.zeros_like(rowt)
    csr[...] = jnp.zeros_like(csr)
    ctv = ct[...]
    row_i, col_i = iota((t, t), 0), iota((t, t), 1)
    later = jnp.where(col_i >= row_i, 1.0, 0.0).astype(BF16)
    sooner = jnp.where(row_i >= col_i, 1.0, 0.0).astype(BF16)
    first = my == 0

    @pl.when(first)
    def _():
        local(x_h, a, 8).wait()

    @pl.when(my == 1)
    def _():
        local(g_h, a, 8).wait()

    def take(kz, acc):
        w_x(kz).wait_recv()
        base = flip(za, kz) * 4
        for j in range(4):
            block = jnp.concatenate([wall[0, base + j], wall[1, base + j]], axis=1)
            term = dot_nt(block, tok[0:t, lanes(base + j, rows)])
            acc = term if acc is None else acc + term
        return acc

    def landed(kz):
        for kp in (1, 2, 3):
            w_p(kz, kp).wait_recv()
        w_x(kz).start()

    for kz in (1, 2, 3):
        w_z(kz).wait_recv()
        if kz > 1:
            for kp in (3, 1, 2):
                w_p(kz, kp).start()
    acc = None
    for kz in range(4):
        landed(kz)
        if kz > 0:
            acc = take(kz - 1, acc)
    for kz in MOVED:
        for kp in (3, 1, 2):
            t_copy(kz, kp).start()
    acc = take(3, acc)

    z = acc[STATE:] + bias_t
    bt = acc[:STATE].astype(BF16)
    dt = jnp.maximum(z, 0.0) + jnp.log1p(jnp.exp(-jnp.abs(z)))
    cum = exact_right(rate_t * dt, later)
    csr[0:HROWS] = cum * LOG2E - jnp.log(jnp.maximum(dt, 1e-37)) * LOG2E
    cst[...] = cum * LOG2E
    wgt = jnp.exp(cum[:, t - 1:t] - cum) * dt
    scale_t = jnp.where(first, wgt, jnp.exp(cum))
    scale = jnp.concatenate([scale_t, jnp.zeros((LANES - HROWS, t), F32)], axis=0).T.astype(BF16)
    csr[...] = csr[...].T
    pad = jnp.zeros((LANES - STATE, t), F32)
    b = jnp.concatenate([bt.astype(F32), pad], axis=0).T[:, :STATE].astype(BF16)
    lt = jnp.where(first, bt, ctv)
    left = jnp.concatenate([lt.astype(F32), pad], axis=0).T[:, :STATE].astype(BF16)
    for q in range(groups):
        at = slice(q * LANES, (q + 1) * LANES)
        s4 = dot(scale, spread[:, at])
        spu[:, at] = jnp.where(first, s4, 0.0)
        ascale[:, at] = (s4 * a[:, at].astype(F32)).astype(BF16)
    ssend[...] = dot(lt, ascale[...]).astype(BF16)
    state_x = mate_copy(ssend, srecv, 1)
    state_x.start()

    scores = jnp.where(col_i >= row_i, dot(b, ctv), 0.0)
    dscore_rows = 32

    def mix(q, carry):
        cs = csr[:, gh * q:gh * q + gh]
        tops = [cst[pl.ds(gh * q + j, 1), :] for j in range(gh)]
        sums = [jnp.zeros((8, t), F32) for _ in range(gh)]
        for r in range(t // dscore_rows):
            at = slice(r * dscore_rows, (r + 1) * dscore_rows)
            total = ds[at]
            for j in range(gh):
                e = jnp.exp2(jnp.minimum(tops[j] - cs[at, j:j + 1], 100.0))
                m = e * scores[at]
                d = dall[q, j * t + r * dscore_rows:j * t + (r + 1) * dscore_rows]
                mall[q, at, j * LANES:(j + 1) * LANES] = m.astype(BF16)
                total = total + d * e
                u = d * m
                for i in range(dscore_rows // 8):
                    sums[j] = sums[j] + u[8 * i:8 * i + 8]
            ds[at] = total
        for j in range(gh):
            rowt[pl.ds(gh * q + j, 1), :] = jnp.sum(sums[j], axis=0, keepdims=True)
        return carry

    for q in range(groups):
        mix(q, 0)
    state_x.wait_recv()
    for q in range(groups):
        at = slice(q * LANES, (q + 1) * LANES)
        u = dot(left, srecv[:, at])
        y = dot(mall[q], gm[q]) + spu[:, at] * u
        au[:, at] = (ascale[:, at].astype(F32) * u).astype(BF16)
        xy[:, at] = (x[:, at].astype(F32) * y).astype(BF16)
        gx[:, at] = (y + dg[:, at]).astype(BF16)
    gx_out = local(gx, gx_h, 9)
    gx_out.start()
    sel = spread[:HROWS]
    qt = dot_nt(sel, xy[...])
    zt = dot_nt(sel, au[...])
    d2 = dot_nt(srecv[...], ascale[...])
    dscore = jnp.where(col_i >= row_i, ds[...], 0.0).astype(BF16)
    dbt = dot_nt(ctv, dscore) + jnp.where(first, d2, 0.0)
    dct = dot(bt, dscore) + jnp.where(first, 0.0, d2)
    gct[...] = dct.astype(BF16)
    gct_out = local(gct, gct_h, 10)
    gct_out.start()
    tail = jnp.sum(zt, axis=1, keepdims=True)
    dcum = rowt[...] - qt + jnp.where(first, jnp.where(iota((HROWS, t), 1) == t - 1, tail, 0.0), zt)
    hi, lo = split(dcum)
    drate = dot(hi, sooner) + dot(lo, sooner)
    sig = 1.0 / (1.0 + jnp.exp(-z))
    ratio = jnp.where(dt > 1e-30, sig / jnp.maximum(dt, 1e-30), 1.0)
    dzt = qt * ratio + rate_t * drate * sig
    proj[0:STATE] = dbt
    proj[STATE:] = dzt
    gph[0] = proj[0:HROWS].astype(BF16)
    gph[1] = jnp.concatenate([proj[cb:cols], jnp.zeros((HROWS - cb, t), F32)], axis=0).astype(BF16)
    g_copy(0, 1).start()
    for k in (3, 1, 2):
        g_copy(k, 0).start()
        g_copy(k, 1).start()
    gpt[...] = proj[0:cols].astype(BF16)
    gpt_out = local(gpt, gpt_h, 11)
    gpt_out.start()

    for kz in MOVED:
        for kp in (3, 1, 2):
            t_copy(kz, kp).wait_recv()
            f_copy(kz, kp).start()
    tok_x.wait_recv()
    g_copy(0, 1).wait_recv()
    lhs = jnp.concatenate([gph[my], gpall[0, 1 - my]], axis=1)

    def r_p(kz, kp):
        to = n_peer(kp) if kz == 1 else p_peer(kp)
        return remote(psend.at[kz, kp], precv.at[kz, kp], rs.at[kz * 4 + kp], rr.at[kz * 4 + kp], to)

    def r_z(kz):
        return remote(qsend.at[kz], qrecv.at[kz - 2], zs.at[kz], zr.at[kz], z_peer(kz))

    def packed(part):
        sides = (part[:, :half], part[:, half:])
        return jnp.concatenate([side[:STATE] for side in sides] + [side[STATE:STATE + 8] for side in sides], axis=0)

    def block(kz, kp):
        return dot(lhs, tok[:, lanes(flip(za, kz) * 4 + flip(pb, kp), rows)])

    summed = [kz for kz in (1, 2, 3) if kz not in MOVED] + [0]
    for kz in summed:
        for kp in (3, 1, 2) + ((0,) if kz else ()):
            psend[kz, kp] = packed(block(kz, kp)).astype(BF16)
            r_p(kz, kp).start()
    for kz in (3, 2, 0):
        pown[kz] = packed(block(kz, 0))
    for kz in MOVED:
        for kp in (3, 1, 2):
            f_copy(kz, kp).wait_recv()
    for k in (1, 2, 3):
        g_copy(k, 0).wait_recv()
        g_copy(k, 1).wait_recv()
    sides = [jnp.concatenate([gpall[k, 0], gpall[k, 1]], axis=1) for k in (1, 2, 3)]
    for kz in MOVED:
        term = dot(sides[0], tokp[kz - 1, 1]) + dot(sides[1], tokp[kz - 1, 2]) + dot(sides[2], tokp[kz - 1, 3])
        qsend[kz] = (pown[kz] + packed(term)).astype(BF16)
        r_z(kz).start()
    total = pown[0]
    for kz, kp in [(0, k) for k in (1, 2, 3)] + [(1, k) for k in range(4)]:
        r_p(kz, kp).wait_recv()
        total = total + precv[kz, kp].astype(F32)
    own[...] = total
    own_out = local(own, own_h, 12)
    own_out.start()

    for k in (1, 2, 3):
        w_z(k).wait_send()
        g_copy(k, 0).wait_send()
        g_copy(k, 1).wait_send()
        for kz in range(4):
            w_p(kz, k).wait_send()
        for kz in summed:
            r_p(kz, k).wait_send()
        for kz in MOVED:
            t_copy(kz, k).wait_send()
            f_copy(kz, k).wait_send()
    r_p(1, 0).wait_send()
    for kz in (3, 2):
        r_z(kz).wait_send()
    for kz in range(4):
        w_x(kz).wait_send()
    tok_x.wait_send()
    state_x.wait_send()
    g_copy(0, 1).wait_send()
    for out in (gx_out, gct_out, gpt_out, own_out):
        out.wait()
    for kz in (3, 2):
        r_z(kz).wait_recv()


def store_pair(*refs):
    (gx, gct, gpt, own, terms), outs, held, ins, done = refs[:5], refs[5:9], refs[9:15], refs[15], refs[16]
    loads = [pltpu.make_async_copy(src, held[i], ins.at[i]) for i, src in enumerate((own, terms, gx, gct, gpt))]
    for load in loads:
        load.start()
    stores = []
    for i in range(3):
        stores.append(pltpu.make_async_copy(held[2 + i], outs[i], done.at[i]))
    stores.append(pltpu.make_async_copy(held[5], outs[3], done.at[3]))
    loads[0].wait()
    loads[1].wait()
    total = held[0][...]
    for k in range(2):
        total = total + held[1][k].astype(F32)
    total = total * (1.0 / 16)
    at = 2 * STATE
    gwt = held[5]
    gwt[0:STATE] = jnp.concatenate([total[:STATE], total[STATE:at]], axis=1)
    gwt[STATE:] = jnp.concatenate([total[at:at + 8], total[at + 8:]], axis=1)[:gwt.shape[0] - STATE]
    stores[3].start()
    for i in range(3):
        loads[2 + i].wait()
        stores[i].start()
    for store in stores:
        store.wait()


def pair_device(layer_in, inner_act, readout, w_in, a_log, dt_bias, d_skip, grad_out):
    tokens, x, ct, g = layer_in[0], inner_act[0], readout[0].T, grad_out[0]
    t, inner = x.shape
    rows, cols = w_in.shape
    heads = a_log.shape[0]
    width = inner // heads
    groups, gh = inner // LANES, LANES // width
    cb = cols // 2
    vm = pltpu.VMEM
    scratch = [
        vm((2 * t, tokens.shape[1]), BF16),
        vm((t, inner), BF16),
        vm((t, inner), BF16),
        vm((t, inner), BF16),
        vm((STATE, t), BF16),
        vm((cols, rows), BF16),
        vm((1, heads), F32),
        vm((1, heads), F32),
        vm((1, heads), F32),
        vm((2, 16, WROWS, rows // 2), BF16),
        vm((LANES, inner), BF16),
        vm((groups, gh * t, t), F32),
        vm((groups, gh * t, LANES), BF16),
        vm((t, inner), F32),
        vm((groups, t, gh * t), BF16),
        vm((t, inner), BF16),
        vm((t, inner), F32),
        vm((STATE, inner), BF16),
        vm((STATE, inner), BF16),
        vm((t, inner), BF16),
        vm((t, inner), BF16),
        vm((WROWS, t), F32),
        vm((t, t), F32),
        vm((HROWS, t), F32),
        vm((HROWS, t), F32),
        vm((LANES, LANES), F32),
        vm((2, HROWS, t), BF16),
        vm((4, 2, HROWS, t), BF16),
        vm((3, 4, 2 * t, rows), BF16),
        vm((4, WROWS, rows // 2), F32),
        vm((4, 4, WROWS, rows // 2), BF16),
        vm((4, 4, WROWS, rows // 2), BF16),
        vm((4, WROWS, rows // 2), BF16),
        vm((t, inner), BF16),
        vm((STATE, t), BF16),
        vm((cols, t), BF16),
        vm((WROWS, rows // 2), F32),
    ]
    dma = pltpu.SemaphoreType.DMA
    scratch += [dma((4,))] * 2 + [dma((16,))] * 2 + [dma((4,))] * 4 + [dma((16,))] * 2 + [dma((4,))] * 2 + [dma((16,))] * 4 + [dma((8,))] * 2 + [dma((13,))]
    hbm = pl.BlockSpec(memory_space=pltpu.HBM)
    results = pl.pallas_call(
        functools.partial(pair_kernel, (t, rows, heads, width, cols)),
        out_shape=(
            jax.ShapeDtypeStruct((t, inner), BF16),
            jax.ShapeDtypeStruct((STATE, t), BF16),
            jax.ShapeDtypeStruct((cols, t), BF16),
            jax.ShapeDtypeStruct((WROWS, rows // 2), F32),
            jax.ShapeDtypeStruct((2, WROWS, rows // 2), BF16),
        ),
        in_specs=[hbm] * 8,
        out_specs=(hbm,) * 5,
        scratch_shapes=scratch,
        compiler_params=pltpu.CompilerParams(
            collective_id=0, has_side_effects=True, vmem_limit_bytes=VMEM_MAIN),
        name="ssm_backward",
    )(tokens, x, g, ct, w_in.T, a_log[None], dt_bias[None], d_skip[None])
    weight = jax.ShapeDtypeStruct((cb, rows), F32)
    held = [*results[3:], *results[:3], weight]
    gx, gct, gpt, gwt = pl.pallas_call(
        store_pair,
        out_shape=tuple(jax.ShapeDtypeStruct(r.shape, r.dtype) for r in results[:3]) + (weight,),
        in_specs=[hbm] * 5,
        out_specs=(hbm,) * 4,
        scratch_shapes=[vm(r.shape, r.dtype) for r in held] + [dma((5,)), dma((4,))],
        compiler_params=pltpu.CompilerParams(vmem_limit_bytes=VMEM_STORE),
        name="store_results",
    )(*results)
    return (gx[None], gct.T[None], gpt.T[None], gwt.T)


def solution(mesh):
    in_specs = (
        P("dp", "ctx", None),
        P("dp", "ctx", None),
        P("dp", "ctx", None),
        P("dp", None),
        P(),
        P(),
        P(),
        P("dp", "ctx", None),
    )
    out_specs = (P("dp", "ctx", None), P("dp", "ctx", None), P("dp", "ctx", None), P("dp", "ctx"))
    pairs = mesh.shape["dp"] == 16 and mesh.shape["ctx"] == 2
    return jax.shard_map(
        pair_device if pairs else per_device, mesh=mesh, in_specs=in_specs, out_specs=out_specs, check_vma=False
    )
```

```python
import functools

import jax
import jax.numpy as jnp
from jax import lax
from jax.experimental import pallas as pl
from jax.experimental.pallas import tpu as pltpu
from jax.sharding import PartitionSpec as P

STATE = 64
MOVED = (2, 3)
LANES = 128
MESH = pl.DeviceIdType.MESH
VMEM_MAIN = 62 * 1024 * 1024
VMEM_STORE = 62 * 1024 * 1024
F32 = jnp.float32
BF16 = jnp.bfloat16


def inner_group(n):
    b = 1
    while b * b < n and n % (2 * b) == 0:
        b *= 2
    return b


def up(n, m):
    return -(-n // m) * m


def dot(a, b):
    return jnp.dot(a, b, preferred_element_type=F32)


def dot_nt(a, b):
    return lax.dot_general(a, b, (((1,), (1,)), ((), ())), preferred_element_type=F32)


def split(v):
    hi = v.astype(BF16)
    return hi, (v - hi.astype(F32)).astype(BF16)


def dot_split(v, b):
    hi, lo = split(v)
    return dot(hi, b) + dot(lo, b)


def dot_exact(sel, v):
    hi, rest = v.astype(BF16), None
    rest = v - hi.astype(F32)
    mid, low = split(rest)
    return dot(sel, hi) + dot(sel, mid) + dot(sel, low)


def iota(shape, dim):
    return lax.broadcasted_iota(jnp.int32, shape, dim)


def kernel(cfg, tok_h, x_h, g_h, c, w, vec, dexp, gx, gc, gp, gw, tok, x, g, wall, trecv, gall, sloc, crecv,
           dall, spread_m, gather_m, xw, gwt, dx, proj, cum_r, dt_r, cumt, rowt, qacc, ds, part, pst, precv,
           decs, decr, wzs, wzr, wfs, wfr, as_, ar, gzs, gzr, gfs, gfr, cs, cr, ps, pr, es, er, ms, mr, ls):
    n_dp, n_ctx, t, rows, heads, width, cols = cfg
    wide = rows % LANES == 0
    halved = wide and rows % (n_ctx * LANES) == 0 and n_ctx == 2
    half = rows // n_ctx
    n_b = inner_group(n_dp)
    n_a = n_dp // n_b
    my_a, my_b = lax.div(lax.axis_index("dp"), n_b), lax.rem(lax.axis_index("dp"), n_b)
    loads = [pltpu.make_async_copy(src, dst, ls.at[i]) for i, (src, dst) in enumerate(((x_h, x), (g_h, g), (tok_h, tok)))]
    for load in loads:
        load.start()
    groups = x.shape[1] // LANES
    gh = LANES // width
    cb = cols // n_ctx
    cbp = up(cb, 8)
    me = lax.axis_index("dp")
    my = lax.axis_index("ctx")

    def peer(k):
        return lax.rem(me + k, n_dp)

    def mate(k):
        return lax.rem(my + k, n_ctx)

    def col(ref, i):
        return ref.at[:, pl.ds(pl.multiple_of(i * rows, LANES), rows)] if wide else ref.at[i]

    def blk(i):
        return pl.ds(pl.multiple_of(i * t, LANES), t)

    def lanes(q):
        return pl.ds(pl.multiple_of(q * LANES, LANES), LANES)

    barrier = pltpu.get_barrier_semaphore()

    def greet(k, carry):
        pl.semaphore_signal(barrier, inc=1, device_id=(peer(k), my), device_id_type=MESH)
        return carry

    def greet_mate(k, carry):
        pl.semaphore_signal(barrier, inc=1, device_id=(me, mate(k)), device_id_type=MESH)
        return carry

    lax.fori_loop(1, n_dp, greet, 0)
    lax.fori_loop(1, n_ctx, greet_mate, 0)
    pl.semaphore_wait(barrier, n_dp + n_ctx - 2)

    def origin(ka, kb):
        return lax.rem(my_a + n_a - ka, n_a) * n_b + lax.rem(my_b + n_b - kb, n_b)

    def w_slot(i):
        if halved:
            return wall.at[my, :, pl.ds(pl.multiple_of(i * half, LANES), half)]
        return col(wall, i)

    def g_slot(i):
        return gall.at[:, blk(i)]

    def far(slot, send, recv, ka):
        return pltpu.make_async_remote_copy(
            src_ref=slot(me), dst_ref=slot(me), send_sem=send.at[ka], recv_sem=recv.at[ka],
            device_id=(lax.rem(my_a + ka, n_a) * n_b + my_b, my), device_id_type=MESH)

    def near(slot, send, recv, ka, kb):
        i = origin(ka, 0)
        return pltpu.make_async_remote_copy(
            src_ref=slot(i), dst_ref=slot(i), send_sem=send.at[ka * n_b + kb], recv_sem=recv.at[ka * n_b + kb],
            device_id=(my_a * n_b + lax.rem(my_b + kb, n_b), my), device_id_type=MESH)

    def across(ka):
        i = lax.rem(my_a + n_a - ka, n_a) * n_b
        block = wall.at[my, :, pl.ds(pl.multiple_of(i * half, LANES), n_b * half)]
        return pltpu.make_async_remote_copy(
            src_ref=block, dst_ref=block, send_sem=ms.at[ka], recv_sem=mr.at[ka],
            device_id=(me, 1 - my), device_id_type=MESH)

    def a_copy(k):
        return pltpu.make_async_remote_copy(
            src_ref=col(tok, peer(k)), dst_ref=trecv.at[blk(me), :], send_sem=as_.at[k],
            recv_sem=ar.at[k], device_id=(peer(k), my), device_id_type=MESH)

    def c_copy(k):
        other = mate(k)
        which = jnp.where(other > my, 0, 1)
        return pltpu.make_async_remote_copy(
            src_ref=sloc.at[which], dst_ref=crecv.at[my], send_sem=cs.at[k], recv_sem=cr.at[k],
            device_id=(me, other), device_id_type=MESH)

    def d_copy(k):
        return pltpu.make_async_remote_copy(
            src_ref=decs, dst_ref=decr.at[my], send_sem=es.at[k], recv_sem=er.at[k],
            device_id=(me, mate(k)), device_id_type=MESH)

    def p_copy(k):
        return pltpu.make_async_remote_copy(
            src_ref=pst.at[mate(k)], dst_ref=precv.at[my], send_sem=ps.at[k], recv_sem=pr.at[k],
            device_id=(me, mate(k)), device_id_type=MESH)

    def each(n, act):
        def step(k, carry):
            act(k)
            return carry

        lax.fori_loop(1, n, step, 0)

    def spread_near(slot, send, recv, ka):
        each(n_b, lambda kb: near(slot, send, recv, ka, kb).start())

    def first(slot, send, recv, fsend, frecv):
        each(n_a, lambda ka: far(slot, send, recv, ka).start())
        spread_near(slot, fsend, frecv, 0)

    def pass_on(slot, send, recv, fsend, frecv):
        def one(ka):
            far(slot, send, recv, ka).wait_recv()
            spread_near(slot, fsend, frecv, ka)

        each(n_a, one)

    def arrive(slot, fsend, frecv, ka):
        each(n_b, lambda kb: near(slot, fsend, frecv, ka, kb).wait_recv())

    def settle(slot, send, recv, fsend, frecv):
        each(n_a, lambda ka: far(slot, send, recv, ka).wait_send())

        def one(ka, carry):
            each(n_b, lambda kb: near(slot, fsend, frecv, ka, kb).wait_send())
            return carry

        lax.fori_loop(0, n_a, one, 0)

    inner = x.shape[1]
    wcols = w.shape[0]
    if halved:
        wall[my, :, pl.ds(pl.multiple_of(me * half, LANES), half)] = w[:, pl.ds(pl.multiple_of(my * half, LANES), half)]
    elif wide:
        wall[:, pl.ds(pl.multiple_of(me * rows, LANES), rows)] = w[...]
    else:
        wall[me] = w[...]
    first(w_slot, wzs, wzr, wfs, wfr)
    loads[0].wait()
    loads[1].wait()
    loads[2].wait()
    pass_on(w_slot, wzs, wzr, wfs, wfr)
    each(n_dp, lambda k: a_copy(k).start())
    if wide:
        trecv[blk(me), :] = tok[:, pl.ds(pl.multiple_of(me * rows, LANES), rows)]
    else:
        trecv[blk(me), :] = tok[me]
    proj[...] = jnp.zeros_like(proj)
    qacc[...] = jnp.zeros_like(qacc)
    ds[...] = jnp.zeros_like(ds)
    rowt[...] = jnp.zeros_like(rowt)
    spread_m[...] = jnp.where(iota((LANES, inner), 0) == iota((LANES, inner), 1) // width, 1.0, 0.0).astype(BF16)
    gather_m[...] = jnp.where(iota((inner, LANES), 1) == iota((inner, LANES), 0) // width, 1.0, 0.0).astype(BF16)
    head = iota((t, LANES), 1) // width

    def outer(q, carry):
        x4 = x[:, lanes(q)]
        zero = jnp.zeros_like(x4)
        xm = jnp.concatenate([jnp.where(head == j, x4, zero) for j in range(gh)], axis=0)
        dall[q] = dot_nt(xm, g[:, lanes(q)])
        return carry

    lax.fori_loop(0, groups, outer, 0)

    def land(ka, carry):
        arrive(w_slot, wfs, wfr, ka)
        if halved:
            across(ka).start()
        return carry

    lax.fori_loop(0, n_a, land, 0)
    if halved:
        lax.fori_loop(0, n_a, lambda ka, carry: (across(ka).wait_recv(), carry)[1], 0)
        total = None
        for k in range(n_ctx):
            picked = jnp.concatenate(
                [tok[:, i * rows + k * half:i * rows + (k + 1) * half] for i in range(n_dp)], axis=1)
            term = dot_nt(picked, wall[k])
            total = term if total is None else total + term
        proj[:, :wcols] = total
    elif wide:
        proj[:, :wcols] = dot_nt(tok[...], wall[...])
    else:
        def shard(i, carry):
            proj[:, :wcols] += dot_nt(tok[i], wall[i])
            return carry

        lax.fori_loop(0, n_dp, shard, 0)
    rate_scale = -jnp.exp(vec[0:1, :])
    b = proj[:, :STATE].astype(BF16)
    z = proj[:, STATE:STATE + LANES] + vec[1:2, :]
    dt = jnp.maximum(z, 0.0) + jnp.log1p(jnp.exp(-jnp.abs(z)))
    row_i, col_i = iota((t, t), 0), iota((t, t), 1)
    lower = jnp.where(row_i >= col_i, 1.0, 0.0).astype(BF16)
    upper = jnp.where(col_i >= row_i, 1.0, 0.0).astype(BF16)
    cum = dot_exact(lower, rate_scale * dt)
    cum_r[...] = cum
    dt_r[...] = dt
    cumt[...] = cum.T
    last = cum_r[t - 1:t, :]
    to_end = jnp.exp(last - cum)
    wgt = to_end * dt
    grow = jnp.exp(cum)
    w_bf = wgt.astype(BF16)
    e_bf = grow.astype(BF16)
    cv = c[...]
    bt = b.astype(F32).T.astype(BF16)
    ct = cv.astype(F32).T.astype(BF16)

    span = [slice(q * LANES, (q + 1) * LANES) for q in range(groups)]
    for at in span:
        xw[:, at] = (dot(w_bf, spread_m[:, at]) * x[:, at].astype(F32)).astype(BF16)
        gwt[:, at] = (dot(e_bf, spread_m[:, at]) * g[:, at].astype(F32)).astype(BF16)
    sloc[0] = dot(bt, xw[...]).astype(BF16)
    sloc[1] = dot(ct, gwt[...]).astype(BF16)
    each(n_ctx, lambda k: c_copy(k).start())
    if n_ctx > 2:
        decs[...] = jnp.broadcast_to(jnp.exp(last), decs.shape)
        crecv[my] = jnp.zeros(crecv.shape[1:], BF16)
        decr[my] = jnp.zeros(decr.shape[1:], F32)
        each(n_ctx, lambda k: d_copy(k).start())

    scores = dot_nt(b, cv)
    causal = col_i >= row_i

    def mix(q, carry):
        g4 = g[:, lanes(q)]
        shift = lax.rem(LANES - gh * q, LANES)
        cum_s = pltpu.roll(cum_r[...], shift, 1)
        dt_s = pltpu.roll(dt_r[...], shift, 1)
        total = ds[...]
        quot = qacc[...]
        mixed = []
        for j in range(gh):
            h = gh * q + j
            spread = cumt[pl.ds(h, 1), :] - cum_s[:, j:j + 1]
            factor = jnp.exp(jnp.where(causal, spread, -1e30))
            step = dt_s[:, j:j + 1]
            d = dall[q, j * t:(j + 1) * t]
            fs = factor * scores
            mixed.append((fs * step).astype(BF16))
            u = d * fs
            quot = jnp.where(col_i == h, jnp.sum(u, axis=1, keepdims=True), quot)
            rowt[pl.ds(h, 1), :] = jnp.sum(u * step, axis=0, keepdims=True)
            total = total + d * (factor * step)
        ds[...] = total
        qacc[...] = quot
        out = dot(jnp.concatenate(mixed, axis=0), g4)
        acc = dexp[:, lanes(q)] * g4.astype(F32)
        for j in range(gh):
            acc = acc + jnp.where(head == j, out[j * t:(j + 1) * t], 0.0)
        dx[:, lanes(q)] = acc
        return carry

    lax.fori_loop(0, groups, mix, 0)
    each(n_ctx, lambda k: c_copy(k).wait_recv())
    if n_ctx > 2:
        each(n_ctx, lambda k: d_copy(k).wait_recv())

    sv = sg = jnp.zeros((t, LANES), F32)
    db2 = dc2 = jnp.zeros((t, STATE), F32)
    gs = jnp.zeros((8, LANES), F32)
    for at in span:
        e, et = spread_m[:, at], gather_m[at, :]
        if n_ctx == 2:
            got = crecv[1 - my, :, at]
            none = jnp.zeros_like(got)
            s4 = jnp.where(my > 0, got, none)
            g4s = jnp.where(my < 1, got, none)
        else:
            s = jnp.zeros((STATE, LANES), F32)
            k = s
            for i in range(n_ctx):
                dec = dot_split(decr[i], e)[0:1]
                s = jnp.where(i < my, dec * s + crecv[i, :, at].astype(F32), s)
            for i in reversed(range(n_ctx)):
                dec = dot_split(decr[i], e)[0:1]
                k = jnp.where(i > my, dec * k + crecv[i, :, at].astype(F32), k)
            s4, g4s = s.astype(BF16), k.astype(BF16)
            both = jnp.sum(s * k, axis=0, keepdims=True)
            gs = gs + dot_split(jnp.broadcast_to(both, (8, LANES)), et)
        us = dot(cv, s4)
        ug = dot(b, g4s)
        sv = sv + dot_split(x[:, at].astype(F32) * ug, et)
        sg = sg + dot_split(g[:, at].astype(F32) * us, et)
        db2 = db2 + dot_nt(xw[:, at], g4s)
        dc2 = dc2 + dot_nt(gwt[:, at], s4)
        gx[:, at] = (dx[:, at] + dot(w_bf, e) * ug).astype(BF16)
    dsv = ds[...]
    db = dot_split(dsv, cv) + db2
    dc = dot_split(dsv.T, b) + dc2
    gc[...] = dc.astype(BF16)
    quot = qacc[...]
    v = sv
    vw = v * wgt
    dcum = rowt[...].T + grow * sg - dt * quot - vw
    tail = jnp.sum(vw, axis=0, keepdims=True)
    if n_ctx > 2:
        tail = tail + jnp.exp(last) * gs[0:1, :]
    dcum = dcum + jnp.where(row_i == t - 1, tail, 0.0)
    drate = dot_exact(upper, dcum)
    ddt = quot + v * to_end + rate_scale * drate
    dz = ddt / (1.0 + jnp.exp(-z))
    proj[...] = jnp.zeros_like(proj)
    proj[:, :STATE] = db.astype(BF16).astype(F32)
    proj[:, STATE:cols] = dz[:, :heads]
    whole = proj[...]
    gall[:, blk(me)] = whole.T[:wcols].astype(BF16)
    first(g_slot, gzs, gzr, gfs, gfr)
    gp[...] = whole[:, :cols].astype(BF16)
    pass_on(g_slot, gzs, gzr, gfs, gfr)
    each(n_dp, lambda k: a_copy(k).wait_recv())
    lax.fori_loop(0, n_a, lambda ka, carry: (arrive(g_slot, gfs, gfr, ka), carry)[1], 0)
    part[...] = dot(gall[...], trecv[...])
    for o in range(n_ctx):
        pst[o] = part[o * cb:o * cb + cbp, :]
    each(n_ctx, lambda k: p_copy(k).start())
    each(n_ctx, lambda k: p_copy(k).wait_recv())

    def add(k, acc):
        return acc + precv[mate(k)]

    total = lax.fori_loop(1, n_ctx, add, pst[my])
    gw[...] = (total * (1.0 / n_dp)).T[:, :cb]
    settle(w_slot, wzs, wzr, wfs, wfr)
    if halved:
        lax.fori_loop(0, n_a, lambda ka, carry: (across(ka).wait_send(), carry)[1], 0)
    each(n_dp, lambda k: a_copy(k).wait_send())
    settle(g_slot, gzs, gzr, gfs, gfr)
    each(n_ctx, lambda k: c_copy(k).wait_send())
    each(n_ctx, lambda k: p_copy(k).wait_send())
    if n_ctx > 2:
        each(n_ctx, lambda k: d_copy(k).wait_send())


def store(*refs):
    sems = refs[-1]
    copies = [pltpu.make_async_copy(refs[i], refs[4 + i], sems.at[i]) for i in range(4)]
    for copy in copies:
        copy.start()
    for copy in copies:
        copy.wait()


def per_device(layer_in, inner_act, readout, w_in, a_log, dt_bias, d_skip, grad_out):
    n_dp, n_ctx = lax.axis_size("dp"), lax.axis_size("ctx")
    tokens, x, c, g = layer_in[0], inner_act[0], readout[0], grad_out[0]
    t, inner = x.shape
    rows, cols = w_in.shape
    heads = a_log.shape[0]
    width = inner // heads
    wcols = up(cols, 16)
    wide = rows % LANES == 0
    wt = jnp.pad(w_in.T, ((0, wcols - cols), (0, 0)))
    if not wide:
        tokens = jnp.swapaxes(tokens.reshape(t, n_dp, rows), 0, 1)
    vec = jnp.pad(jnp.stack([a_log, dt_bias]), ((0, 6), (0, LANES - heads)))
    dexp = jnp.repeat(d_skip, width)[None]
    cb = cols // n_ctx
    cbp = up(cb, 8)
    vm = pltpu.VMEM
    n_a = n_dp // inner_group(n_dp)
    if not wide:
        wall = (n_dp, wcols, rows)
    elif rows % (n_ctx * LANES) == 0 and n_ctx == 2:
        wall = (n_ctx, wcols, n_dp * rows // n_ctx)
    else:
        wall = (wcols, n_dp * rows)
    scratch = [
        vm(tokens.shape, BF16),
        vm((t, inner), BF16),
        vm((t, inner), BF16),
        vm(wall, BF16),
        vm((n_dp * t, rows), BF16),
        vm((wcols, n_dp * t), BF16),
        vm((2, STATE, inner), BF16),
        vm((n_ctx, STATE, inner), BF16),
        vm((inner // LANES, LANES // width * t, t), F32),
        vm((LANES, inner), BF16),
        vm((inner, LANES), BF16),
        vm((t, inner), BF16),
        vm((t, inner), BF16),
        vm((t, inner), F32),
        vm((t, 2 * LANES), F32),
        vm((t, LANES), F32),
        vm((t, LANES), F32),
        vm((LANES, t), F32),
        vm((LANES, t), F32),
        vm((t, LANES), F32),
        vm((t, t), F32),
        vm((wcols, rows), F32),
        vm((n_ctx, cbp, rows), F32),
        vm((n_ctx, cbp, rows), F32),
        vm((8, LANES), F32),
        vm((n_ctx, 8, LANES), F32),
    ]
    dma = pltpu.SemaphoreType.DMA
    scratch += [dma((n_a,))] * 2 + [dma((n_dp,))] * 4 + [dma((n_a,))] * 2 + [dma((n_dp,))] * 2
    scratch += [dma((n_ctx,))] * 6 + [dma((n_a,))] * 2 + [dma((3,))]
    hbm = pl.BlockSpec(memory_space=pltpu.HBM)
    spec = pl.BlockSpec(memory_space=pltpu.VMEM)
    cfg = (n_dp, n_ctx, t, rows, heads, width, cols)
    results = pl.pallas_call(
        functools.partial(kernel, cfg),
        out_shape=(
            jax.ShapeDtypeStruct((t, inner), BF16),
            jax.ShapeDtypeStruct((t, STATE), BF16),
            jax.ShapeDtypeStruct((t, cols), BF16),
            jax.ShapeDtypeStruct((rows, cb), F32),
        ),
        in_specs=[hbm] * 3 + [spec] * 4,
        out_specs=(spec,) * 4,
        scratch_shapes=scratch,
        compiler_params=pltpu.CompilerParams(
            collective_id=0, has_side_effects=True, vmem_limit_bytes=48 * 1024 * 1024),
        name="ssm_backward",
    )(tokens, x, g, c, wt, vec, dexp)
    gx, gc, gp, gw = pl.pallas_call(
        store,
        out_shape=tuple(jax.ShapeDtypeStruct(r.shape, r.dtype) for r in results),
        in_specs=[spec] * 4,
        out_specs=(hbm,) * 4,
        scratch_shapes=[dma((4,))],
        name="store_results",
    )(*results)
    return (gx[None], gc[None], gp[None], gw)


LOG2E = 1.4426950408889634
HROWS = 80
WROWS = 144


def exact_right(v, sel):
    hi = v.astype(BF16)
    mid, low = split(v - hi.astype(F32))
    return dot(hi, sel) + dot(mid, sel) + dot(low, sel)


def flip(i, k):
    if k == 0:
        return i
    if k == 1:
        return i + 1 - 2 * lax.rem(i, 2)
    if k == 2:
        return i + 2 - 4 * lax.div(i, 2)
    return 3 - i


def pair_kernel(cfg, tok_h, x_h, g_h, ct_h, w_h, alog_h, bias_h, skip_h, gx_h, gct_h, gpt_h, own_h, qrecv,
                tok, x, g, a, ct, wv, alog, bias, skip, wall, spread, dall, gm, dg, mall, ascale, spu, ssend, srecv,
                xy, au, proj, ds, rowt, cst, csr, gph, gpall, tokp, pown, psend, precv, qsend,
                gx, gct, gpt, own,
                wzs, wzr, wps, wpr, xs, xr, ks, kr, rs, rr, zs, zr, ts, tr, fs, fr, gs, gr, es, er, ls):
    t, rows, heads, width, cols = cfg
    half = rows // 2
    inner = x.shape[1]
    groups = inner // LANES
    gh = LANES // width
    cb = cols // 2
    me, my = lax.axis_index("dp"), lax.axis_index("ctx")
    za, pb = lax.div(me, 4), lax.rem(me, 4)
    mate = (me, 1 - my)

    def lanes(q, n=LANES):
        return pl.ds(pl.multiple_of(q * n, LANES), n)

    def local(src, dst, i):
        return pltpu.make_async_copy(src, dst, ls.at[i])

    smalls = [local(w_h, wv, 0), local(alog_h, alog, 1), local(bias_h, bias, 2), local(skip_h, skip, 3), local(ct_h, ct, 4)]
    tok_in = local(tok_h, tok.at[pl.ds(0, t)], 5)
    x_in, g_in = local(x_h, x, 6), local(g_h, g, 7)
    for load in smalls:
        load.start()
    tok_in.start()
    x_in.start()
    g_in.start()

    @pl.when(my == 0)
    def _():
        local(x_h, a, 8).start()

    @pl.when(my == 1)
    def _():
        local(g_h, a, 8).start()

    def remote(src, dst, send, recv, to):
        return pltpu.make_async_remote_copy(
            src_ref=src, dst_ref=dst, send_sem=send, recv_sem=recv, device_id=to, device_id_type=MESH)

    def z_peer(k):
        return (flip(za, k) * 4 + pb, my)

    def p_peer(k):
        return (za * 4 + flip(pb, k), my)

    def c_peer(k):
        return (za * 4 + flip(pb, k), 1 - my)

    def n_peer(k):
        return (flip(za, 1) * 4 + flip(pb, k), my)

    barrier = pltpu.get_barrier_semaphore()
    for to in [z_peer(k) for k in (3, 2, 1)] + [n_peer(k) for k in (3, 2, 1)] + [p_peer(k) for k in (3, 2, 1)] + [c_peer(k) for k in (3, 2, 1)] + [mate]:
        pl.semaphore_signal(barrier, inc=1, device_id=to, device_id_type=MESH)

    smalls[0].wait()
    wfull = jnp.concatenate([wv[...], jnp.zeros((WROWS - cols, rows), BF16)], axis=0)
    wall[my, me] = jnp.where(my == 0, wfull[:, :half], wfull[:, half:])

    pl.semaphore_wait(barrier, 13)

    def w_z(k):
        return remote(wall.at[my, me], wall.at[my, me], wzs.at[k], wzr.at[k], z_peer(k))

    def w_p(kz, kp):
        if kz == 1:
            return remote(wall.at[my, me], wall.at[my, me], wps.at[4 + kp], wpr.at[4 + kp], n_peer(kp))
        slot = wall.at[my, flip(za, kz) * 4 + pb]
        return remote(slot, slot, wps.at[kz * 4 + kp], wpr.at[kz * 4 + kp], p_peer(kp))

    def w_x(kz):
        block = wall.at[my, pl.ds(flip(za, kz) * 4, 4)]
        return remote(block, block, xs.at[kz], xr.at[kz], mate)

    def t_copy(kz, kp):
        i = flip(za, kz) * 4 + flip(pb, kp)
        return remote(tok.at[pl.ds(0, t), lanes(i, rows)], tokp.at[kz - 1, kp, pl.ds(pl.multiple_of(my * t, t), t)],
                      ts.at[kz * 4 + kp], tr.at[kz * 4 + kp], p_peer(kp))

    def f_copy(kz, kp):
        block = tokp.at[kz - 1, kp, pl.ds(pl.multiple_of(my * t, t), t)]
        return remote(block, block, fs.at[kz * 4 + kp], fr.at[kz * 4 + kp], mate)

    def g_copy():
        return remote(gph.at[1 - my], gpall.at[0, my], gs.at[0], gr.at[0], mate)

    def piece(k, c, source, at, send, recv):
        return remote(gph.at[c, at], gpall.at[k, source, at], send, recv.at[2 * k + source], (za * 4 + flip(pb, k), c))

    def early(k, source):
        return piece(k, 0, source, pl.ds(0, STATE), es.at[k], er)

    def late(k, c, source):
        at = pl.ds(0, HROWS) if c else pl.ds(STATE, HROWS - STATE)
        return piece(k, c, source, at, gs.at[2 * k + c], gr)

    def mate_copy(src, dst, i):
        return remote(src, dst, ks.at[i], kr.at[i], mate)

    for k in (3, 2, 1):
        w_z(k).start()
    for kz in (0, 1):
        for k in (3, 1, 2):
            w_p(kz, k).start()
    tok_in.wait()
    tok_x = mate_copy(tok.at[pl.ds(0, t)], tok.at[pl.ds(t, t)], 0)
    tok_x.start()

    for load in smalls[1:]:
        load.wait()
    spread[...] = jnp.where(iota((LANES, inner), 0) == iota((LANES, inner), 1) // width, 1.0, 0.0).astype(BF16)

    def row(ref):
        return jnp.concatenate([ref[...], jnp.zeros((1, LANES - heads), F32)], axis=1)

    rate_t = -jnp.exp(jnp.broadcast_to(row(alog), (LANES, LANES)).T[:HROWS])
    bias_t = jnp.broadcast_to(row(bias), (LANES, LANES)).T[:HROWS]
    skip_hi, skip_lo = split(jnp.broadcast_to(row(skip), (16, LANES)))
    x_in.wait()
    g_in.wait()
    head = iota((t, LANES), 1) // width

    def outer(q, carry):
        x4, g4 = x[:, lanes(q)], g[:, lanes(q)]
        zero = jnp.zeros_like(x4)
        dall[q] = dot_nt(jnp.concatenate([jnp.where(head == j, x4, zero) for j in range(gh)], axis=0), g4)
        gm[q] = jnp.concatenate([jnp.where(head == j, g4, zero) for j in range(gh)], axis=0)
        e = spread[:, lanes(q)]
        skip4 = (dot(skip_hi, e) + dot(skip_lo, e))[0:1]
        dg[:, lanes(q)] = skip4 * g4.astype(F32)
        return carry

    lax.fori_loop(0, groups, outer, 0)
    ds[...] = jnp.zeros_like(ds)
    rowt[...] = jnp.zeros_like(rowt)
    csr[...] = jnp.zeros_like(csr)
    ctv = ct[...]
    row_i, col_i = iota((t, t), 0), iota((t, t), 1)
    later = jnp.where(col_i >= row_i, 1.0, 0.0).astype(BF16)
    sooner = jnp.where(row_i >= col_i, 1.0, 0.0).astype(BF16)
    first = my == 0

    @pl.when(first)
    def _():
        local(x_h, a, 8).wait()

    @pl.when(my == 1)
    def _():
        local(g_h, a, 8).wait()

    def take(kz, acc):
        w_x(kz).wait_recv()
        base = flip(za, kz) * 4
        for j in range(4):
            block = jnp.concatenate([wall[0, base + j], wall[1, base + j]], axis=1)
            term = dot_nt(block, tok[0:t, lanes(base + j, rows)])
            acc = term if acc is None else acc + term
        return acc

    def landed(kz):
        for kp in (1, 2, 3):
            w_p(kz, kp).wait_recv()
        w_x(kz).start()

    for kz in (1, 2, 3):
        w_z(kz).wait_recv()
        if kz > 1:
            for kp in (3, 1, 2):
                w_p(kz, kp).start()
    acc = None
    for kz in range(4):
        if kz == 3:
            for ky in MOVED:
                for kp in (3, 1, 2):
                    t_copy(ky, kp).start()
        landed(kz)
        if kz > 0:
            acc = take(kz - 1, acc)
    acc = take(3, acc)

    z = acc[STATE:] + bias_t
    bt = acc[:STATE].astype(BF16)
    dt = jnp.maximum(z, 0.0) + jnp.log1p(jnp.exp(-jnp.abs(z)))
    cum = exact_right(rate_t * dt, later)
    csr[0:HROWS] = cum * LOG2E - jnp.log(jnp.maximum(dt, 1e-37)) * LOG2E
    cst[...] = cum * LOG2E
    wgt = jnp.exp(cum[:, t - 1:t] - cum) * dt
    scale_t = jnp.where(first, wgt, jnp.exp(cum))
    scale = jnp.concatenate([scale_t, jnp.zeros((LANES - HROWS, t), F32)], axis=0).T.astype(BF16)
    csr[...] = csr[...].T
    pad = jnp.zeros((LANES - STATE, t), F32)
    b = jnp.concatenate([bt.astype(F32), pad], axis=0).T[:, :STATE].astype(BF16)
    lt = jnp.where(first, bt, ctv)
    left = jnp.concatenate([lt.astype(F32), pad], axis=0).T[:, :STATE].astype(BF16)
    for q in range(groups):
        at = slice(q * LANES, (q + 1) * LANES)
        s4 = dot(scale, spread[:, at])
        spu[:, at] = jnp.where(first, s4, 0.0)
        ascale[:, at] = (s4 * a[:, at].astype(F32)).astype(BF16)
    ssend[...] = dot(lt, ascale[...]).astype(BF16)
    state_x = mate_copy(ssend, srecv, 1)
    state_x.start()

    scores = jnp.where(col_i >= row_i, dot(b, ctv), 0.0)
    dscore_rows = 32

    def mix(q, carry):
        cs = csr[:, gh * q:gh * q + gh]
        tops = [cst[pl.ds(gh * q + j, 1), :] for j in range(gh)]
        sums = [jnp.zeros((8, t), F32) for _ in range(gh)]
        for r in range(t // dscore_rows):
            at = slice(r * dscore_rows, (r + 1) * dscore_rows)
            total = ds[at]
            for j in range(gh):
                e = jnp.exp2(jnp.minimum(tops[j] - cs[at, j:j + 1], 100.0))
                m = e * scores[at]
                d = dall[q, j * t + r * dscore_rows:j * t + (r + 1) * dscore_rows]
                mall[q, at, j * LANES:(j + 1) * LANES] = m.astype(BF16)
                total = total + d * e
                u = d * m
                for i in range(dscore_rows // 8):
                    sums[j] = sums[j] + u[8 * i:8 * i + 8]
            ds[at] = total
        for j in range(gh):
            rowt[pl.ds(gh * q + j, 1), :] = jnp.sum(sums[j], axis=0, keepdims=True)
        return carry

    for q in range(groups):
        mix(q, 0)
    state_x.wait_recv()
    d2 = dot_nt(srecv[...], ascale[...])
    dscore = jnp.where(col_i >= row_i, ds[...], 0.0).astype(BF16)
    dbt = dot_nt(ctv, dscore) + jnp.where(first, d2, 0.0)
    dct = dot(bt, dscore) + jnp.where(first, 0.0, d2)
    gph[0, 0:STATE] = dbt.astype(BF16)
    for k in (3, 1, 2):
        early(k, my).start()
    gct[...] = dct.astype(BF16)
    gct_out = local(gct, gct_h, 10)
    gct_out.start()
    for q in range(groups):
        at = slice(q * LANES, (q + 1) * LANES)
        u = dot(left, srecv[:, at])
        y = dot(mall[q], gm[q]) + spu[:, at] * u
        au[:, at] = (ascale[:, at].astype(F32) * u).astype(BF16)
        xy[:, at] = (x[:, at].astype(F32) * y).astype(BF16)
        gx[:, at] = (y + dg[:, at]).astype(BF16)
    gx_out = local(gx, gx_h, 9)
    gx_out.start()
    sel = spread[:HROWS]
    qt = dot_nt(sel, xy[...])
    zt = dot_nt(sel, au[...])
    tail = jnp.sum(zt, axis=1, keepdims=True)
    dcum = rowt[...] - qt + jnp.where(first, jnp.where(iota((HROWS, t), 1) == t - 1, tail, 0.0), zt)
    hi, lo = split(dcum)
    drate = dot(hi, sooner) + dot(lo, sooner)
    sig = 1.0 / (1.0 + jnp.exp(-z))
    ratio = jnp.where(dt > 1e-30, sig / jnp.maximum(dt, 1e-30), 1.0)
    dzt = qt * ratio + rate_t * drate * sig
    proj[0:STATE] = dbt
    proj[STATE:] = dzt
    gph[0, STATE:HROWS] = proj[STATE:HROWS].astype(BF16)
    gph[1] = jnp.concatenate([proj[cb:cols], jnp.zeros((HROWS - cb, t), F32)], axis=0).astype(BF16)
    g_copy().start()
    for k in (3, 1, 2):
        late(k, 1, my).start()
        late(k, 0, my).start()
    gpt[...] = proj[0:cols].astype(BF16)
    gpt_out = local(gpt, gpt_h, 11)
    gpt_out.start()

    for kz in MOVED:
        for kp in (3, 1, 2):
            t_copy(kz, kp).wait_recv()
            f_copy(kz, kp).start()
    tok_x.wait_recv()
    g_copy().wait_recv()
    lhs = jnp.concatenate([gph[my], gpall[0, 1 - my]], axis=1)

    def r_p(kz, kp):
        to = n_peer(kp) if kz == 1 else p_peer(kp)
        return remote(psend.at[kz, kp], precv.at[kz, kp], rs.at[kz * 4 + kp], rr.at[kz * 4 + kp], to)

    def r_z(kz):
        return remote(qsend.at[kz], qrecv.at[kz - 2], zs.at[kz], zr.at[kz], z_peer(kz))

    def packed(part):
        sides = (part[:, :half], part[:, half:])
        return jnp.concatenate([side[:STATE] for side in sides] + [side[STATE:STATE + 8] for side in sides], axis=0)

    def block(kz, kp):
        return dot(lhs, tok[:, lanes(flip(za, kz) * 4 + flip(pb, kp), rows)])

    summed = [kz for kz in (1, 2, 3) if kz not in MOVED] + [0]
    for kz in summed:
        for kp in (3, 1, 2) + ((0,) if kz else ()):
            psend[kz, kp] = packed(block(kz, kp)).astype(BF16)
            r_p(kz, kp).start()
    for kz in (3, 2, 0):
        pown[kz] = packed(block(kz, 0))
    for kz in MOVED:
        for kp in (3, 1, 2):
            f_copy(kz, kp).wait_recv()

    @pl.when(first)
    def _():
        for k in (1, 2, 3):
            for source in (0, 1):
                early(k, source).wait_recv()
                late(k, 0, source).wait_recv()

    @pl.when(my == 1)
    def _():
        for k in (1, 2, 3):
            for source in (0, 1):
                late(k, 1, source).wait_recv()

    sides = [jnp.concatenate([gpall[k, 0], gpall[k, 1]], axis=1) for k in (1, 2, 3)]
    for kz in MOVED:
        term = dot(sides[0], tokp[kz - 1, 1]) + dot(sides[1], tokp[kz - 1, 2]) + dot(sides[2], tokp[kz - 1, 3])
        qsend[kz] = (pown[kz] + packed(term)).astype(BF16)
        r_z(kz).start()
    total = pown[0]
    for kz, kp in [(0, k) for k in (1, 2, 3)] + [(1, k) for k in range(4)]:
        r_p(kz, kp).wait_recv()
        total = total + precv[kz, kp].astype(F32)
    own[...] = total
    own_out = local(own, own_h, 12)
    own_out.start()

    for k in (1, 2, 3):
        w_z(k).wait_send()
        early(k, my).wait_send()
        late(k, 0, my).wait_send()
        late(k, 1, my).wait_send()
        for kz in range(4):
            w_p(kz, k).wait_send()
        for kz in summed:
            r_p(kz, k).wait_send()
        for kz in MOVED:
            t_copy(kz, k).wait_send()
            f_copy(kz, k).wait_send()
    r_p(1, 0).wait_send()
    for kz in (3, 2):
        r_z(kz).wait_send()
    for kz in range(4):
        w_x(kz).wait_send()
    tok_x.wait_send()
    state_x.wait_send()
    g_copy().wait_send()
    for out in (gx_out, gct_out, gpt_out, own_out):
        out.wait()
    for kz in (3, 2):
        r_z(kz).wait_recv()


def store_pair(*refs):
    (gx, gct, gpt, own, terms), outs, held, ins, done = refs[:5], refs[5:9], refs[9:15], refs[15], refs[16]
    loads = [pltpu.make_async_copy(src, held[i], ins.at[i]) for i, src in enumerate((own, terms, gx, gct, gpt))]
    for load in loads:
        load.start()
    stores = []
    for i in range(3):
        stores.append(pltpu.make_async_copy(held[2 + i], outs[i], done.at[i]))
    stores.append(pltpu.make_async_copy(held[5], outs[3], done.at[3]))
    loads[0].wait()
    loads[1].wait()
    total = held[0][...]
    for k in range(2):
        total = total + held[1][k].astype(F32)
    total = total * (1.0 / 16)
    at = 2 * STATE
    gwt = held[5]
    gwt[0:STATE] = jnp.concatenate([total[:STATE], total[STATE:at]], axis=1)
    gwt[STATE:] = jnp.concatenate([total[at:at + 8], total[at + 8:]], axis=1)[:gwt.shape[0] - STATE]
    stores[3].start()
    for i in range(3):
        loads[2 + i].wait()
        stores[i].start()
    for store in stores:
        store.wait()


def pair_device(layer_in, inner_act, readout, w_in, a_log, dt_bias, d_skip, grad_out):
    tokens, x, ct, g = layer_in[0], inner_act[0], readout[0].T, grad_out[0]
    t, inner = x.shape
    rows, cols = w_in.shape
    heads = a_log.shape[0]
    width = inner // heads
    groups, gh = inner // LANES, LANES // width
    cb = cols // 2
    vm = pltpu.VMEM
    scratch = [
        vm((2 * t, tokens.shape[1]), BF16),
        vm((t, inner), BF16),
        vm((t, inner), BF16),
        vm((t, inner), BF16),
        vm((STATE, t), BF16),
        vm((cols, rows), BF16),
        vm((1, heads), F32),
        vm((1, heads), F32),
        vm((1, heads), F32),
        vm((2, 16, WROWS, rows // 2), BF16),
        vm((LANES, inner), BF16),
        vm((groups, gh * t, t), F32),
        vm((groups, gh * t, LANES), BF16),
        vm((t, inner), F32),
        vm((groups, t, gh * t), BF16),
        vm((t, inner), BF16),
        vm((t, inner), F32),
        vm((STATE, inner), BF16),
        vm((STATE, inner), BF16),
        vm((t, inner), BF16),
        vm((t, inner), BF16),
        vm((WROWS, t), F32),
        vm((t, t), F32),
        vm((HROWS, t), F32),
        vm((HROWS, t), F32),
        vm((LANES, LANES), F32),
        vm((2, HROWS, t), BF16),
        vm((4, 2, HROWS, t), BF16),
        vm((3, 4, 2 * t, rows), BF16),
        vm((4, WROWS, rows // 2), F32),
        vm((4, 4, WROWS, rows // 2), BF16),
        vm((4, 4, WROWS, rows // 2), BF16),
        vm((4, WROWS, rows // 2), BF16),
        vm((t, inner), BF16),
        vm((STATE, t), BF16),
        vm((cols, t), BF16),
        vm((WROWS, rows // 2), F32),
    ]
    dma = pltpu.SemaphoreType.DMA
    scratch += [dma((4,))] * 2 + [dma((16,))] * 2 + [dma((4,))] * 4 + [dma((16,))] * 2 + [dma((4,))] * 2 + [dma((16,))] * 4 + [dma((8,))] * 4 + [dma((13,))]
    hbm = pl.BlockSpec(memory_space=pltpu.HBM)
    results = pl.pallas_call(
        functools.partial(pair_kernel, (t, rows, heads, width, cols)),
        out_shape=(
            jax.ShapeDtypeStruct((t, inner), BF16),
            jax.ShapeDtypeStruct((STATE, t), BF16),
            jax.ShapeDtypeStruct((cols, t), BF16),
            jax.ShapeDtypeStruct((WROWS, rows // 2), F32),
            jax.ShapeDtypeStruct((2, WROWS, rows // 2), BF16),
        ),
        in_specs=[hbm] * 8,
        out_specs=(hbm,) * 5,
        scratch_shapes=scratch,
        compiler_params=pltpu.CompilerParams(
            collective_id=0, has_side_effects=True, vmem_limit_bytes=VMEM_MAIN),
        name="ssm_backward",
    )(tokens, x, g, ct, w_in.T, a_log[None], dt_bias[None], d_skip[None])
    weight = jax.ShapeDtypeStruct((cb, rows), F32)
    held = [*results[3:], *results[:3], weight]
    gx, gct, gpt, gwt = pl.pallas_call(
        store_pair,
        out_shape=tuple(jax.ShapeDtypeStruct(r.shape, r.dtype) for r in results[:3]) + (weight,),
        in_specs=[hbm] * 5,
        out_specs=(hbm,) * 4,
        scratch_shapes=[vm(r.shape, r.dtype) for r in held] + [dma((5,)), dma((4,))],
        compiler_params=pltpu.CompilerParams(vmem_limit_bytes=VMEM_STORE),
        name="store_results",
    )(*results)
    return (gx[None], gct.T[None], gpt.T[None], gwt.T)


def solution(mesh):
    in_specs = (
        P("dp", "ctx", None),
        P("dp", "ctx", None),
        P("dp", "ctx", None),
        P("dp", None),
        P(),
        P(),
        P(),
        P("dp", "ctx", None),
    )
    out_specs = (P("dp", "ctx", None), P("dp", "ctx", None), P("dp", "ctx", None), P("dp", "ctx"))
    pairs = mesh.shape["dp"] == 16 and mesh.shape["ctx"] == 2
    return jax.shard_map(
        pair_device if pairs else per_device, mesh=mesh, in_specs=in_specs, out_specs=out_specs, check_vma=False
    )
```

```python
import functools

import jax
import jax.numpy as jnp
from jax import lax
from jax.experimental import pallas as pl
from jax.experimental.pallas import tpu as pltpu
from jax.sharding import PartitionSpec as P

STATE = 64
MOVED = (2, 3)
LANES = 128
MESH = pl.DeviceIdType.MESH
VMEM_MAIN = 62 * 1024 * 1024
VMEM_STORE = 62 * 1024 * 1024
F32 = jnp.float32
BF16 = jnp.bfloat16


def inner_group(n):
    b = 1
    while b * b < n and n % (2 * b) == 0:
        b *= 2
    return b


def up(n, m):
    return -(-n // m) * m


def dot(a, b):
    return jnp.dot(a, b, preferred_element_type=F32)


def dot_nt(a, b):
    return lax.dot_general(a, b, (((1,), (1,)), ((), ())), preferred_element_type=F32)


def split(v):
    hi = v.astype(BF16)
    return hi, (v - hi.astype(F32)).astype(BF16)


def dot_split(v, b):
    hi, lo = split(v)
    return dot(hi, b) + dot(lo, b)


def dot_exact(sel, v):
    hi, rest = v.astype(BF16), None
    rest = v - hi.astype(F32)
    mid, low = split(rest)
    return dot(sel, hi) + dot(sel, mid) + dot(sel, low)


def iota(shape, dim):
    return lax.broadcasted_iota(jnp.int32, shape, dim)


def kernel(cfg, tok_h, x_h, g_h, c, w, vec, dexp, gx, gc, gp, gw, tok, x, g, wall, trecv, gall, sloc, crecv,
           dall, spread_m, gather_m, xw, gwt, dx, proj, cum_r, dt_r, cumt, rowt, qacc, ds, part, pst, precv,
           decs, decr, wzs, wzr, wfs, wfr, as_, ar, gzs, gzr, gfs, gfr, cs, cr, ps, pr, es, er, ms, mr, ls):
    n_dp, n_ctx, t, rows, heads, width, cols = cfg
    wide = rows % LANES == 0
    halved = wide and rows % (n_ctx * LANES) == 0 and n_ctx == 2
    half = rows // n_ctx
    n_b = inner_group(n_dp)
    n_a = n_dp // n_b
    my_a, my_b = lax.div(lax.axis_index("dp"), n_b), lax.rem(lax.axis_index("dp"), n_b)
    loads = [pltpu.make_async_copy(src, dst, ls.at[i]) for i, (src, dst) in enumerate(((x_h, x), (g_h, g), (tok_h, tok)))]
    for load in loads:
        load.start()
    groups = x.shape[1] // LANES
    gh = LANES // width
    cb = cols // n_ctx
    cbp = up(cb, 8)
    me = lax.axis_index("dp")
    my = lax.axis_index("ctx")

    def peer(k):
        return lax.rem(me + k, n_dp)

    def mate(k):
        return lax.rem(my + k, n_ctx)

    def col(ref, i):
        return ref.at[:, pl.ds(pl.multiple_of(i * rows, LANES), rows)] if wide else ref.at[i]

    def blk(i):
        return pl.ds(pl.multiple_of(i * t, LANES), t)

    def lanes(q):
        return pl.ds(pl.multiple_of(q * LANES, LANES), LANES)

    barrier = pltpu.get_barrier_semaphore()

    def greet(k, carry):
        pl.semaphore_signal(barrier, inc=1, device_id=(peer(k), my), device_id_type=MESH)
        return carry

    def greet_mate(k, carry):
        pl.semaphore_signal(barrier, inc=1, device_id=(me, mate(k)), device_id_type=MESH)
        return carry

    lax.fori_loop(1, n_dp, greet, 0)
    lax.fori_loop(1, n_ctx, greet_mate, 0)
    pl.semaphore_wait(barrier, n_dp + n_ctx - 2)

    def origin(ka, kb):
        return lax.rem(my_a + n_a - ka, n_a) * n_b + lax.rem(my_b + n_b - kb, n_b)

    def w_slot(i):
        if halved:
            return wall.at[my, :, pl.ds(pl.multiple_of(i * half, LANES), half)]
        return col(wall, i)

    def g_slot(i):
        return gall.at[:, blk(i)]

    def far(slot, send, recv, ka):
        return pltpu.make_async_remote_copy(
            src_ref=slot(me), dst_ref=slot(me), send_sem=send.at[ka], recv_sem=recv.at[ka],
            device_id=(lax.rem(my_a + ka, n_a) * n_b + my_b, my), device_id_type=MESH)

    def near(slot, send, recv, ka, kb):
        i = origin(ka, 0)
        return pltpu.make_async_remote_copy(
            src_ref=slot(i), dst_ref=slot(i), send_sem=send.at[ka * n_b + kb], recv_sem=recv.at[ka * n_b + kb],
            device_id=(my_a * n_b + lax.rem(my_b + kb, n_b), my), device_id_type=MESH)

    def across(ka):
        i = lax.rem(my_a + n_a - ka, n_a) * n_b
        block = wall.at[my, :, pl.ds(pl.multiple_of(i * half, LANES), n_b * half)]
        return pltpu.make_async_remote_copy(
            src_ref=block, dst_ref=block, send_sem=ms.at[ka], recv_sem=mr.at[ka],
            device_id=(me, 1 - my), device_id_type=MESH)

    def a_copy(k):
        return pltpu.make_async_remote_copy(
            src_ref=col(tok, peer(k)), dst_ref=trecv.at[blk(me), :], send_sem=as_.at[k],
            recv_sem=ar.at[k], device_id=(peer(k), my), device_id_type=MESH)

    def c_copy(k):
        other = mate(k)
        which = jnp.where(other > my, 0, 1)
        return pltpu.make_async_remote_copy(
            src_ref=sloc.at[which], dst_ref=crecv.at[my], send_sem=cs.at[k], recv_sem=cr.at[k],
            device_id=(me, other), device_id_type=MESH)

    def d_copy(k):
        return pltpu.make_async_remote_copy(
            src_ref=decs, dst_ref=decr.at[my], send_sem=es.at[k], recv_sem=er.at[k],
            device_id=(me, mate(k)), device_id_type=MESH)

    def p_copy(k):
        return pltpu.make_async_remote_copy(
            src_ref=pst.at[mate(k)], dst_ref=precv.at[my], send_sem=ps.at[k], recv_sem=pr.at[k],
            device_id=(me, mate(k)), device_id_type=MESH)

    def each(n, act):
        def step(k, carry):
            act(k)
            return carry

        lax.fori_loop(1, n, step, 0)

    def spread_near(slot, send, recv, ka):
        each(n_b, lambda kb: near(slot, send, recv, ka, kb).start())

    def first(slot, send, recv, fsend, frecv):
        each(n_a, lambda ka: far(slot, send, recv, ka).start())
        spread_near(slot, fsend, frecv, 0)

    def pass_on(slot, send, recv, fsend, frecv):
        def one(ka):
            far(slot, send, recv, ka).wait_recv()
            spread_near(slot, fsend, frecv, ka)

        each(n_a, one)

    def arrive(slot, fsend, frecv, ka):
        each(n_b, lambda kb: near(slot, fsend, frecv, ka, kb).wait_recv())

    def settle(slot, send, recv, fsend, frecv):
        each(n_a, lambda ka: far(slot, send, recv, ka).wait_send())

        def one(ka, carry):
            each(n_b, lambda kb: near(slot, fsend, frecv, ka, kb).wait_send())
            return carry

        lax.fori_loop(0, n_a, one, 0)

    inner = x.shape[1]
    wcols = w.shape[0]
    if halved:
        wall[my, :, pl.ds(pl.multiple_of(me * half, LANES), half)] = w[:, pl.ds(pl.multiple_of(my * half, LANES), half)]
    elif wide:
        wall[:, pl.ds(pl.multiple_of(me * rows, LANES), rows)] = w[...]
    else:
        wall[me] = w[...]
    first(w_slot, wzs, wzr, wfs, wfr)
    loads[0].wait()
    loads[1].wait()
    loads[2].wait()
    pass_on(w_slot, wzs, wzr, wfs, wfr)
    each(n_dp, lambda k: a_copy(k).start())
    if wide:
        trecv[blk(me), :] = tok[:, pl.ds(pl.multiple_of(me * rows, LANES), rows)]
    else:
        trecv[blk(me), :] = tok[me]
    proj[...] = jnp.zeros_like(proj)
    qacc[...] = jnp.zeros_like(qacc)
    ds[...] = jnp.zeros_like(ds)
    rowt[...] = jnp.zeros_like(rowt)
    spread_m[...] = jnp.where(iota((LANES, inner), 0) == iota((LANES, inner), 1) // width, 1.0, 0.0).astype(BF16)
    gather_m[...] = jnp.where(iota((inner, LANES), 1) == iota((inner, LANES), 0) // width, 1.0, 0.0).astype(BF16)
    head = iota((t, LANES), 1) // width

    def outer(q, carry):
        x4 = x[:, lanes(q)]
        zero = jnp.zeros_like(x4)
        xm = jnp.concatenate([jnp.where(head == j, x4, zero) for j in range(gh)], axis=0)
        dall[q] = dot_nt(xm, g[:, lanes(q)])
        return carry

    lax.fori_loop(0, groups, outer, 0)

    def land(ka, carry):
        arrive(w_slot, wfs, wfr, ka)
        if halved:
            across(ka).start()
        return carry

    lax.fori_loop(0, n_a, land, 0)
    if halved:
        lax.fori_loop(0, n_a, lambda ka, carry: (across(ka).wait_recv(), carry)[1], 0)
        total = None
        for k in range(n_ctx):
            picked = jnp.concatenate(
                [tok[:, i * rows + k * half:i * rows + (k + 1) * half] for i in range(n_dp)], axis=1)
            term = dot_nt(picked, wall[k])
            total = term if total is None else total + term
        proj[:, :wcols] = total
    elif wide:
        proj[:, :wcols] = dot_nt(tok[...], wall[...])
    else:
        def shard(i, carry):
            proj[:, :wcols] += dot_nt(tok[i], wall[i])
            return carry

        lax.fori_loop(0, n_dp, shard, 0)
    rate_scale = -jnp.exp(vec[0:1, :])
    b = proj[:, :STATE].astype(BF16)
    z = proj[:, STATE:STATE + LANES] + vec[1:2, :]
    dt = jnp.maximum(z, 0.0) + jnp.log1p(jnp.exp(-jnp.abs(z)))
    row_i, col_i = iota((t, t), 0), iota((t, t), 1)
    lower = jnp.where(row_i >= col_i, 1.0, 0.0).astype(BF16)
    upper = jnp.where(col_i >= row_i, 1.0, 0.0).astype(BF16)
    cum = dot_exact(lower, rate_scale * dt)
    cum_r[...] = cum
    dt_r[...] = dt
    cumt[...] = cum.T
    last = cum_r[t - 1:t, :]
    to_end = jnp.exp(last - cum)
    wgt = to_end * dt
    grow = jnp.exp(cum)
    w_bf = wgt.astype(BF16)
    e_bf = grow.astype(BF16)
    cv = c[...]
    bt = b.astype(F32).T.astype(BF16)
    ct = cv.astype(F32).T.astype(BF16)

    span = [slice(q * LANES, (q + 1) * LANES) for q in range(groups)]
    for at in span:
        xw[:, at] = (dot(w_bf, spread_m[:, at]) * x[:, at].astype(F32)).astype(BF16)
        gwt[:, at] = (dot(e_bf, spread_m[:, at]) * g[:, at].astype(F32)).astype(BF16)
    sloc[0] = dot(bt, xw[...]).astype(BF16)
    sloc[1] = dot(ct, gwt[...]).astype(BF16)
    each(n_ctx, lambda k: c_copy(k).start())
    if n_ctx > 2:
        decs[...] = jnp.broadcast_to(jnp.exp(last), decs.shape)
        crecv[my] = jnp.zeros(crecv.shape[1:], BF16)
        decr[my] = jnp.zeros(decr.shape[1:], F32)
        each(n_ctx, lambda k: d_copy(k).start())

    scores = dot_nt(b, cv)
    causal = col_i >= row_i

    def mix(q, carry):
        g4 = g[:, lanes(q)]
        shift = lax.rem(LANES - gh * q, LANES)
        cum_s = pltpu.roll(cum_r[...], shift, 1)
        dt_s = pltpu.roll(dt_r[...], shift, 1)
        total = ds[...]
        quot = qacc[...]
        mixed = []
        for j in range(gh):
            h = gh * q + j
            spread = cumt[pl.ds(h, 1), :] - cum_s[:, j:j + 1]
            factor = jnp.exp(jnp.where(causal, spread, -1e30))
            step = dt_s[:, j:j + 1]
            d = dall[q, j * t:(j + 1) * t]
            fs = factor * scores
            mixed.append((fs * step).astype(BF16))
            u = d * fs
            quot = jnp.where(col_i == h, jnp.sum(u, axis=1, keepdims=True), quot)
            rowt[pl.ds(h, 1), :] = jnp.sum(u * step, axis=0, keepdims=True)
            total = total + d * (factor * step)
        ds[...] = total
        qacc[...] = quot
        out = dot(jnp.concatenate(mixed, axis=0), g4)
        acc = dexp[:, lanes(q)] * g4.astype(F32)
        for j in range(gh):
            acc = acc + jnp.where(head == j, out[j * t:(j + 1) * t], 0.0)
        dx[:, lanes(q)] = acc
        return carry

    lax.fori_loop(0, groups, mix, 0)
    each(n_ctx, lambda k: c_copy(k).wait_recv())
    if n_ctx > 2:
        each(n_ctx, lambda k: d_copy(k).wait_recv())

    sv = sg = jnp.zeros((t, LANES), F32)
    db2 = dc2 = jnp.zeros((t, STATE), F32)
    gs = jnp.zeros((8, LANES), F32)
    for at in span:
        e, et = spread_m[:, at], gather_m[at, :]
        if n_ctx == 2:
            got = crecv[1 - my, :, at]
            none = jnp.zeros_like(got)
            s4 = jnp.where(my > 0, got, none)
            g4s = jnp.where(my < 1, got, none)
        else:
            s = jnp.zeros((STATE, LANES), F32)
            k = s
            for i in range(n_ctx):
                dec = dot_split(decr[i], e)[0:1]
                s = jnp.where(i < my, dec * s + crecv[i, :, at].astype(F32), s)
            for i in reversed(range(n_ctx)):
                dec = dot_split(decr[i], e)[0:1]
                k = jnp.where(i > my, dec * k + crecv[i, :, at].astype(F32), k)
            s4, g4s = s.astype(BF16), k.astype(BF16)
            both = jnp.sum(s * k, axis=0, keepdims=True)
            gs = gs + dot_split(jnp.broadcast_to(both, (8, LANES)), et)
        us = dot(cv, s4)
        ug = dot(b, g4s)
        sv = sv + dot_split(x[:, at].astype(F32) * ug, et)
        sg = sg + dot_split(g[:, at].astype(F32) * us, et)
        db2 = db2 + dot_nt(xw[:, at], g4s)
        dc2 = dc2 + dot_nt(gwt[:, at], s4)
        gx[:, at] = (dx[:, at] + dot(w_bf, e) * ug).astype(BF16)
    dsv = ds[...]
    db = dot_split(dsv, cv) + db2
    dc = dot_split(dsv.T, b) + dc2
    gc[...] = dc.astype(BF16)
    quot = qacc[...]
    v = sv
    vw = v * wgt
    dcum = rowt[...].T + grow * sg - dt * quot - vw
    tail = jnp.sum(vw, axis=0, keepdims=True)
    if n_ctx > 2:
        tail = tail + jnp.exp(last) * gs[0:1, :]
    dcum = dcum + jnp.where(row_i == t - 1, tail, 0.0)
    drate = dot_exact(upper, dcum)
    ddt = quot + v * to_end + rate_scale * drate
    dz = ddt / (1.0 + jnp.exp(-z))
    proj[...] = jnp.zeros_like(proj)
    proj[:, :STATE] = db.astype(BF16).astype(F32)
    proj[:, STATE:cols] = dz[:, :heads]
    whole = proj[...]
    gall[:, blk(me)] = whole.T[:wcols].astype(BF16)
    first(g_slot, gzs, gzr, gfs, gfr)
    gp[...] = whole[:, :cols].astype(BF16)
    pass_on(g_slot, gzs, gzr, gfs, gfr)
    each(n_dp, lambda k: a_copy(k).wait_recv())
    lax.fori_loop(0, n_a, lambda ka, carry: (arrive(g_slot, gfs, gfr, ka), carry)[1], 0)
    part[...] = dot(gall[...], trecv[...])
    for o in range(n_ctx):
        pst[o] = part[o * cb:o * cb + cbp, :]
    each(n_ctx, lambda k: p_copy(k).start())
    each(n_ctx, lambda k: p_copy(k).wait_recv())

    def add(k, acc):
        return acc + precv[mate(k)]

    total = lax.fori_loop(1, n_ctx, add, pst[my])
    gw[...] = (total * (1.0 / n_dp)).T[:, :cb]
    settle(w_slot, wzs, wzr, wfs, wfr)
    if halved:
        lax.fori_loop(0, n_a, lambda ka, carry: (across(ka).wait_send(), carry)[1], 0)
    each(n_dp, lambda k: a_copy(k).wait_send())
    settle(g_slot, gzs, gzr, gfs, gfr)
    each(n_ctx, lambda k: c_copy(k).wait_send())
    each(n_ctx, lambda k: p_copy(k).wait_send())
    if n_ctx > 2:
        each(n_ctx, lambda k: d_copy(k).wait_send())


def store(*refs):
    sems = refs[-1]
    copies = [pltpu.make_async_copy(refs[i], refs[4 + i], sems.at[i]) for i in range(4)]
    for copy in copies:
        copy.start()
    for copy in copies:
        copy.wait()


def per_device(layer_in, inner_act, readout, w_in, a_log, dt_bias, d_skip, grad_out):
    n_dp, n_ctx = lax.axis_size("dp"), lax.axis_size("ctx")
    tokens, x, c, g = layer_in[0], inner_act[0], readout[0], grad_out[0]
    t, inner = x.shape
    rows, cols = w_in.shape
    heads = a_log.shape[0]
    width = inner // heads
    wcols = up(cols, 16)
    wide = rows % LANES == 0
    wt = jnp.pad(w_in.T, ((0, wcols - cols), (0, 0)))
    if not wide:
        tokens = jnp.swapaxes(tokens.reshape(t, n_dp, rows), 0, 1)
    vec = jnp.pad(jnp.stack([a_log, dt_bias]), ((0, 6), (0, LANES - heads)))
    dexp = jnp.repeat(d_skip, width)[None]
    cb = cols // n_ctx
    cbp = up(cb, 8)
    vm = pltpu.VMEM
    n_a = n_dp // inner_group(n_dp)
    if not wide:
        wall = (n_dp, wcols, rows)
    elif rows % (n_ctx * LANES) == 0 and n_ctx == 2:
        wall = (n_ctx, wcols, n_dp * rows // n_ctx)
    else:
        wall = (wcols, n_dp * rows)
    scratch = [
        vm(tokens.shape, BF16),
        vm((t, inner), BF16),
        vm((t, inner), BF16),
        vm(wall, BF16),
        vm((n_dp * t, rows), BF16),
        vm((wcols, n_dp * t), BF16),
        vm((2, STATE, inner), BF16),
        vm((n_ctx, STATE, inner), BF16),
        vm((inner // LANES, LANES // width * t, t), F32),
        vm((LANES, inner), BF16),
        vm((inner, LANES), BF16),
        vm((t, inner), BF16),
        vm((t, inner), BF16),
        vm((t, inner), F32),
        vm((t, 2 * LANES), F32),
        vm((t, LANES), F32),
        vm((t, LANES), F32),
        vm((LANES, t), F32),
        vm((LANES, t), F32),
        vm((t, LANES), F32),
        vm((t, t), F32),
        vm((wcols, rows), F32),
        vm((n_ctx, cbp, rows), F32),
        vm((n_ctx, cbp, rows), F32),
        vm((8, LANES), F32),
        vm((n_ctx, 8, LANES), F32),
    ]
    dma = pltpu.SemaphoreType.DMA
    scratch += [dma((n_a,))] * 2 + [dma((n_dp,))] * 4 + [dma((n_a,))] * 2 + [dma((n_dp,))] * 2
    scratch += [dma((n_ctx,))] * 6 + [dma((n_a,))] * 2 + [dma((3,))]
    hbm = pl.BlockSpec(memory_space=pltpu.HBM)
    spec = pl.BlockSpec(memory_space=pltpu.VMEM)
    cfg = (n_dp, n_ctx, t, rows, heads, width, cols)
    results = pl.pallas_call(
        functools.partial(kernel, cfg),
        out_shape=(
            jax.ShapeDtypeStruct((t, inner), BF16),
            jax.ShapeDtypeStruct((t, STATE), BF16),
            jax.ShapeDtypeStruct((t, cols), BF16),
            jax.ShapeDtypeStruct((rows, cb), F32),
        ),
        in_specs=[hbm] * 3 + [spec] * 4,
        out_specs=(spec,) * 4,
        scratch_shapes=scratch,
        compiler_params=pltpu.CompilerParams(
            collective_id=0, has_side_effects=True, vmem_limit_bytes=48 * 1024 * 1024),
        name="ssm_backward",
    )(tokens, x, g, c, wt, vec, dexp)
    gx, gc, gp, gw = pl.pallas_call(
        store,
        out_shape=tuple(jax.ShapeDtypeStruct(r.shape, r.dtype) for r in results),
        in_specs=[spec] * 4,
        out_specs=(hbm,) * 4,
        scratch_shapes=[dma((4,))],
        name="store_results",
    )(*results)
    return (gx[None], gc[None], gp[None], gw)


LOG2E = 1.4426950408889634
HROWS = 80
WROWS = 144


def exact_right(v, sel):
    hi = v.astype(BF16)
    mid, low = split(v - hi.astype(F32))
    return dot(hi, sel) + dot(mid, sel) + dot(low, sel)


def flip(i, k):
    if k == 0:
        return i
    if k == 1:
        return i + 1 - 2 * lax.rem(i, 2)
    if k == 2:
        return i + 2 - 4 * lax.div(i, 2)
    return 3 - i


def pair_kernel(cfg, tok_h, x_h, g_h, ct_h, w_h, alog_h, bias_h, skip_h, gx_h, gct_h, gpt_h, own_h, qrecv,
                tok, x, g, a, ct, wv, alog, bias, skip, wall, spread, dall, gm, dg, mall, ascale, spu, ssend, srecv,
                xy, au, proj, ds, rowt, cst, csr, gph, gpall, tokp, pown, psend, precv, qsend,
                gx, gct, gpt, own,
                wzs, wzr, wps, wpr, xs, xr, ks, kr, rs, rr, zs, zr, ts, tr, fs, fr, gs, gr, es, er, ls):
    t, rows, heads, width, cols = cfg
    half = rows // 2
    inner = x.shape[1]
    groups = inner // LANES
    gh = LANES // width
    cb = cols // 2
    me, my = lax.axis_index("dp"), lax.axis_index("ctx")
    za, pb = lax.div(me, 4), lax.rem(me, 4)
    mate = (me, 1 - my)

    def lanes(q, n=LANES):
        return pl.ds(pl.multiple_of(q * n, LANES), n)

    def local(src, dst, i):
        return pltpu.make_async_copy(src, dst, ls.at[i])

    def remote(src, dst, send, recv, to):
        return pltpu.make_async_remote_copy(
            src_ref=src, dst_ref=dst, send_sem=send, recv_sem=recv, device_id=to, device_id_type=MESH)

    def z_peer(k):
        return (flip(za, k) * 4 + pb, my)

    def p_peer(k):
        return (za * 4 + flip(pb, k), my)

    def c_peer(k):
        return (za * 4 + flip(pb, k), 1 - my)

    def n_peer(k):
        return (flip(za, 1) * 4 + flip(pb, k), my)

    barrier = pltpu.get_barrier_semaphore()
    for to in [z_peer(k) for k in (3, 2, 1)] + [n_peer(k) for k in (3, 2, 1)] + [p_peer(k) for k in (3, 2, 1)] + [c_peer(k) for k in (3, 2, 1)] + [mate]:
        pl.semaphore_signal(barrier, inc=1, device_id=to, device_id_type=MESH)

    smalls = [local(w_h, wv, 0), local(alog_h, alog, 1), local(bias_h, bias, 2), local(skip_h, skip, 3), local(ct_h, ct, 4)]
    tok_in = local(tok_h, tok.at[pl.ds(0, t)], 5)
    x_in, g_in = local(x_h, x, 6), local(g_h, g, 7)
    for load in smalls:
        load.start()
    tok_in.start()
    x_in.start()
    g_in.start()

    @pl.when(my == 0)
    def _():
        local(x_h, a, 8).start()

    @pl.when(my == 1)
    def _():
        local(g_h, a, 8).start()

    smalls[0].wait()
    wfull = jnp.concatenate([wv[...], jnp.zeros((WROWS - cols, rows), BF16)], axis=0)
    wall[my, me] = jnp.where(my == 0, wfull[:, :half], wfull[:, half:])

    pl.semaphore_wait(barrier, 13)

    def w_z(k):
        return remote(wall.at[my, me], wall.at[my, me], wzs.at[k], wzr.at[k], z_peer(k))

    def w_p(kz, kp):
        if kz == 1:
            return remote(wall.at[my, me], wall.at[my, me], wps.at[4 + kp], wpr.at[4 + kp], n_peer(kp))
        slot = wall.at[my, flip(za, kz) * 4 + pb]
        return remote(slot, slot, wps.at[kz * 4 + kp], wpr.at[kz * 4 + kp], p_peer(kp))

    def w_x(kz):
        block = wall.at[my, pl.ds(flip(za, kz) * 4, 4)]
        return remote(block, block, xs.at[kz], xr.at[kz], mate)

    def t_copy(kz, kp):
        i = flip(za, kz) * 4 + flip(pb, kp)
        return remote(tok.at[pl.ds(0, t), lanes(i, rows)], tokp.at[kz - 1, kp, pl.ds(pl.multiple_of(my * t, t), t)],
                      ts.at[kz * 4 + kp], tr.at[kz * 4 + kp], p_peer(kp))

    def f_copy(kz, kp):
        block = tokp.at[kz - 1, kp, pl.ds(pl.multiple_of(my * t, t), t)]
        return remote(block, block, fs.at[kz * 4 + kp], fr.at[kz * 4 + kp], mate)

    def g_copy():
        return remote(gph.at[1 - my], gpall.at[0, my], gs.at[0], gr.at[0], mate)

    def piece(k, c, source, at, send, recv):
        return remote(gph.at[c, at], gpall.at[k, source, at], send, recv.at[2 * k + source], (za * 4 + flip(pb, k), c))

    def early(k, source):
        return piece(k, 0, source, pl.ds(0, STATE), es.at[k], er)

    def late(k, c, source):
        at = pl.ds(0, HROWS) if c else pl.ds(STATE, HROWS - STATE)
        return piece(k, c, source, at, gs.at[2 * k + c], gr)

    def mate_copy(src, dst, i):
        return remote(src, dst, ks.at[i], kr.at[i], mate)

    for k in (3, 2, 1):
        w_z(k).start()
    for kz in (0, 1):
        for k in (3, 1, 2):
            w_p(kz, k).start()
    tok_in.wait()
    tok_x = mate_copy(tok.at[pl.ds(0, t)], tok.at[pl.ds(t, t)], 0)
    tok_x.start()

    for load in smalls[1:]:
        load.wait()
    spread[...] = jnp.where(iota((LANES, inner), 0) == iota((LANES, inner), 1) // width, 1.0, 0.0).astype(BF16)

    def row(ref):
        return jnp.concatenate([ref[...], jnp.zeros((1, LANES - heads), F32)], axis=1)

    rate_t = -jnp.exp(jnp.broadcast_to(row(alog), (LANES, LANES)).T[:HROWS])
    bias_t = jnp.broadcast_to(row(bias), (LANES, LANES)).T[:HROWS]
    skip_hi, skip_lo = split(jnp.broadcast_to(row(skip), (16, LANES)))
    x_in.wait()
    g_in.wait()
    head = iota((t, LANES), 1) // width

    def outer(q, carry):
        x4, g4 = x[:, lanes(q)], g[:, lanes(q)]
        zero = jnp.zeros_like(x4)
        dall[q] = dot_nt(jnp.concatenate([jnp.where(head == j, x4, zero) for j in range(gh)], axis=0), g4)
        gm[q] = jnp.concatenate([jnp.where(head == j, g4, zero) for j in range(gh)], axis=0)
        e = spread[:, lanes(q)]
        skip4 = (dot(skip_hi, e) + dot(skip_lo, e))[0:1]
        dg[:, lanes(q)] = skip4 * g4.astype(F32)
        return carry

    lax.fori_loop(0, groups, outer, 0)
    ds[...] = jnp.zeros_like(ds)
    rowt[...] = jnp.zeros_like(rowt)
    csr[...] = jnp.zeros_like(csr)
    ctv = ct[...]
    row_i, col_i = iota((t, t), 0), iota((t, t), 1)
    later = jnp.where(col_i >= row_i, 1.0, 0.0).astype(BF16)
    sooner = jnp.where(row_i >= col_i, 1.0, 0.0).astype(BF16)
    first = my == 0

    @pl.when(first)
    def _():
        local(x_h, a, 8).wait()

    @pl.when(my == 1)
    def _():
        local(g_h, a, 8).wait()

    def take(kz, acc):
        w_x(kz).wait_recv()
        base = flip(za, kz) * 4
        for j in range(4):
            block = jnp.concatenate([wall[0, base + j], wall[1, base + j]], axis=1)
            term = dot_nt(block, tok[0:t, lanes(base + j, rows)])
            acc = term if acc is None else acc + term
        return acc

    def landed(kz):
        for kp in (1, 2, 3):
            w_p(kz, kp).wait_recv()
        w_x(kz).start()

    for kz in (1, 2, 3):
        w_z(kz).wait_recv()
        if kz > 1:
            for kp in (3, 1, 2):
                w_p(kz, kp).start()
    acc = None
    for kz in range(4):
        if kz == 3:
            for ky in MOVED:
                for kp in (3, 1, 2):
                    t_copy(ky, kp).start()
        landed(kz)
        if kz > 0:
            acc = take(kz - 1, acc)
    acc = take(3, acc)

    z = acc[STATE:] + bias_t
    bt = acc[:STATE].astype(BF16)
    dt = jnp.maximum(z, 0.0) + jnp.log1p(jnp.exp(-jnp.abs(z)))
    cum = exact_right(rate_t * dt, later)
    csr[0:HROWS] = cum * LOG2E - jnp.log(jnp.maximum(dt, 1e-37)) * LOG2E
    cst[...] = cum * LOG2E
    wgt = jnp.exp(cum[:, t - 1:t] - cum) * dt
    scale_t = jnp.where(first, wgt, jnp.exp(cum))
    scale = jnp.concatenate([scale_t, jnp.zeros((LANES - HROWS, t), F32)], axis=0).T.astype(BF16)
    csr[...] = csr[...].T
    pad = jnp.zeros((LANES - STATE, t), F32)
    b = jnp.concatenate([bt.astype(F32), pad], axis=0).T[:, :STATE].astype(BF16)
    lt = jnp.where(first, bt, ctv)
    left = jnp.concatenate([lt.astype(F32), pad], axis=0).T[:, :STATE].astype(BF16)
    for q in range(groups):
        at = slice(q * LANES, (q + 1) * LANES)
        s4 = dot(scale, spread[:, at])
        spu[:, at] = jnp.where(first, s4, 0.0)
        ascale[:, at] = (s4 * a[:, at].astype(F32)).astype(BF16)
    ssend[...] = dot(lt, ascale[...]).astype(BF16)
    state_x = mate_copy(ssend, srecv, 1)
    state_x.start()

    scores = jnp.where(col_i >= row_i, dot(b, ctv), 0.0)
    dscore_rows = 32

    def mix(q, carry):
        cs = csr[:, gh * q:gh * q + gh]
        tops = [cst[pl.ds(gh * q + j, 1), :] for j in range(gh)]
        sums = [jnp.zeros((8, t), F32) for _ in range(gh)]
        for r in range(t // dscore_rows):
            at = slice(r * dscore_rows, (r + 1) * dscore_rows)
            total = ds[at]
            for j in range(gh):
                e = jnp.exp2(jnp.minimum(tops[j] - cs[at, j:j + 1], 100.0))
                m = e * scores[at]
                d = dall[q, j * t + r * dscore_rows:j * t + (r + 1) * dscore_rows]
                mall[q, at, j * LANES:(j + 1) * LANES] = m.astype(BF16)
                total = total + d * e
                u = d * m
                for i in range(dscore_rows // 8):
                    sums[j] = sums[j] + u[8 * i:8 * i + 8]
            ds[at] = total
        for j in range(gh):
            rowt[pl.ds(gh * q + j, 1), :] = jnp.sum(sums[j], axis=0, keepdims=True)
        return carry

    for q in range(groups):
        mix(q, 0)
    state_x.wait_recv()
    for q in range(groups):
        at = slice(q * LANES, (q + 1) * LANES)
        u = dot(left, srecv[:, at])
        y = dot(mall[q], gm[q]) + spu[:, at] * u
        au[:, at] = (ascale[:, at].astype(F32) * u).astype(BF16)
        xy[:, at] = (x[:, at].astype(F32) * y).astype(BF16)
        gx[:, at] = (y + dg[:, at]).astype(BF16)
    d2 = dot_nt(srecv[...], ascale[...])
    dscore = jnp.where(col_i >= row_i, ds[...], 0.0).astype(BF16)
    dbt = dot_nt(ctv, dscore) + jnp.where(first, d2, 0.0)
    dct = dot(bt, dscore) + jnp.where(first, 0.0, d2)
    gph[0, 0:STATE] = dbt.astype(BF16)
    for k in (3, 1, 2):
        early(k, my).start()
    gct[...] = dct.astype(BF16)
    gct_out = local(gct, gct_h, 10)
    gct_out.start()
    gx_out = local(gx, gx_h, 9)
    gx_out.start()
    sel = spread[:HROWS]
    qt = dot_nt(sel, xy[...])
    zt = dot_nt(sel, au[...])
    tail = jnp.sum(zt, axis=1, keepdims=True)
    dcum = rowt[...] - qt + jnp.where(first, jnp.where(iota((HROWS, t), 1) == t - 1, tail, 0.0), zt)
    hi, lo = split(dcum)
    drate = dot(hi, sooner) + dot(lo, sooner)
    sig = 1.0 / (1.0 + jnp.exp(-z))
    ratio = jnp.where(dt > 1e-30, sig / jnp.maximum(dt, 1e-30), 1.0)
    dzt = qt * ratio + rate_t * drate * sig
    proj[0:STATE] = dbt
    proj[STATE:] = dzt
    gph[0, STATE:HROWS] = proj[STATE:HROWS].astype(BF16)
    gph[1] = jnp.concatenate([proj[cb:cols], jnp.zeros((HROWS - cb, t), F32)], axis=0).astype(BF16)
    g_copy().start()
    for k in (3, 1, 2):
        late(k, 1, my).start()
        late(k, 0, my).start()
    gpt[...] = proj[0:cols].astype(BF16)
    gpt_out = local(gpt, gpt_h, 11)
    gpt_out.start()

    for kz in MOVED:
        for kp in (3, 1, 2):
            t_copy(kz, kp).wait_recv()
            f_copy(kz, kp).start()
    tok_x.wait_recv()
    g_copy().wait_recv()
    lhs = jnp.concatenate([gph[my], gpall[0, 1 - my]], axis=1)

    def r_p(kz, kp):
        to = n_peer(kp) if kz == 1 else p_peer(kp)
        return remote(psend.at[kz, kp], precv.at[kz, kp], rs.at[kz * 4 + kp], rr.at[kz * 4 + kp], to)

    def r_z(kz):
        return remote(qsend.at[kz], qrecv.at[kz - 2], zs.at[kz], zr.at[kz], z_peer(kz))

    def packed(part):
        sides = (part[:, :half], part[:, half:])
        return jnp.concatenate([side[:STATE] for side in sides] + [side[STATE:STATE + 8] for side in sides], axis=0)

    def block(kz, kp):
        return dot(lhs, tok[:, lanes(flip(za, kz) * 4 + flip(pb, kp), rows)])

    summed = [kz for kz in (1, 2, 3) if kz not in MOVED] + [0]
    for kz in summed:
        for kp in (3, 1, 2) + ((0,) if kz else ()):
            psend[kz, kp] = packed(block(kz, kp)).astype(BF16)
            r_p(kz, kp).start()
    for kz in (3, 2, 0):
        pown[kz] = packed(block(kz, 0))
    for kz in MOVED:
        for kp in (3, 1, 2):
            f_copy(kz, kp).wait_recv()

    @pl.when(first)
    def _():
        for k in (1, 2, 3):
            for source in (0, 1):
                early(k, source).wait_recv()
                late(k, 0, source).wait_recv()

    @pl.when(my == 1)
    def _():
        for k in (1, 2, 3):
            for source in (0, 1):
                late(k, 1, source).wait_recv()

    sides = [jnp.concatenate([gpall[k, 0], gpall[k, 1]], axis=1) for k in (1, 2, 3)]
    for kz in MOVED:
        term = dot(sides[0], tokp[kz - 1, 1]) + dot(sides[1], tokp[kz - 1, 2]) + dot(sides[2], tokp[kz - 1, 3])
        qsend[kz] = (pown[kz] + packed(term)).astype(BF16)
        r_z(kz).start()
    total = pown[0]
    for kz, kp in [(0, k) for k in (1, 2, 3)] + [(1, k) for k in range(4)]:
        r_p(kz, kp).wait_recv()
        total = total + precv[kz, kp].astype(F32)
    own[...] = total
    own_out = local(own, own_h, 12)
    own_out.start()

    for k in (1, 2, 3):
        w_z(k).wait_send()
        early(k, my).wait_send()
        late(k, 0, my).wait_send()
        late(k, 1, my).wait_send()
        for kz in range(4):
            w_p(kz, k).wait_send()
        for kz in summed:
            r_p(kz, k).wait_send()
        for kz in MOVED:
            t_copy(kz, k).wait_send()
            f_copy(kz, k).wait_send()
    r_p(1, 0).wait_send()
    for kz in (3, 2):
        r_z(kz).wait_send()
    for kz in range(4):
        w_x(kz).wait_send()
    tok_x.wait_send()
    state_x.wait_send()
    g_copy().wait_send()
    for out in (gx_out, gct_out, gpt_out, own_out):
        out.wait()
    for kz in (3, 2):
        r_z(kz).wait_recv()


def store_pair(*refs):
    (gx, gct, gpt, own, terms), outs, held, ins, done = refs[:5], refs[5:9], refs[9:15], refs[15], refs[16]
    loads = [pltpu.make_async_copy(src, held[i], ins.at[i]) for i, src in enumerate((own, terms, gx, gct, gpt))]
    for i in (2, 0, 1, 3, 4):
        loads[i].start()
    stores = []
    for i in range(3):
        stores.append(pltpu.make_async_copy(held[2 + i], outs[i], done.at[i]))
    stores.append(pltpu.make_async_copy(held[5], outs[3], done.at[3]))
    loads[0].wait()
    loads[1].wait()
    loads[2].wait()
    stores[0].start()
    total = held[0][...]
    for k in range(2):
        total = total + held[1][k].astype(F32)
    total = total * (1.0 / 16)
    at = 2 * STATE
    gwt = held[5]
    gwt[0:STATE] = jnp.concatenate([total[:STATE], total[STATE:at]], axis=1)
    gwt[STATE:] = jnp.concatenate([total[at:at + 8], total[at + 8:]], axis=1)[:gwt.shape[0] - STATE]
    stores[3].start()
    for i in (1, 2):
        loads[2 + i].wait()
        stores[i].start()
    for store in stores:
        store.wait()


def pair_device(layer_in, inner_act, readout, w_in, a_log, dt_bias, d_skip, grad_out):
    tokens, x, ct, g = layer_in[0], inner_act[0], readout[0].T, grad_out[0]
    t, inner = x.shape
    rows, cols = w_in.shape
    heads = a_log.shape[0]
    width = inner // heads
    groups, gh = inner // LANES, LANES // width
    cb = cols // 2
    vm = pltpu.VMEM
    scratch = [
        vm((2 * t, tokens.shape[1]), BF16),
        vm((t, inner), BF16),
        vm((t, inner), BF16),
        vm((t, inner), BF16),
        vm((STATE, t), BF16),
        vm((cols, rows), BF16),
        vm((1, heads), F32),
        vm((1, heads), F32),
        vm((1, heads), F32),
        vm((2, 16, WROWS, rows // 2), BF16),
        vm((LANES, inner), BF16),
        vm((groups, gh * t, t), F32),
        vm((groups, gh * t, LANES), BF16),
        vm((t, inner), F32),
        vm((groups, t, gh * t), BF16),
        vm((t, inner), BF16),
        vm((t, inner), F32),
        vm((STATE, inner), BF16),
        vm((STATE, inner), BF16),
        vm((t, inner), BF16),
        vm((t, inner), BF16),
        vm((WROWS, t), F32),
        vm((t, t), F32),
        vm((HROWS, t), F32),
        vm((HROWS, t), F32),
        vm((LANES, LANES), F32),
        vm((2, HROWS, t), BF16),
        vm((4, 2, HROWS, t), BF16),
        vm((3, 4, 2 * t, rows), BF16),
        vm((4, WROWS, rows // 2), F32),
        vm((4, 4, WROWS, rows // 2), BF16),
        vm((4, 4, WROWS, rows // 2), BF16),
        vm((4, WROWS, rows // 2), BF16),
        vm((t, inner), BF16),
        vm((STATE, t), BF16),
        vm((cols, t), BF16),
        vm((WROWS, rows // 2), F32),
    ]
    dma = pltpu.SemaphoreType.DMA
    scratch += [dma((4,))] * 2 + [dma((16,))] * 2 + [dma((4,))] * 4 + [dma((16,))] * 2 + [dma((4,))] * 2 + [dma((16,))] * 4 + [dma((8,))] * 4 + [dma((13,))]
    hbm = pl.BlockSpec(memory_space=pltpu.HBM)
    results = pl.pallas_call(
        functools.partial(pair_kernel, (t, rows, heads, width, cols)),
        out_shape=(
            jax.ShapeDtypeStruct((t, inner), BF16),
            jax.ShapeDtypeStruct((STATE, t), BF16),
            jax.ShapeDtypeStruct((cols, t), BF16),
            jax.ShapeDtypeStruct((WROWS, rows // 2), F32),
            jax.ShapeDtypeStruct((2, WROWS, rows // 2), BF16),
        ),
        in_specs=[hbm] * 8,
        out_specs=(hbm,) * 5,
        scratch_shapes=scratch,
        compiler_params=pltpu.CompilerParams(
            collective_id=0, has_side_effects=True, vmem_limit_bytes=VMEM_MAIN),
        name="ssm_backward",
    )(tokens, x, g, ct, w_in.T, a_log[None], dt_bias[None], d_skip[None])
    weight = jax.ShapeDtypeStruct((cb, rows), F32)
    held = [*results[3:], *results[:3], weight]
    gx, gct, gpt, gwt = pl.pallas_call(
        store_pair,
        out_shape=tuple(jax.ShapeDtypeStruct(r.shape, r.dtype) for r in results[:3]) + (weight,),
        in_specs=[hbm] * 5,
        out_specs=(hbm,) * 4,
        scratch_shapes=[vm(r.shape, r.dtype) for r in held] + [dma((5,)), dma((4,))],
        compiler_params=pltpu.CompilerParams(vmem_limit_bytes=VMEM_STORE),
        name="store_results",
    )(*results)
    return (gx[None], gct.T[None], gpt.T[None], gwt.T)


def solution(mesh):
    in_specs = (
        P("dp", "ctx", None),
        P("dp", "ctx", None),
        P("dp", "ctx", None),
        P("dp", None),
        P(),
        P(),
        P(),
        P("dp", "ctx", None),
    )
    out_specs = (P("dp", "ctx", None), P("dp", "ctx", None), P("dp", "ctx", None), P("dp", "ctx"))
    pairs = mesh.shape["dp"] == 16 and mesh.shape["ctx"] == 2
    return jax.shard_map(
        pair_device if pairs else per_device, mesh=mesh, in_specs=in_specs, out_specs=out_specs, check_vma=False
    )
```
